32 devices in a mesh: seq: 4 (over x, core), fsdp: 8 (over z, y).
Axes of the slice: x: 2, y: 2, z: 4, core: 2. Of those that a mesh axis runs over, the one named last changes fastest.
Arguments:
- inputs: bfloat16 [4096, 2304], P(('fsdp', 'seq')), may hold values from -6 to 6
- cotangent: bfloat16 [4096, 2304], P(('fsdp', 'seq')), may hold values from -6 to 6
- segments: int32 [4096], replicated, may hold values from 0 to 3, never falling along the last dimension, each value on 1 to 2048 neighbouring positions
- first_gain: bfloat16 [2304], P(('seq', 'fsdp')), may hold values from -0.5 to 0.5
- second_gain: bfloat16 [2304], P(('seq', 'fsdp')), may hold values from -0.5 to 0.5
- third_gain: bfloat16 [2304], P(('seq', 'fsdp')), may hold values from -0.5 to 0.5
- fourth_gain: bfloat16 [2304], P(('seq', 'fsdp')), may hold values from -0.5 to 0.5
- query_weight: bfloat16 [2304, 2048], P(('seq', 'fsdp')), may hold values from -0.125 to 0.125
- key_weight: bfloat16 [2304, 1024], P(('seq', 'fsdp')), may hold values from -0.125 to 0.125
- value_weight: bfloat16 [2304, 1024], P(('seq', 'fsdp')), may hold values from -0.125 to 0.125
- output_weight: bfloat16 [2304, 2048], P(('seq', 'fsdp')), may hold values from -0.125 to 0.125
- gate_weight: bfloat16 [9216, 2304], P(('seq', 'fsdp')), may hold values from -0.125 to 0.125
- up_weight: bfloat16 [9216, 2304], P(('seq', 'fsdp')), may hold values from -0.125 to 0.125
- down_weight: bfloat16 [9216, 2304], P(('seq', 'fsdp')), may hold values from -0.0625 to 0.0625
Outputs:
- layer_out: float32 [4096, 2304], P(('fsdp', 'seq'))
- input_grad: float32 [4096, 2304], P(('fsdp', 'seq'))
- first_grad: float32 [2304], P(('seq', 'fsdp'))
- second_grad: float32 [2304], P(('seq', 'fsdp'))
- third_grad: float32 [2304], P(('seq', 'fsdp'))
- fourth_grad: float32 [2304], P(('seq', 'fsdp'))
- query_grad: float32 [2304, 2048], P(('seq', 'fsdp'))
- key_grad: float32 [2304, 1024], P(('seq', 'fsdp'))
- value_grad: float32 [2304, 1024], P(('seq', 'fsdp'))
- output_grad: float32 [2304, 2048], P(('seq', 'fsdp'))
- gate_grad: float32 [9216, 2304], P(('seq', 'fsdp'))
- up_grad: float32 [9216, 2304], P(('seq', 'fsdp'))
- down_grad: float32 [9216, 2304], P(('seq', 'fsdp'))
The draws below stay inside these ranges and needn't reach their ends.
Inputs may be any that keep to these rules, and one draw needn't show every extreme that they name: `segments`: document numbers never fall along the batch; every document number appears, each document holds at most 2048 tokens, and one holds exactly 2048.
All inputs are finite; a program needn't handle non-finite values.
Results may differ from the reference program's by a relative error of at most 0.02.
Values may be sent and summed in bfloat16 or wider, within the bound.
No kernel may reach another device: no remote copies, remote signals or barrier semaphores. Data moves between devices by JAX's collectives and lax.ppermute only.
A program may use at most 384 MiB of HBM per device.

```python
import math
import jax
import jax.numpy as jnp
import numpy as np
from jax import lax

D = 2304
HEADS = 8
KV_HEADS = 4
HEAD_DIM = 256
FF = 9216
DOCS = 4
TOKENS = 4096


def levels(own_key, dims, pieces, least, high):
    level, own = 1.0, jax.random.fold_in(own_key, 6)
    for dim, parts in pieces:
        heights = jnp.exp(jax.random.uniform(jax.random.fold_in(own, dim), (parts,), jnp.float32, least / len(pieces), high / len(pieces)))
        level = level * jnp.repeat(heights, dims[dim] // parts).reshape([-1 if axis == dim else 1 for axis in range(len(dims))])
    return level


def split_up(amount, total, bound, lean):
    loads = [(1 << 20) // math.isqrt(grade ** lean) + 1 for grade in range(2, amount + 1)]
    surplus, given = total - bound - (amount - 1), [1] * (amount - 1)
    while surplus > 0:
        candidates = [i for i in range(amount - 1) if given[i] < bound]
        mass, left = sum([loads[i] for i in candidates]), surplus
        for i in candidates:
            extra = min(bound - given[i], max(1, left * loads[i] // mass), surplus)
            given[i] = given[i] + extra
            surplus = surplus - extra
    return np.array([bound] + given)


def uneven(own_key, amount, total, limit, skew):
    if amount == 2:
        one = jax.random.randint(own_key, (), max(1, total - limit), min(limit, total - 1) + 1)
        return jnp.stack([one, total - one])
    lengths = jnp.asarray(split_up(amount, total, limit, skew), jnp.int32)
    couples = (amount - 1) // 2
    donor, receiver = lengths[1:1 + 2 * couples:2], lengths[2:2 + 2 * couples:2]
    margin = jnp.minimum(donor - 1, limit - receiver)
    moved = jax.random.randint(jax.random.fold_in(own_key, 1), (couples,), 0, 1 << 20) % (margin + 1)
    lengths = lengths.at[1:1 + 2 * couples:2].set(donor - moved).at[2:2 + 2 * couples:2].set(receiver + moved)
    return lengths[jax.random.permutation(jax.random.fold_in(own_key, 2), amount)]


def gaussian(own_key, extent, deviation, reach, split=(), kind=jnp.bfloat16):
    values = jax.random.normal(own_key, extent, jnp.float32) * deviation
    if len(split) > 0:
        values = levels(own_key, extent, split, -0.22, 0.18) * values
    return jnp.clip(values, min=-reach, max=reach).astype(kind)


def setup_inputs(seed: int = 0) -> dict:
    arg_keys = jax.random.split(jax.random.key(seed), 15)
    inputs = gaussian(arg_keys[0], (TOKENS, D), 1.0, 6.0, ((0, 32),))
    cotangent = gaussian(arg_keys[1], (TOKENS, D), 1.0, 6.0, ((0, 32),))
    segments = jnp.searchsorted(jnp.cumsum(uneven(arg_keys[2], DOCS, TOKENS, TOKENS // 2, 0)), jnp.arange(TOKENS), side="right").astype(jnp.int32)
    first_gain = jnp.clip(jax.random.uniform(arg_keys[3], (D,), jnp.float32, -0.5, 0.5) * levels(arg_keys[3], (D,), ((0, 32),), -0.4, 0.0), -0.5, 0.5).astype(jnp.bfloat16)
    second_gain = jnp.clip(jax.random.uniform(arg_keys[4], (D,), jnp.float32, -0.5, 0.5) * levels(arg_keys[4], (D,), ((0, 32),), -0.4, 0.0), -0.5, 0.5).astype(jnp.bfloat16)
    third_gain = jnp.clip(jax.random.uniform(arg_keys[5], (D,), jnp.float32, -0.5, 0.5) * levels(arg_keys[5], (D,), ((0, 32),), -0.4, 0.0), -0.5, 0.5).astype(jnp.bfloat16)
    fourth_gain = jnp.clip(jax.random.uniform(arg_keys[6], (D,), jnp.float32, -0.5, 0.5) * levels(arg_keys[6], (D,), ((0, 32),), -0.4, 0.0), -0.5, 0.5).astype(jnp.bfloat16)
    query_weight = gaussian(arg_keys[7], (D, HEADS * HEAD_DIM), D ** -0.5, 0.125, ((0, 32),))
    key_weight = gaussian(arg_keys[8], (D, KV_HEADS * HEAD_DIM), D ** -0.5, 0.125, ((0, 32),))
    value_weight = gaussian(arg_keys[9], (D, KV_HEADS * HEAD_DIM), D ** -0.5, 0.125, ((0, 32),))
    output_weight = gaussian(arg_keys[10], (D, HEADS * HEAD_DIM), (HEADS * HEAD_DIM) ** -0.5, 0.125, ((0, 32),))
    gate_weight = gaussian(arg_keys[11], (FF, D), D ** -0.5, 0.125, ((0, 32),))
    up_weight = gaussian(arg_keys[12], (FF, D), D ** -0.5, 0.125, ((0, 32),))
    down_weight = gaussian(arg_keys[13], (FF, D), FF ** -0.5, 0.0625, ((0, 32),))
    return dict(inputs=inputs, cotangent=cotangent, segments=segments, first_gain=first_gain, second_gain=second_gain, third_gain=third_gain, fourth_gain=fourth_gain, query_weight=query_weight, key_weight=key_weight, value_weight=value_weight, output_weight=output_weight, gate_weight=gate_weight, up_weight=up_weight, down_weight=down_weight)


epsilon = 1e-06
softcap = 50.0
rope_base = 10000.0
gelu_coef = 0.7978845608028654
cubic_coef = 0.044715

def rms_forward(values, gain):
    scaling = lax.rsqrt(lax.optimization_barrier(jnp.mean(values * values, axis=-1, keepdims=True)) + epsilon)
    return values * scaling * (1.0 + gain.astype(jnp.float32))

def rms_backward(values, gain, upstream):
    scaling = lax.rsqrt(lax.optimization_barrier(jnp.mean(values * values, axis=-1, keepdims=True)) + epsilon)
    weighted = upstream * (1.0 + gain.astype(jnp.float32))
    inner = lax.optimization_barrier(jnp.mean(weighted * values, axis=-1, keepdims=True))
    grad_values = scaling * weighted - values * (scaling * scaling * scaling) * inner
    grad_gain = lax.optimization_barrier(jnp.sum(upstream * values * scaling, axis=0))
    return (grad_values, grad_gain)

def rotation(positions):
    half = HEAD_DIM // 2
    frequency = jnp.power(rope_base, -jnp.arange(half, dtype=jnp.float32) / half)
    angles = positions.astype(jnp.float32)[:, None] * frequency[None, :]
    return (jnp.cos(angles), jnp.sin(angles))

def rope_apply(values, cosine, sine, inverse):
    rows = values.shape[0]
    half = HEAD_DIM // 2
    shaped = values.reshape(rows, -1, HEAD_DIM)
    first = shaped[:, :, :half]
    second = shaped[:, :, half:]
    cosine_row = cosine[:, None, :]
    sine_row = sine[:, None, :]
    if inverse:
        sine_row = -sine_row
    turned = jnp.concatenate([first * cosine_row - second * sine_row, second * cosine_row + first * sine_row], axis=-1)
    return turned.reshape(rows, -1)

def gelu_value(gate):
    bent = jnp.tanh(gelu_coef * (gate + cubic_coef * gate * gate * gate))
    return 0.5 * gate * (1.0 + bent)

def gelu_slope(gate):
    bent = jnp.tanh(gelu_coef * (gate + cubic_coef * gate * gate * gate))
    return 0.5 * (1.0 + bent) + 0.5 * gate * (1.0 - bent * bent) * gelu_coef * (1.0 + 3.0 * cubic_coef * gate * gate)

def to_bf16_float(values):
    rounded = lax.optimization_barrier(values.astype(jnp.bfloat16))
    return rounded.astype(jnp.float32)

def local_attention(query, keys, values, query_pos, query_seg, segments):
    rows = query.shape[0]
    heads_here = keys.shape[1] // HEAD_DIM
    group = query.shape[1] // keys.shape[1]
    total = keys.shape[0]
    block = min(1024, total)
    count = total // block
    scale = HEAD_DIM ** (-0.5)
    shaped = query.astype(jnp.float32).reshape(rows, heads_here, group, HEAD_DIM)
    key_pos = jnp.arange(total, dtype=jnp.int32)

    def step(state, index):
        start = index * block
        key_block = lax.dynamic_slice_in_dim(keys, start, block, 0).astype(jnp.float32).reshape(block, heads_here, HEAD_DIM)
        value_block = lax.dynamic_slice_in_dim(values, start, block, 0).astype(jnp.float32).reshape(block, heads_here, HEAD_DIM)
        key_seg = lax.dynamic_slice_in_dim(segments, start, block, 0)
        key_at = lax.dynamic_slice_in_dim(key_pos, start, block, 0)
        allowed = (query_seg[:, None] == key_seg[None, :]) & (key_at[None, :] <= query_pos[:, None])

        def compute(inner):
            scores = jnp.einsum('qcgd,kcd->cgqk', shaped, key_block) * scale
            expo = jnp.where(allowed, jnp.exp(softcap * jnp.tanh(scores / softcap)), 0.0)
            weights = to_bf16_float(expo)
            return (inner[0] + jnp.einsum('cgqk,kcd->qcgd', weights, value_block), inner[1] + lax.optimization_barrier(jnp.sum(expo, axis=-1)))
        return (lax.cond(jnp.any(allowed), compute, lambda inner: inner, state), None)
    start_state = (jnp.zeros((rows, heads_here, group, HEAD_DIM), jnp.float32), jnp.zeros((heads_here, group, rows), jnp.float32))
    (numerator, totals), unused = lax.scan(step, start_state, jnp.arange(count))
    mixed = numerator / jnp.transpose(totals, (2, 0, 1))[..., None]
    return (mixed.astype(jnp.bfloat16).reshape(rows, -1), jnp.log(totals))

def local_attention_backward(query, keys, values, mixed, log_totals, mixed_grad, query_pos, query_seg, segments):
    rows = query.shape[0]
    heads_here = keys.shape[1] // HEAD_DIM
    group = query.shape[1] // keys.shape[1]
    total = keys.shape[0]
    block = min(1024, total)
    count = total // block
    scale = HEAD_DIM ** (-0.5)
    shaped = query.astype(jnp.float32).reshape(rows, heads_here, group, HEAD_DIM)
    outgrad = mixed_grad.astype(jnp.float32).reshape(rows, heads_here, group, HEAD_DIM)
    result = mixed.astype(jnp.float32).reshape(rows, heads_here, group, HEAD_DIM)
    delta = jnp.einsum('qcgd,qcgd->cgq', outgrad, result)
    key_pos = jnp.arange(total, dtype=jnp.int32)

    def step(running, index):
        start = index * block
        key_block = lax.dynamic_slice_in_dim(keys, start, block, 0).astype(jnp.float32).reshape(block, heads_here, HEAD_DIM)
        value_block = lax.dynamic_slice_in_dim(values, start, block, 0).astype(jnp.float32).reshape(block, heads_here, HEAD_DIM)
        key_seg = lax.dynamic_slice_in_dim(segments, start, block, 0)
        key_at = lax.dynamic_slice_in_dim(key_pos, start, block, 0)
        allowed = (query_seg[:, None] == key_seg[None, :]) & (key_at[None, :] <= query_pos[:, None])

        def compute(inner):
            scores = jnp.einsum('qcgd,kcd->cgqk', shaped, key_block) * scale
            bent = jnp.tanh(scores / softcap)
            probs = jnp.where(allowed, jnp.exp(softcap * bent - log_totals[..., None]), 0.0)
            value_part = jnp.einsum('cgqk,qcgd->kcd', to_bf16_float(probs), outgrad)
            prob_grad = jnp.einsum('qcgd,kcd->cgqk', outgrad, value_block)
            score_grad = to_bf16_float(probs * (prob_grad - delta[..., None]) * (1.0 - bent * bent))
            inner = inner + jnp.einsum('cgqk,kcd->qcgd', score_grad, key_block)
            key_part = jnp.einsum('cgqk,qcgd->kcd', score_grad, shaped)
            return (inner, key_part.reshape(block, -1), value_part.reshape(block, -1))

        def passby(inner):
            blank = jnp.zeros((block, heads_here * HEAD_DIM), jnp.float32)
            return (inner, blank, blank)
        running, key_part, value_part = lax.cond(jnp.any(allowed), compute, passby, running)
        return (running, (key_part, value_part))
    start_state = jnp.zeros((rows, heads_here, group, HEAD_DIM), jnp.float32)
    query_sum, (key_parts, value_parts) = lax.scan(step, start_state, jnp.arange(count))
    return ((query_sum * scale).reshape(rows, -1), (key_parts * scale).reshape(total, -1), value_parts.reshape(total, -1))

def reference(inputs, cotangent, segments, first_gain, second_gain, third_gain, fourth_gain, query_weight, key_weight, value_weight, output_weight, gate_weight, up_weight, down_weight):
    total = inputs.shape[0]
    width = inputs.shape[1]
    positions = jnp.arange(total, dtype=jnp.int32)
    cosine, sine = rotation(positions)
    whole = inputs.astype(jnp.float32)
    normed = rms_forward(whole, first_gain).astype(jnp.bfloat16)
    queries = rope_apply(jnp.dot(normed, query_weight, preferred_element_type=jnp.float32), cosine, sine, False).astype(jnp.bfloat16)
    keys = rope_apply(jnp.dot(normed, key_weight, preferred_element_type=jnp.float32), cosine, sine, False).astype(jnp.bfloat16)
    values = jnp.dot(normed, value_weight, preferred_element_type=jnp.float32).astype(jnp.bfloat16)
    qblock = min(1024, total)
    qcount = total // qblock

    def attend(carry, index):
        start = index * qblock
        mixed, log_totals = local_attention(lax.dynamic_slice_in_dim(queries, start, qblock, 0), keys, values, lax.dynamic_slice_in_dim(positions, start, qblock, 0), lax.dynamic_slice_in_dim(segments, start, qblock, 0), segments)
        return (carry, (mixed, log_totals))
    unused, (mixed_parts, log_parts) = lax.scan(attend, jnp.zeros((), jnp.float32), jnp.arange(qcount))
    mixed_all = mixed_parts.reshape(total, -1)
    tblock = min(4096, total)
    tcount = total // tblock

    def feed(carry, index):
        down_sum, gate_sum, up_sum, output_sum, second_sum, third_sum, fourth_sum = carry
        start = index * tblock
        rows_in = lax.dynamic_slice_in_dim(whole, start, tblock, 0)
        mixed_rows = lax.dynamic_slice_in_dim(mixed_all, start, tblock, 0)
        upstream = lax.dynamic_slice_in_dim(cotangent, start, tblock, 0).astype(jnp.float32)
        attended = jnp.dot(mixed_rows, output_weight.T, preferred_element_type=jnp.float32)
        middle = rows_in + rms_forward(attended, second_gain)
        ffn_in = rms_forward(middle, third_gain).astype(jnp.bfloat16)
        gate = jnp.dot(ffn_in, gate_weight.T, preferred_element_type=jnp.float32)
        up = jnp.dot(ffn_in, up_weight.T, preferred_element_type=jnp.float32)
        hidden = (gelu_value(gate) * up).astype(jnp.bfloat16)
        mlp = jnp.dot(hidden, down_weight, preferred_element_type=jnp.float32)
        layer_rows = middle + rms_forward(mlp, fourth_gain)
        mlp_grad, fourth_part = rms_backward(mlp, fourth_gain, upstream)
        mlp_round = mlp_grad.astype(jnp.bfloat16)
        hidden_grad = jnp.dot(mlp_round, down_weight.T, preferred_element_type=jnp.float32)
        gate_delta = (hidden_grad * up * gelu_slope(gate)).astype(jnp.bfloat16)
        up_delta = (hidden_grad * gelu_value(gate)).astype(jnp.bfloat16)
        down_sum = down_sum + jnp.dot(hidden.T, mlp_round, preferred_element_type=jnp.float32)
        gate_sum = gate_sum + jnp.dot(gate_delta.T, ffn_in, preferred_element_type=jnp.float32)
        up_sum = up_sum + jnp.dot(up_delta.T, ffn_in, preferred_element_type=jnp.float32)
        ffn_in_grad = jnp.dot(gate_delta, gate_weight, preferred_element_type=jnp.float32) + jnp.dot(up_delta, up_weight, preferred_element_type=jnp.float32)
        middle_part, third_part = rms_backward(middle, third_gain, ffn_in_grad)
        middle_grad = upstream + middle_part
        attended_grad, second_part = rms_backward(attended, second_gain, middle_grad)
        attended_round = attended_grad.astype(jnp.bfloat16)
        output_sum = output_sum + jnp.dot(attended_round.T, mixed_rows, preferred_element_type=jnp.float32)
        mixed_grad = jnp.dot(attended_round, output_weight, preferred_element_type=jnp.float32).astype(jnp.bfloat16)
        carry = (down_sum, gate_sum, up_sum, output_sum, second_sum + second_part, third_sum + third_part, fourth_sum + fourth_part)
        return (carry, (layer_rows, middle_grad, mixed_grad))
    start_state = (jnp.zeros((FF, width), jnp.float32), jnp.zeros((FF, width), jnp.float32), jnp.zeros((FF, width), jnp.float32), jnp.zeros(output_weight.shape, jnp.float32), jnp.zeros((width,), jnp.float32), jnp.zeros((width,), jnp.float32), jnp.zeros((width,), jnp.float32))
    sums, (layer_parts, middle_parts, grad_parts) = lax.scan(feed, start_state, jnp.arange(tcount))
    down_grad, gate_grad, up_grad, output_grad, second_grad, third_grad, fourth_grad = sums
    layer_out = layer_parts.reshape(total, width)
    middle_grads = middle_parts.reshape(total, width)
    mixed_grads = grad_parts.reshape(total, -1)

    def attend_back(carry, index):
        key_total, value_total = carry
        start = index * qblock
        query_part, key_part, value_part = local_attention_backward(lax.dynamic_slice_in_dim(queries, start, qblock, 0), keys, values, lax.dynamic_slice_in_dim(mixed_all, start, qblock, 0), log_parts[index], lax.dynamic_slice_in_dim(mixed_grads, start, qblock, 0), lax.dynamic_slice_in_dim(positions, start, qblock, 0), lax.dynamic_slice_in_dim(segments, start, qblock, 0), segments)
        return ((key_total + key_part, value_total + value_part), query_part)
    start_back = (jnp.zeros(keys.shape, jnp.float32), jnp.zeros(values.shape, jnp.float32))
    (keys_grad, values_grad), query_parts = lax.scan(attend_back, start_back, jnp.arange(qcount))
    queries_grad = query_parts.reshape(total, -1)
    query_back = rope_apply(queries_grad, cosine, sine, True).astype(jnp.bfloat16)
    key_back = rope_apply(keys_grad, cosine, sine, True).astype(jnp.bfloat16)
    value_back = values_grad.astype(jnp.bfloat16)
    normed_grad = jnp.dot(query_back, query_weight.T, preferred_element_type=jnp.float32) + jnp.dot(key_back, key_weight.T, preferred_element_type=jnp.float32) + jnp.dot(value_back, value_weight.T, preferred_element_type=jnp.float32)
    query_grad = jnp.dot(normed.T, query_back, preferred_element_type=jnp.float32)
    key_grad = jnp.dot(normed.T, key_back, preferred_element_type=jnp.float32)
    value_grad = jnp.dot(normed.T, value_back, preferred_element_type=jnp.float32)
    input_part, first_grad = rms_backward(whole, first_gain, normed_grad)
    input_grad = middle_grads + input_part
    return (layer_out, input_grad, first_grad, second_grad, third_grad, fourth_grad, query_grad, key_grad, value_grad, output_grad, gate_grad, up_grad, down_grad)
```

```python
import jax
import jax.numpy as jnp
from jax import lax
from jax.sharding import PartitionSpec as P

HEAD_DIM = 256


epsilon = 1e-06
softcap = 50.0
rope_base = 10000.0
gelu_coef = 0.7978845608028654
cubic_coef = 0.044715


def rms_forward(values, gain):
    scaling = lax.rsqrt(jnp.mean(values * values, axis=-1, keepdims=True) + epsilon)
    return values * scaling * (1.0 + gain.astype(jnp.float32))


def rms_backward(values, gain, upstream):
    scaling = lax.rsqrt(jnp.mean(values * values, axis=-1, keepdims=True) + epsilon)
    weighted = upstream * (1.0 + gain.astype(jnp.float32))
    inner = jnp.mean(weighted * values, axis=-1, keepdims=True)
    grad_values = scaling * weighted - values * (scaling * scaling * scaling) * inner
    grad_gain = jnp.sum(upstream * values * scaling, axis=0)
    return (grad_values, grad_gain)


def rotation(positions):
    half = HEAD_DIM // 2
    frequency = jnp.power(rope_base, -jnp.arange(half, dtype=jnp.float32) / half)
    angles = positions.astype(jnp.float32)[:, None] * frequency[None, :]
    return (jnp.cos(angles), jnp.sin(angles))


def rope_apply(values, cosine, sine, inverse):
    rows = values.shape[0]
    half = HEAD_DIM // 2
    shaped = values.reshape(rows, -1, HEAD_DIM)
    first = shaped[:, :, :half]
    second = shaped[:, :, half:]
    cosine_row = cosine[:, None, :]
    sine_row = sine[:, None, :]
    if inverse:
        sine_row = -sine_row
    turned = jnp.concatenate(
        [first * cosine_row - second * sine_row, second * cosine_row + first * sine_row], axis=-1
    )
    return turned.reshape(rows, -1)


def gelu_value(gate):
    bent = jnp.tanh(gelu_coef * (gate + cubic_coef * gate * gate * gate))
    return 0.5 * gate * (1.0 + bent)


def gelu_slope(gate):
    bent = jnp.tanh(gelu_coef * (gate + cubic_coef * gate * gate * gate))
    return 0.5 * (1.0 + bent) + 0.5 * gate * (1.0 - bent * bent) * gelu_coef * (
        1.0 + 3.0 * cubic_coef * gate * gate
    )


def contract_rows(left, right):
    return lax.dot_general(
        left, right, (((0,), (0,)), ((), ())), preferred_element_type=jnp.float32
    )


def contract_cols(left, right):
    return lax.dot_general(
        left, right, (((1,), (1,)), ((), ())), preferred_element_type=jnp.float32
    )


def local_attention(query, keys, values, query_pos, query_start, key_pos, blocks):
    rows = query.shape[0]
    heads_here = keys.shape[1] // HEAD_DIM
    group = query.shape[1] // keys.shape[1]
    block = keys.shape[0] // blocks
    scale = HEAD_DIM ** (-0.5)
    shaped = query.reshape(rows, heads_here, group, HEAD_DIM)

    def step(state, index):
        start = index * block
        key_block = lax.dynamic_slice_in_dim(keys, start, block, 0).reshape(
            block, heads_here, HEAD_DIM
        )
        value_block = lax.dynamic_slice_in_dim(values, start, block, 0).reshape(
            block, heads_here, HEAD_DIM
        )
        key_at = lax.dynamic_slice_in_dim(key_pos, start, block, 0)
        allowed = (key_at[None, :] >= query_start[:, None]) & (
            key_at[None, :] <= query_pos[:, None]
        )

        def compute(inner):
            scores = (
                jnp.einsum("qcgd,kcd->cgqk", shaped, key_block, preferred_element_type=jnp.float32)
                * scale
            )
            expo = jnp.where(allowed, jnp.exp(softcap * jnp.tanh(scores / softcap)), 0.0)
            added = jnp.einsum(
                "cgqk,kcd->qcgd",
                expo.astype(jnp.bfloat16),
                value_block,
                preferred_element_type=jnp.float32,
            )
            return (inner[0] + added, inner[1] + jnp.sum(expo, axis=-1))

        return (lax.cond(jnp.any(allowed), compute, lambda inner: inner, state), None)

    start_state = (
        jnp.zeros((rows, heads_here, group, HEAD_DIM), jnp.float32),
        jnp.zeros((heads_here, group, rows), jnp.float32),
    )
    (numerator, totals), unused = lax.scan(step, start_state, jnp.arange(blocks))
    mixed = numerator / jnp.transpose(totals, (2, 0, 1))[..., None]
    return (mixed.astype(jnp.bfloat16).reshape(rows, -1), jnp.log(totals))


def local_attention_backward(
    query, keys, values, mixed, log_totals, mixed_grad, query_pos, query_start, key_pos, blocks
):
    rows = query.shape[0]
    heads_here = keys.shape[1] // HEAD_DIM
    group = query.shape[1] // keys.shape[1]
    total = keys.shape[0]
    block = total // blocks
    scale = HEAD_DIM ** (-0.5)
    shaped = query.reshape(rows, heads_here, group, HEAD_DIM)
    outgrad = mixed_grad.reshape(rows, heads_here, group, HEAD_DIM)
    result = mixed.reshape(rows, heads_here, group, HEAD_DIM)
    delta = jnp.einsum("qcgd,qcgd->cgq", outgrad, result, preferred_element_type=jnp.float32)

    def step(running, index):
        start = index * block
        key_block = lax.dynamic_slice_in_dim(keys, start, block, 0).reshape(
            block, heads_here, HEAD_DIM
        )
        value_block = lax.dynamic_slice_in_dim(values, start, block, 0).reshape(
            block, heads_here, HEAD_DIM
        )
        key_at = lax.dynamic_slice_in_dim(key_pos, start, block, 0)
        allowed = (key_at[None, :] >= query_start[:, None]) & (
            key_at[None, :] <= query_pos[:, None]
        )

        def compute(inner):
            scores = (
                jnp.einsum("qcgd,kcd->cgqk", shaped, key_block, preferred_element_type=jnp.float32)
                * scale
            )
            bent = jnp.tanh(scores / softcap)
            probs = jnp.where(allowed, jnp.exp(softcap * bent - log_totals[..., None]), 0.0)
            value_part = jnp.einsum(
                "cgqk,qcgd->kcd",
                probs.astype(jnp.bfloat16),
                outgrad,
                preferred_element_type=jnp.float32,
            )
            prob_grad = jnp.einsum(
                "qcgd,kcd->cgqk", outgrad, value_block, preferred_element_type=jnp.float32
            )
            score_grad = (probs * (prob_grad - delta[..., None]) * (1.0 - bent * bent)).astype(
                jnp.bfloat16
            )
            inner = inner + jnp.einsum(
                "cgqk,kcd->qcgd", score_grad, key_block, preferred_element_type=jnp.float32
            )
            key_part = jnp.einsum(
                "cgqk,qcgd->kcd", score_grad, shaped, preferred_element_type=jnp.float32
            )
            both = jnp.concatenate(
                [key_part.reshape(block, -1) * scale, value_part.reshape(block, -1)], axis=1
            )
            return (inner, both.astype(jnp.bfloat16))

        def passby(inner):
            return (inner, jnp.zeros((block, 2 * heads_here * HEAD_DIM), jnp.bfloat16))

        return lax.cond(jnp.any(allowed), compute, passby, running)

    start_state = jnp.zeros((rows, heads_here, group, HEAD_DIM), jnp.float32)
    query_sum, parts = lax.scan(step, start_state, jnp.arange(blocks))
    return ((query_sum * scale).reshape(rows, -1), parts.reshape(total, -1))


def after(value, *others):
    return lax.optimization_barrier((value,) + others)[0]


def on_device(
    inputs,
    cotangent,
    segments,
    first_gain,
    second_gain,
    third_gain,
    fourth_gain,
    query_weight,
    key_weight,
    value_weight,
    output_weight,
    gate_weight,
    up_weight,
    down_weight,
):
    tokens = inputs.shape[0]
    width = inputs.shape[1]
    own_rows = query_weight.shape[0]
    seq_count = lax.axis_size("seq")
    count = lax.axis_size("fsdp")
    seq_rank = lax.axis_index("seq")
    fsdp_rank = lax.axis_index("fsdp")
    half = count // 2
    bf16 = jnp.bfloat16
    head_rows = tokens * seq_count
    query_cols = query_weight.shape[1] // seq_count
    key_cols = key_weight.shape[1] // seq_count

    cycle = [2 * i for i in range(half)] + [2 * i + 1 for i in reversed(range(half))]
    ahead = [(cycle[i], cycle[(i + 1) % count]) for i in range(count)]
    behind = [(b, a) for a, b in ahead]
    place = jnp.where(fsdp_rank % 2 == 0, fsdp_rank // 2, count - 1 - fsdp_rank // 2)

    def rank_at(step):
        spot = lax.rem(place + step + count, count)
        return jnp.where(spot < half, 2 * spot, 2 * (count - 1 - spot) + 1)

    def flip(value, bits):
        return lax.ppermute(value, "seq", [(i, i ^ bits) for i in range(seq_count)])

    def ring_gather(value, axis):
        groups = [[value]]
        from_behind = value
        from_ahead = value
        for unused in range(half - 1):
            from_behind = lax.ppermute(from_behind, "fsdp", ahead)
            from_ahead = lax.ppermute(from_ahead, "fsdp", behind)
            groups.append([from_behind, from_ahead])
        cut = value.shape[axis] // 2
        low = lax.slice_in_dim(from_behind, 0, cut, axis=axis)
        high = lax.slice_in_dim(from_ahead, cut, value.shape[axis], axis=axis)
        low = lax.ppermute(low, "fsdp", ahead)
        high = lax.ppermute(high, "fsdp", behind)
        groups.append([jnp.concatenate([low, high], axis=axis)])
        return groups

    def ring_scatter(part_at, axis):
        far = part_at(half)
        cut = far.shape[axis] // 2
        low = lax.slice_in_dim(far, 0, cut, axis=axis).astype(bf16)
        high = lax.slice_in_dim(far, cut, far.shape[axis], axis=axis).astype(bf16)
        low = lax.ppermute(low, "fsdp", ahead).astype(jnp.float32)
        high = lax.ppermute(high, "fsdp", behind).astype(jnp.float32)
        blank = jnp.zeros_like(low)
        onward = jnp.concatenate([low, blank], axis=axis)
        back = jnp.concatenate([blank, high], axis=axis)
        for step in range(half - 1, 0, -1):
            onward = (part_at(step) + onward).astype(bf16)
            back = (part_at(-step) + back).astype(bf16)
            onward = lax.ppermute(onward, "fsdp", ahead).astype(jnp.float32)
            back = lax.ppermute(back, "fsdp", behind).astype(jnp.float32)
        return part_at(0) + onward + back

    def seq_gather(value):
        across = flip(value, 2)
        beside = flip(value, 1)
        return [value, beside, across, flip(across, 1)]

    def seq_scatter(parts):
        near = flip(parts[1].astype(bf16), 1).astype(jnp.float32)
        far = flip(parts[3].astype(bf16), 1).astype(jnp.float32)
        across = flip((parts[2] + far).astype(bf16), 2).astype(jnp.float32)
        return parts[0] + near + across

    packed = jnp.concatenate([first_gain, second_gain, third_gain, fourth_gain])
    lanes = -(-packed.shape[0] // 128) * 128
    packed = jnp.pad(packed, (0, lanes - packed.shape[0])).reshape(1, 1, lanes)
    packed = jnp.broadcast_to(packed, (1, 8, lanes))
    gains = lax.all_gather(packed, ("seq", "fsdp"), axis=0, tiled=True)[:, 0, : 4 * own_rows]
    gains = jnp.transpose(gains.reshape(-1, 4, own_rows), (1, 0, 2)).reshape(4, width)
    gain_one, gain_two, gain_three, gain_four = gains[0], gains[1], gains[2], gains[3]

    def columns(weight, rank, size):
        return lax.dynamic_slice_in_dim(weight, rank * size, size, 1)

    def head_columns(rank):
        return jnp.concatenate(
            [
                columns(query_weight, rank, query_cols),
                columns(key_weight, rank, key_cols),
                columns(value_weight, rank, key_cols),
            ],
            axis=1,
        )

    def exchange(pick):
        pieces = [pick(seq_rank)] + [
            flip(pick(seq_rank ^ j), j) for j in range(1, seq_count)
        ]
        chunk = jnp.zeros((seq_count,) + pieces[0].shape, bf16)
        for j, piece in enumerate(pieces):
            chunk = lax.dynamic_update_slice(chunk, piece[None], (seq_rank ^ j, 0, 0))
        return chunk

    def assemble(groups):
        cols = groups[0][0].shape[2]
        whole_weight = jnp.zeros((seq_count, count, own_rows, cols), bf16)
        for step, group in enumerate(groups):
            for rank, piece in zip((rank_at(-step), rank_at(step)), group):
                whole_weight = lax.dynamic_update_slice(
                    whole_weight, piece[:, None], (0, rank, 0, 0)
                )
        return whole_weight.reshape(width, cols)

    head_chunk = exchange(head_columns)
    rows_in = seq_gather(after(inputs, head_chunk))
    out_chunk = exchange(lambda rank: columns(output_weight, rank, query_cols))
    head_groups = ring_gather(head_chunk, 2)
    in_full = assemble(head_groups)

    def block_pos(rank):
        return jnp.concatenate(
            [
                (rank * seq_count + (seq_rank ^ j)) * tokens + jnp.arange(tokens, dtype=jnp.int32)
                for j in range(seq_count)
            ]
        )

    head_pos = block_pos(fsdp_rank)
    head_seg = jnp.concatenate(
        [
            lax.dynamic_slice_in_dim(
                segments, (fsdp_rank * seq_count + (seq_rank ^ j)) * tokens, tokens, 0
            )
            for j in range(seq_count)
        ]
    )
    head_start = jnp.sum((segments[None, :] < head_seg[:, None]).astype(jnp.int32), axis=1)

    head_in = jnp.concatenate(rows_in, axis=0).astype(jnp.float32)
    whole = inputs.astype(jnp.float32)
    normed = rms_forward(head_in, gain_one).astype(bf16)
    head_cos, head_sin = rotation(head_pos)
    projected = jnp.dot(normed, in_full, preferred_element_type=jnp.float32)
    turned = rope_apply(projected[:, : query_cols + key_cols], head_cos, head_sin, False)
    query_head = turned[:, :query_cols].astype(bf16)
    pair = jnp.concatenate(
        [turned[:, query_cols:], projected[:, query_cols + key_cols :]], axis=1
    ).astype(bf16)

    up_line = [(i, i + 2) for i in range(count - 2)]
    down_line = [(b, a) for a, b in up_line]
    reach = half // 2

    def sideways(step, reverse):
        to_odd = [(2 * i, 2 * i + 1) for i in range(half)]
        to_even = [(2 * i + 1, 2 * i) for i in range(half)]
        pairs = to_odd if step == 0 else to_even if step == reach else to_odd + to_even
        return [(b, a) for a, b in pairs] if reverse else pairs

    line = [pair]
    for unused in range(reach):
        line.append(lax.ppermute(line[-1], "fsdp", up_line))
    side = [lax.ppermute(line[k], "fsdp", sideways(k, False)) for k in range(reach + 1)]
    out_chunk = after(out_chunk, head_groups[-1][0], pair)
    out_groups = ring_gather(out_chunk, 2)
    out_full = assemble(out_groups)

    pieces = []
    places = []
    for k in range(reach + 1):
        pieces += [line[k], side[k]]
        places += [block_pos(fsdp_rank - 2 * k), block_pos((fsdp_rank ^ 1) - 2 * k)]
    pairs_all = jnp.concatenate(pieces, axis=0)
    key_pos = jnp.concatenate(places)
    key_all = pairs_all[:, :key_cols]
    value_all = pairs_all[:, key_cols:]
    mixed_head, log_totals = local_attention(
        query_head, key_all, value_all, head_pos, head_start, key_pos, reach + 1
    )
    attended_part = contract_cols(mixed_head, out_full)
    attended = seq_scatter(jnp.split(attended_part, seq_count, axis=0))
    middle = whole + rms_forward(attended, gain_two)
    ffn_in = rms_forward(middle, gain_three).astype(bf16)
    upstream = cotangent.astype(jnp.float32)

    gate_units, up_units, down_units = (
        jnp.concatenate(seq_gather(after(weight, rows_in[2])), axis=0)
        for weight in (gate_weight, up_weight, down_weight)
    )

    def joined(groups):
        return [group[0] if len(group) == 1 else jnp.concatenate(group, axis=0) for group in groups]

    def part_of(parts):
        def part_at(step):
            if step == 0:
                return parts[0]
            if abs(step) == half:
                return parts[half]
            part = parts[abs(step)]
            return part[tokens:] if step > 0 else part[:tokens]

        return part_at

    row_groups = joined(ring_gather(ffn_in, 0))
    gates, ups, hiddens, mlp_parts = [], [], [], []
    for rows in row_groups:
        gate = contract_cols(rows, gate_units)
        up = contract_cols(rows, up_units)
        hidden = (gelu_value(gate) * up).astype(bf16)
        gates.append(gate)
        ups.append(up)
        hiddens.append(hidden)
        mlp_parts.append(jnp.dot(hidden, down_units, preferred_element_type=jnp.float32))
    mlp = ring_scatter(part_of(mlp_parts), 0)
    layer_out = middle + rms_forward(mlp, gain_four)
    mlp_grad, fourth_part = rms_backward(mlp, gain_four, upstream)
    mlp_round = mlp_grad.astype(bf16)
    grad_groups = joined(ring_gather(mlp_round, 0))
    gate_deltas, up_deltas, in_parts = [], [], []
    for grads, gate, up in zip(grad_groups, gates, ups):
        hidden_grad = contract_cols(grads, down_units)
        gate_delta = (hidden_grad * up * gelu_slope(gate)).astype(bf16)
        up_delta = (hidden_grad * gelu_value(gate)).astype(bf16)
        gate_deltas.append(gate_delta)
        up_deltas.append(up_delta)
        in_parts.append(
            jnp.dot(gate_delta, gate_units, preferred_element_type=jnp.float32)
            + jnp.dot(up_delta, up_units, preferred_element_type=jnp.float32)
        )
    ffn_in_grad = ring_scatter(part_of(in_parts), 0)

    middle_part, third_part = rms_backward(middle, gain_three, ffn_in_grad)
    middle_grad = upstream + middle_part
    attended_grad, second_part = rms_backward(attended, gain_two, middle_grad)
    attended_round = attended_grad.astype(bf16)
    attended_blocks = seq_gather(attended_round)
    attended_rows = jnp.concatenate(attended_blocks, axis=0)

    all_rows = jnp.concatenate(row_groups, axis=0)
    all_grads = jnp.concatenate(grad_groups, axis=0)

    def unit_grad(left, right):
        full = contract_rows(jnp.concatenate(left, axis=0), right)
        return seq_scatter(jnp.split(after(full, attended_blocks[2]), seq_count, axis=0))

    down_grad = unit_grad(hiddens, all_grads)
    gate_grad = unit_grad(gate_deltas, all_rows)
    up_grad = unit_grad(up_deltas, all_rows)

    mixed_grad_head = jnp.dot(
        attended_rows, out_full, preferred_element_type=jnp.float32
    ).astype(bf16)

    def weight_grad(left, right):
        full = contract_rows(left, right).reshape(seq_count, count, own_rows, -1)
        chunk = ring_scatter(
            lambda step: lax.dynamic_slice_in_dim(full, rank_at(step), 1, 1)[:, 0], 2
        )
        chunk = chunk.astype(bf16)
        return [
            flip(lax.dynamic_slice_in_dim(chunk, seq_rank ^ j, 1, 0)[0], j)
            if j
            else lax.dynamic_slice_in_dim(chunk, seq_rank, 1, 0)[0]
            for j in range(seq_count)
        ]

    def spread(pieces):
        cols = pieces[0].shape[1]
        out = jnp.zeros((own_rows, cols * seq_count), jnp.float32)
        for j, piece in enumerate(pieces):
            out = lax.dynamic_update_slice(
                out, piece.astype(jnp.float32), (0, (seq_rank ^ j) * cols)
            )
        return out

    output_grad = spread(weight_grad(attended_rows, mixed_head))
    queries_grad, pair_parts = local_attention_backward(
        query_head,
        key_all,
        value_all,
        mixed_head,
        log_totals,
        mixed_grad_head,
        head_pos,
        head_start,
        key_pos,
        reach + 1,
    )
    pair_parts = pair_parts.reshape(reach + 1, 2, head_rows, 2 * key_cols)
    total = None
    for k in range(reach, -1, -1):
        here = pair_parts[k, 0].astype(jnp.float32) + lax.ppermute(
            pair_parts[k, 1], "fsdp", sideways(k, True)
        ).astype(jnp.float32)
        if total is not None:
            here = here + lax.ppermute(total.astype(bf16), "fsdp", down_line).astype(jnp.float32)
        total = here
    query_back = rope_apply(queries_grad, head_cos, head_sin, True).astype(bf16)
    key_back = rope_apply(total[:, :key_cols], head_cos, head_sin, True).astype(bf16)
    value_back = total[:, key_cols:].astype(bf16)
    query_grad = spread(weight_grad(normed, query_back))
    pair_back = jnp.concatenate([key_back, value_back], axis=1)
    pair_pieces = weight_grad(normed, pair_back)
    key_grad = spread([piece[:, :key_cols] for piece in pair_pieces])
    value_grad = spread([piece[:, key_cols:] for piece in pair_pieces])
    normed_part = contract_cols(jnp.concatenate([query_back, pair_back], axis=1), in_full)
    normed_grad = seq_scatter(jnp.split(normed_part, seq_count, axis=0))
    head_scaling = lax.rsqrt(jnp.mean(head_in * head_in, axis=-1, keepdims=True) + epsilon)
    first_part = jnp.sum(normed_part * head_in * head_scaling, axis=0)
    input_part, unused = rms_backward(whole, gain_one, normed_grad)
    input_grad = middle_grad + input_part

    gain_parts = jnp.stack([first_part, second_part, third_part, fourth_part])
    gain_parts = gain_parts.reshape(4, seq_count, count, own_rows)
    gain_sums = ring_small(gain_parts, rank_at, ahead, behind, half, count)
    mine = [
        lax.dynamic_slice_in_dim(gain_sums, seq_rank ^ j, 1, 1)[:, 0] for j in range(seq_count)
    ]
    near = flip(mine[1], 1)
    far = flip(mine[3], 1)
    gain_grads = mine[0] + near + flip(mine[2] + far, 2)
    return (
        layer_out,
        input_grad,
        gain_grads[0],
        gain_grads[1],
        gain_grads[2],
        gain_grads[3],
        query_grad,
        key_grad,
        value_grad,
        output_grad,
        gate_grad,
        up_grad,
        down_grad,
    )


def ring_small(parts, rank_at, ahead, behind, half, count):
    def part_at(step):
        return lax.dynamic_slice_in_dim(parts, rank_at(step), 1, 2)[:, :, 0]

    onward = part_at(half)
    back = None
    for step in range(half - 1, -1, -1):
        onward = lax.ppermute(onward, "fsdp", ahead)
        if step:
            onward = onward + part_at(step)
            back = part_at(-step) if back is None else back + part_at(-step)
            back = lax.ppermute(back, "fsdp", behind)
    return part_at(0) + onward + back


def solution(mesh):
    placed = (
        P(("fsdp", "seq"), None),
        P(("fsdp", "seq"), None),
        P(),
        P(("seq", "fsdp")),
        P(("seq", "fsdp")),
        P(("seq", "fsdp")),
        P(("seq", "fsdp")),
        P(("seq", "fsdp"), None),
        P(("seq", "fsdp"), None),
        P(("seq", "fsdp"), None),
        P(("seq", "fsdp"), None),
        P(("seq", "fsdp"), None),
        P(("seq", "fsdp"), None),
        P(("seq", "fsdp"), None),
    )
    return jax.shard_map(
        on_device,
        mesh=mesh,
        in_specs=placed,
        out_specs=(
            P(("fsdp", "seq"), None),
            P(("fsdp", "seq"), None),
            P(("seq", "fsdp")),
            P(("seq", "fsdp")),
            P(("seq", "fsdp")),
            P(("seq", "fsdp")),
            P(("seq", "fsdp"), None),
            P(("seq", "fsdp"), None),
            P(("seq", "fsdp"), None),
            P(("seq", "fsdp"), None),
            P(("seq", "fsdp"), None),
            P(("seq", "fsdp"), None),
            P(("seq", "fsdp"), None),
        ),
        check_vma=False,
    )
```

```python
import functools

import jax
import jax.numpy as jnp
from jax import lax
from jax.experimental import pallas as pl
from jax.experimental.pallas import tpu as pltpu
from jax.sharding import PartitionSpec as P

HEAD_DIM = 256


epsilon = 1e-06
softcap = 50.0
rope_base = 10000.0
gelu_coef = 0.7978845608028654
cubic_coef = 0.044715


def rms_forward(values, gain):
    scaling = lax.rsqrt(jnp.mean(values * values, axis=-1, keepdims=True) + epsilon)
    return values * scaling * (1.0 + gain.astype(jnp.float32))


def rms_backward(values, gain, upstream):
    scaling = lax.rsqrt(jnp.mean(values * values, axis=-1, keepdims=True) + epsilon)
    weighted = upstream * (1.0 + gain.astype(jnp.float32))
    inner = jnp.mean(weighted * values, axis=-1, keepdims=True)
    grad_values = scaling * weighted - values * (scaling * scaling * scaling) * inner
    grad_gain = jnp.sum(upstream * values * scaling, axis=0)
    return (grad_values, grad_gain)


def rotation(positions):
    half = HEAD_DIM // 2
    frequency = jnp.power(rope_base, -jnp.arange(half, dtype=jnp.float32) / half)
    angles = positions.astype(jnp.float32)[:, None] * frequency[None, :]
    return (jnp.cos(angles), jnp.sin(angles))


def rope_apply(values, cosine, sine, inverse):
    rows = values.shape[0]
    half = HEAD_DIM // 2
    shaped = values.reshape(rows, -1, HEAD_DIM)
    first = shaped[:, :, :half]
    second = shaped[:, :, half:]
    cosine_row = cosine[:, None, :]
    sine_row = sine[:, None, :]
    if inverse:
        sine_row = -sine_row
    turned = jnp.concatenate(
        [first * cosine_row - second * sine_row, second * cosine_row + first * sine_row], axis=-1
    )
    return turned.reshape(rows, -1)


def gelu_value(gate):
    bent = jnp.tanh(gelu_coef * (gate + cubic_coef * gate * gate * gate))
    return 0.5 * gate * (1.0 + bent)


def gelu_slope(gate):
    bent = jnp.tanh(gelu_coef * (gate + cubic_coef * gate * gate * gate))
    return 0.5 * (1.0 + bent) + 0.5 * gate * (1.0 - bent * bent) * gelu_coef * (
        1.0 + 3.0 * cubic_coef * gate * gate
    )


def contract_rows(left, right):
    return lax.dot_general(
        left, right, (((0,), (0,)), ((), ())), preferred_element_type=jnp.float32
    )


def contract_cols(left, right):
    return lax.dot_general(
        left, right, (((1,), (1,)), ((), ())), preferred_element_type=jnp.float32
    )


def attend_kernel(heads, live_ref, query_ref, pair_ref, at_ref, pos_ref, start_ref, mixed_ref, log_ref, sums, totals):
    step = pl.program_id(0)
    scale = HEAD_DIM ** (-0.5)

    @pl.when(step == 0)
    def _():
        sums[...] = jnp.zeros_like(sums)
        totals[...] = jnp.zeros_like(totals)

    @pl.when(live_ref[step] > 0)
    def _():
        keys = pair_ref[:, :HEAD_DIM]
        turned = pair_ref[:, HEAD_DIM:].T
        allowed = (at_ref[...] >= start_ref[...]) & (at_ref[...] <= pos_ref[...])
        for head in range(heads):
            cols = slice(head * HEAD_DIM, (head + 1) * HEAD_DIM)
            bent = jnp.tanh(contract_cols(keys, query_ref[:, cols]) * (scale / softcap))
            expo = jnp.where(allowed, jnp.exp(softcap * bent), 0.0)
            totals[head : head + 1, :] += jnp.sum(expo, axis=0, keepdims=True)
            sums[head] += jnp.dot(turned, expo.astype(jnp.bfloat16), preferred_element_type=jnp.float32)

    @pl.when(step == pl.num_programs(0) - 1)
    def _():
        log_ref[...] = jnp.log(totals[...])
        for head in range(heads):
            cols = slice(head * HEAD_DIM, (head + 1) * HEAD_DIM)
            mixed = sums[head] / totals[head : head + 1, :]
            mixed_ref[:, cols] = mixed.T.astype(jnp.bfloat16)


def attend(live, query, pairs, key_at, query_pos, query_start, block):
    rows, width = query.shape
    heads = width // HEAD_DIM
    steps = pairs.shape[0] // block
    row = pl.BlockSpec((1, rows), lambda i, live: (0, 0))
    return pl.pallas_call(
        functools.partial(attend_kernel, heads),
        grid_spec=pltpu.PrefetchScalarGridSpec(
            num_scalar_prefetch=1,
            grid=(steps,),
            in_specs=[
                pl.BlockSpec((rows, width), lambda i, live: (0, 0)),
                pl.BlockSpec((block, pairs.shape[1]), lambda i, live: (i, 0)),
                pl.BlockSpec((block, 1), lambda i, live: (i, 0)),
                row,
                row,
            ],
            out_specs=[
                pl.BlockSpec((rows, width), lambda i, live: (0, 0)),
                pl.BlockSpec((heads, rows), lambda i, live: (0, 0)),
            ],
            scratch_shapes=[
                pltpu.VMEM((heads, HEAD_DIM, rows), jnp.float32),
                pltpu.VMEM((heads, rows), jnp.float32),
            ],
        ),
        out_shape=[
            jax.ShapeDtypeStruct((rows, width), jnp.bfloat16),
            jax.ShapeDtypeStruct((heads, rows), jnp.float32),
        ],
        cost_estimate=pl.CostEstimate(
            flops=4 * rows * width * pairs.shape[0],
            bytes_accessed=2 * pairs.size + 4 * query.size,
            transcendentals=2 * rows * heads * pairs.shape[0],
        ),
        name="attend",
    )(live, query, pairs, key_at[:, None], query_pos[None, :], query_start[None, :])


def attend_back_kernel(heads, first, live_ref, query_ref, grad_ref, pair_ref, at_ref, pos_ref, start_ref, log_ref, delta_ref, query_grad_ref, pair_grad_ref, sums):
    step = pl.program_id(0)
    scale = HEAD_DIM ** (-0.5)

    @pl.when(step == 0)
    def _():
        sums[...] = jnp.zeros_like(sums)

    @pl.when(live_ref[step + first] == 0)
    def _():
        pair_grad_ref[...] = jnp.zeros_like(pair_grad_ref)

    @pl.when(live_ref[step + first] > 0)
    def _():
        keys = pair_ref[:, :HEAD_DIM]
        values = pair_ref[:, HEAD_DIM:]
        allowed = (at_ref[...] >= start_ref[...]) & (at_ref[...] <= pos_ref[...])
        key_grad = None
        value_grad = None
        for head in range(heads):
            cols = slice(head * HEAD_DIM, (head + 1) * HEAD_DIM)
            query = query_ref[:, cols]
            grad = grad_ref[:, cols]
            bent = jnp.tanh(contract_cols(keys, query) * (scale / softcap))
            probs = jnp.where(allowed, jnp.exp(softcap * bent - log_ref[head : head + 1, :]), 0.0)
            value_part = jnp.dot(probs.astype(jnp.bfloat16), grad, preferred_element_type=jnp.float32)
            slope = contract_cols(values, grad) - delta_ref[head : head + 1, :]
            score = (probs * slope * (1.0 - bent * bent)).astype(jnp.bfloat16)
            key_part = jnp.dot(score, query, preferred_element_type=jnp.float32)
            sums[:, cols] += contract_rows(score, keys)
            key_grad = key_part if key_grad is None else key_grad + key_part
            value_grad = value_part if value_grad is None else value_grad + value_part
        pair_grad_ref[:, :HEAD_DIM] = (key_grad * scale).astype(jnp.bfloat16)
        pair_grad_ref[:, HEAD_DIM:] = value_grad.astype(jnp.bfloat16)

    @pl.when(step == pl.num_programs(0) - 1)
    def _():
        query_grad_ref[...] = sums[...] * scale


def attend_back(
    live, query, grad, pairs, key_at, query_pos, query_start, log_totals, delta, block, first, steps
):
    rows, width = query.shape
    heads = width // HEAD_DIM
    row = pl.BlockSpec((1, rows), lambda i, live: (0, 0))
    head_row = pl.BlockSpec((heads, rows), lambda i, live: (0, 0))
    full = pl.BlockSpec((rows, width), lambda i, live: (0, 0))
    pair_spec = pl.BlockSpec((block, pairs.shape[1]), lambda i, live: (i + first, 0))
    out_spec = pl.BlockSpec((block, pairs.shape[1]), lambda i, live: (i, 0))
    return pl.pallas_call(
        functools.partial(attend_back_kernel, heads, first),
        grid_spec=pltpu.PrefetchScalarGridSpec(
            num_scalar_prefetch=1,
            grid=(steps,),
            in_specs=[
                full,
                full,
                pair_spec,
                pl.BlockSpec((block, 1), lambda i, live: (i + first, 0)),
                row,
                row,
                head_row,
                head_row,
            ],
            out_specs=[full, out_spec],
            scratch_shapes=[pltpu.VMEM((rows, width), jnp.float32)],
        ),
        out_shape=[
            jax.ShapeDtypeStruct((rows, width), jnp.float32),
            jax.ShapeDtypeStruct((steps * block, pairs.shape[1]), jnp.bfloat16),
        ],
        cost_estimate=pl.CostEstimate(
            flops=10 * rows * width * steps * block,
            bytes_accessed=4 * steps * block * width + 8 * query.size,
            transcendentals=2 * rows * heads * steps * block,
        ),
        name="attend_back",
    )(live, query, grad, pairs, key_at[:, None], query_pos[None, :], query_start[None, :], log_totals, delta)


def after(value, *others):
    return lax.optimization_barrier((value,) + others)[0]


def on_device(
    inputs,
    cotangent,
    segments,
    first_gain,
    second_gain,
    third_gain,
    fourth_gain,
    query_weight,
    key_weight,
    value_weight,
    output_weight,
    gate_weight,
    up_weight,
    down_weight,
):
    tokens = inputs.shape[0]
    width = inputs.shape[1]
    own_rows = query_weight.shape[0]
    seq_count = lax.axis_size("seq")
    count = lax.axis_size("fsdp")
    seq_rank = lax.axis_index("seq")
    fsdp_rank = lax.axis_index("fsdp")
    half = count // 2
    bf16 = jnp.bfloat16
    head_rows = tokens * seq_count
    query_cols = query_weight.shape[1] // seq_count
    key_cols = key_weight.shape[1] // seq_count

    cycle = [2 * i for i in range(half)] + [2 * i + 1 for i in reversed(range(half))]
    ahead = [(cycle[i], cycle[(i + 1) % count]) for i in range(count)]
    behind = [(b, a) for a, b in ahead]
    place = jnp.where(fsdp_rank % 2 == 0, fsdp_rank // 2, count - 1 - fsdp_rank // 2)

    def rank_at(step):
        spot = lax.rem(place + step + count, count)
        return jnp.where(spot < half, 2 * spot, 2 * (count - 1 - spot) + 1)

    def flip(value, bits):
        return lax.ppermute(value, "seq", [(i, i ^ bits) for i in range(seq_count)])

    def ring_gather(value, axis):
        groups = [[value]]
        from_behind = value
        from_ahead = value
        for unused in range(half - 1):
            from_behind = lax.ppermute(from_behind, "fsdp", ahead)
            from_ahead = lax.ppermute(from_ahead, "fsdp", behind)
            groups.append([from_behind, from_ahead])
        cut = value.shape[axis] // 2
        low = lax.slice_in_dim(from_behind, 0, cut, axis=axis)
        high = lax.slice_in_dim(from_ahead, cut, value.shape[axis], axis=axis)
        low = lax.ppermute(low, "fsdp", ahead)
        high = lax.ppermute(high, "fsdp", behind)
        groups.append([jnp.concatenate([low, high], axis=axis)])
        return groups

    def ring_scatter(part_at, axis):
        far = part_at(half)
        cut = far.shape[axis] // 2
        low = lax.slice_in_dim(far, 0, cut, axis=axis).astype(bf16)
        high = lax.slice_in_dim(far, cut, far.shape[axis], axis=axis).astype(bf16)
        low = lax.ppermute(low, "fsdp", ahead).astype(jnp.float32)
        high = lax.ppermute(high, "fsdp", behind).astype(jnp.float32)
        blank = jnp.zeros_like(low)
        onward = jnp.concatenate([low, blank], axis=axis)
        back = jnp.concatenate([blank, high], axis=axis)
        for step in range(half - 1, 0, -1):
            onward = (part_at(step) + onward).astype(bf16)
            back = (part_at(-step) + back).astype(bf16)
            onward = lax.ppermute(onward, "fsdp", ahead).astype(jnp.float32)
            back = lax.ppermute(back, "fsdp", behind).astype(jnp.float32)
        return part_at(0) + onward + back

    def seq_gather(value):
        across = flip(value, 2)
        beside = flip(value, 1)
        return [value, beside, across, flip(across, 1)]

    def seq_scatter(parts):
        near = flip(parts[1].astype(bf16), 1).astype(jnp.float32)
        far = flip(parts[3].astype(bf16), 1).astype(jnp.float32)
        across = flip((parts[2] + far).astype(bf16), 2).astype(jnp.float32)
        return parts[0] + near + across

    def turn(value, step):
        return lax.ppermute(value, "fsdp", [(i, (i + step) % count) for i in range(count)])

    packed = jnp.stack([first_gain, second_gain, third_gain, fourth_gain])
    row = jnp.zeros((seq_count, 4, own_rows), bf16)
    for j in range(seq_count):
        piece = flip(packed, j) if j else packed
        row = lax.dynamic_update_slice(row, piece[None], (seq_rank ^ j, 0, 0))
    gains = jnp.zeros((count, seq_count, 4, own_rows), bf16)
    for step in range(count):
        piece = turn(row, step) if step else row
        gains = lax.dynamic_update_slice(
            gains, piece[None], (lax.rem(fsdp_rank - step + count, count), 0, 0, 0)
        )
    gains = jnp.transpose(gains, (2, 1, 0, 3)).reshape(4, width)
    gain_one, gain_two, gain_three, gain_four = gains[0], gains[1], gains[2], gains[3]

    def columns(weight, rank, size):
        return lax.dynamic_slice_in_dim(weight, rank * size, size, 1)

    def head_columns(rank):
        return jnp.concatenate(
            [
                columns(query_weight, rank, query_cols),
                columns(key_weight, rank, key_cols),
                columns(value_weight, rank, key_cols),
            ],
            axis=1,
        )

    def exchange(pick):
        pieces = [pick(seq_rank)] + [
            flip(pick(seq_rank ^ j), j) for j in range(1, seq_count)
        ]
        chunk = jnp.zeros((seq_count,) + pieces[0].shape, bf16)
        for j, piece in enumerate(pieces):
            chunk = lax.dynamic_update_slice(chunk, piece[None], (seq_rank ^ j, 0, 0))
        return chunk

    def assemble(groups):
        cols = groups[0][0].shape[2]
        whole_weight = jnp.zeros((seq_count, count, own_rows, cols), bf16)
        for step, group in enumerate(groups):
            for rank, piece in zip((rank_at(-step), rank_at(step)), group):
                whole_weight = lax.dynamic_update_slice(
                    whole_weight, piece[:, None], (0, rank, 0, 0)
                )
        return whole_weight.reshape(width, cols)

    head_chunk = exchange(head_columns)
    rows_in = seq_gather(after(inputs, head_chunk))
    out_chunk = exchange(lambda rank: columns(output_weight, rank, query_cols))
    head_groups = ring_gather(head_chunk, 2)
    in_full = assemble(head_groups)

    def block_pos(rank):
        return jnp.concatenate(
            [
                (rank * seq_count + (seq_rank ^ j)) * tokens + jnp.arange(tokens, dtype=jnp.int32)
                for j in range(seq_count)
            ]
        )

    head_pos = block_pos(fsdp_rank)
    head_seg = jnp.concatenate(
        [
            lax.dynamic_slice_in_dim(
                segments, (fsdp_rank * seq_count + (seq_rank ^ j)) * tokens, tokens, 0
            )
            for j in range(seq_count)
        ]
    )
    head_start = jnp.sum((segments[None, :] < head_seg[:, None]).astype(jnp.int32), axis=1)

    head_in = jnp.concatenate(rows_in, axis=0).astype(jnp.float32)
    whole = inputs.astype(jnp.float32)
    normed = rms_forward(head_in, gain_one).astype(bf16)
    head_cos, head_sin = rotation(head_pos)
    projected = jnp.dot(normed, in_full, preferred_element_type=jnp.float32)
    turned = rope_apply(projected[:, : query_cols + key_cols], head_cos, head_sin, False)
    query_head = turned[:, :query_cols].astype(bf16)
    pair = jnp.concatenate(
        [turned[:, query_cols:], projected[:, query_cols + key_cols :]], axis=1
    ).astype(bf16)

    up_line = [(i, i + 2) for i in range(count - 2)]
    down_line = [(b, a) for a, b in up_line]
    reach = half // 2

    def sideways(step, reverse):
        to_odd = [(2 * i, 2 * i + 1) for i in range(half)]
        to_even = [(2 * i + 1, 2 * i) for i in range(half)]
        pairs = to_odd if step == 0 else to_even if step == reach else to_odd + to_even
        return [(b, a) for a, b in pairs] if reverse else pairs

    line = [pair]
    for unused in range(reach):
        line.append(lax.ppermute(line[-1], "fsdp", up_line))
    side = [lax.ppermute(line[k], "fsdp", sideways(k, False)) for k in range(reach + 1)]
    out_chunk = after(out_chunk, line[reach])
    out_groups = ring_gather(out_chunk, 2)
    out_full = assemble(out_groups)

    pieces = []
    places = []
    for k in range(reach + 1):
        pieces += [line[k], side[k]]
        places += [block_pos(fsdp_rank - 2 * k), block_pos((fsdp_rank ^ 1) - 2 * k)]
    pairs_all = jnp.concatenate(pieces, axis=0)
    key_pos = jnp.concatenate(places)
    low_start = jnp.min(head_start)
    ranks = []
    for k in range(reach + 1):
        ranks += [fsdp_rank - 2 * k, (fsdp_rank ^ 1) - 2 * k]
    ranks = jnp.stack(ranks)
    live = (ranks >= 0) & (ranks <= fsdp_rank) & ((ranks + 1) * head_rows > low_start)
    live = live.astype(jnp.int32)
    mixed_head, log_totals = attend(
        live, query_head, pairs_all, key_pos, head_pos, head_start, head_rows
    )
    attended_part = contract_cols(mixed_head, out_full)
    attended = seq_scatter(jnp.split(attended_part, seq_count, axis=0))
    middle = whole + rms_forward(attended, gain_two)
    ffn_in = rms_forward(middle, gain_three).astype(bf16)
    upstream = cotangent.astype(jnp.float32)

    def unit_rows(weight):
        weight = after(weight, rows_in[2])
        across = flip(weight, 2)
        beside = flip(weight, 1)
        return jnp.concatenate([weight, across, beside, flip(after(across, pairs_all), 1)], axis=0)

    gate_units, up_units, down_units = (
        unit_rows(weight) for weight in (gate_weight, up_weight, down_weight)
    )

    def joined(groups):
        return [group[0] if len(group) == 1 else jnp.concatenate(group, axis=0) for group in groups]

    def part_of(parts):
        def part_at(step):
            if step == 0:
                return parts[0]
            if abs(step) == half:
                return parts[half]
            part = parts[abs(step)]
            return part[tokens:] if step > 0 else part[:tokens]

        return part_at

    row_groups = joined(ring_gather(ffn_in, 0))
    gates, ups, hiddens, mlp_parts = [], [], [], []
    for rows in row_groups:
        gate = contract_cols(rows, gate_units)
        up = contract_cols(rows, up_units)
        hidden = (gelu_value(gate) * up).astype(bf16)
        gates.append(gate)
        ups.append(up)
        hiddens.append(hidden)
        mlp_parts.append(jnp.dot(hidden, down_units, preferred_element_type=jnp.float32))
    mlp = ring_scatter(part_of(mlp_parts), 0)
    layer_out = middle + rms_forward(mlp, gain_four)
    mlp_grad, fourth_part = rms_backward(mlp, gain_four, upstream)
    mlp_round = mlp_grad.astype(bf16)
    grad_groups = joined(ring_gather(mlp_round, 0))
    gate_deltas, up_deltas, in_parts = [], [], []
    for grads, gate, up in zip(grad_groups, gates, ups):
        hidden_grad = contract_cols(grads, down_units)
        gate_delta = (hidden_grad * up * gelu_slope(gate)).astype(bf16)
        up_delta = (hidden_grad * gelu_value(gate)).astype(bf16)
        gate_deltas.append(gate_delta)
        up_deltas.append(up_delta)
        in_parts.append(
            jnp.dot(gate_delta, gate_units, preferred_element_type=jnp.float32)
            + jnp.dot(up_delta, up_units, preferred_element_type=jnp.float32)
        )
    ffn_in_grad = ring_scatter(part_of(in_parts), 0)

    middle_part, third_part = rms_backward(middle, gain_three, ffn_in_grad)
    middle_grad = upstream + middle_part
    attended_grad, second_part = rms_backward(attended, gain_two, middle_grad)
    attended_round = attended_grad.astype(bf16)
    attended_blocks = seq_gather(attended_round)
    attended_rows = jnp.concatenate(attended_blocks, axis=0)

    all_rows = jnp.concatenate(row_groups, axis=0)
    all_grads = jnp.concatenate(grad_groups, axis=0)

    def unit_grad(left, right, gate):
        full = contract_rows(jnp.concatenate(left, axis=0), right).astype(bf16)
        if gate is not None:
            full = after(full, gate)
        cut = full.shape[0] // 2
        near = full[:cut].astype(jnp.float32) + flip(full[cut:], 1).astype(jnp.float32)
        across = flip(near[cut // 2 :].astype(bf16), 2)
        return near[: cut // 2] + across.astype(jnp.float32)

    down_grad = unit_grad(hiddens, all_grads, None)
    gate_grad = unit_grad(gate_deltas, all_rows, attended_blocks[2])
    up_grad = unit_grad(up_deltas, all_rows, attended_blocks[2])

    mixed_grad_head = jnp.dot(
        attended_rows, out_full, preferred_element_type=jnp.float32
    ).astype(bf16)

    def weight_grad(left, right):
        full = contract_rows(left, right).reshape(seq_count, count, own_rows, -1)
        chunk = ring_scatter(
            lambda step: lax.dynamic_slice_in_dim(full, rank_at(step), 1, 1)[:, 0], 2
        )
        chunk = chunk.astype(bf16)
        return [
            flip(lax.dynamic_slice_in_dim(chunk, seq_rank ^ j, 1, 0)[0], j)
            if j
            else lax.dynamic_slice_in_dim(chunk, seq_rank, 1, 0)[0]
            for j in range(seq_count)
        ]

    def spread(pieces):
        cols = pieces[0].shape[1]
        out = jnp.zeros((own_rows, cols * seq_count), jnp.float32)
        for j, piece in enumerate(pieces):
            out = lax.dynamic_update_slice(
                out, piece.astype(jnp.float32), (0, (seq_rank ^ j) * cols)
            )
        return out

    delta = jnp.sum(
        (mixed_grad_head.astype(jnp.float32) * mixed_head.astype(jnp.float32)).reshape(
            head_rows, -1, HEAD_DIM
        ),
        axis=-1,
    ).T
    queries_grad = None
    total = None
    for k in range(reach, -1, -1):
        query_part, pair_part = attend_back(
            live,
            query_head,
            mixed_grad_head,
            pairs_all,
            key_pos,
            head_pos,
            head_start,
            log_totals,
            delta,
            head_rows,
            2 * k,
            2,
        )
        queries_grad = query_part if queries_grad is None else queries_grad + query_part
        here = pair_part[:head_rows].astype(jnp.float32) + lax.ppermute(
            pair_part[head_rows:], "fsdp", sideways(k, True)
        ).astype(jnp.float32)
        if total is not None:
            here = here + lax.ppermute(total.astype(bf16), "fsdp", down_line).astype(jnp.float32)
        total = here
    query_back = rope_apply(queries_grad, head_cos, head_sin, True).astype(bf16)
    key_back = rope_apply(total[:, :key_cols], head_cos, head_sin, True).astype(bf16)
    value_back = total[:, key_cols:].astype(bf16)
    output_grad = spread(weight_grad(attended_rows, mixed_head))
    query_grad = spread(weight_grad(normed, query_back))
    pair_back = jnp.concatenate([key_back, value_back], axis=1)
    pair_pieces = weight_grad(normed, pair_back)
    key_grad = spread([piece[:, :key_cols] for piece in pair_pieces])
    value_grad = spread([piece[:, key_cols:] for piece in pair_pieces])
    normed_part = contract_cols(jnp.concatenate([query_back, pair_back], axis=1), in_full)
    normed_grad = seq_scatter(jnp.split(normed_part, seq_count, axis=0))
    head_scaling = lax.rsqrt(jnp.mean(head_in * head_in, axis=-1, keepdims=True) + epsilon)
    first_part = jnp.sum(normed_part * head_in * head_scaling, axis=0)
    input_part, unused = rms_backward(whole, gain_one, normed_grad)
    input_grad = middle_grad + input_part

    gain_parts = jnp.stack([first_part, second_part, third_part, fourth_part])
    gain_parts = gain_parts.reshape(4, seq_count, count, own_rows)
    gain_sums = None
    for step in range(count):
        piece = lax.dynamic_slice_in_dim(gain_parts, lax.rem(fsdp_rank + step, count), 1, 2)
        piece = turn(piece, step) if step else piece
        gain_sums = piece if gain_sums is None else gain_sums + piece
    gain_sums = gain_sums[:, :, 0]
    gain_grads = None
    for j in range(seq_count):
        piece = lax.dynamic_slice_in_dim(gain_sums, seq_rank ^ j, 1, 1)[:, 0]
        piece = flip(piece, j) if j else piece
        gain_grads = piece if gain_grads is None else gain_grads + piece
    return (
        layer_out,
        input_grad,
        gain_grads[0],
        gain_grads[1],
        gain_grads[2],
        gain_grads[3],
        query_grad,
        key_grad,
        value_grad,
        output_grad,
        gate_grad,
        up_grad,
        down_grad,
    )


def solution(mesh):
    placed = (
        P(("fsdp", "seq"), None),
        P(("fsdp", "seq"), None),
        P(),
        P(("seq", "fsdp")),
        P(("seq", "fsdp")),
        P(("seq", "fsdp")),
        P(("seq", "fsdp")),
        P(("seq", "fsdp"), None),
        P(("seq", "fsdp"), None),
        P(("seq", "fsdp"), None),
        P(("seq", "fsdp"), None),
        P(("seq", "fsdp"), None),
        P(("seq", "fsdp"), None),
        P(("seq", "fsdp"), None),
    )
    return jax.shard_map(
        on_device,
        mesh=mesh,
        in_specs=placed,
        out_specs=(
            P(("fsdp", "seq"), None),
            P(("fsdp", "seq"), None),
            P(("seq", "fsdp")),
            P(("seq", "fsdp")),
            P(("seq", "fsdp")),
            P(("seq", "fsdp")),
            P(("seq", "fsdp"), None),
            P(("seq", "fsdp"), None),
            P(("seq", "fsdp"), None),
            P(("seq", "fsdp"), None),
            P(("seq", "fsdp"), None),
            P(("seq", "fsdp"), None),
            P(("seq", "fsdp"), None),
        ),
        check_vma=False,
    )
```

```python
import functools

import jax
import jax.numpy as jnp
from jax import lax
from jax.experimental import pallas as pl
from jax.experimental.pallas import tpu as pltpu
from jax.sharding import PartitionSpec as P


HEAD_DIM = 256


epsilon = 1e-06
softcap = 50.0
rope_base = 10000.0
gelu_coef = 0.7978845608028654
cubic_coef = 0.044715


def rms_forward(values, gain):
    scaling = lax.rsqrt(jnp.mean(values * values, axis=-1, keepdims=True) + epsilon)
    return values * scaling * (1.0 + gain.astype(jnp.float32))


def rms_backward(values, gain, upstream):
    scaling = lax.rsqrt(jnp.mean(values * values, axis=-1, keepdims=True) + epsilon)
    weighted = upstream * (1.0 + gain.astype(jnp.float32))
    inner = jnp.mean(weighted * values, axis=-1, keepdims=True)
    grad_values = scaling * weighted - values * (scaling * scaling * scaling) * inner
    grad_gain = jnp.sum(upstream * values * scaling, axis=0)
    return (grad_values, grad_gain)


def rotation(positions):
    half = HEAD_DIM // 2
    frequency = jnp.power(rope_base, -jnp.arange(half, dtype=jnp.float32) / half)
    angles = positions.astype(jnp.float32)[:, None] * frequency[None, :]
    return (jnp.cos(angles), jnp.sin(angles))


def rope_apply(values, cosine, sine, inverse):
    rows = values.shape[0]
    half = HEAD_DIM // 2
    shaped = values.reshape(rows, -1, HEAD_DIM)
    first = shaped[:, :, :half]
    second = shaped[:, :, half:]
    cosine_row = cosine[:, None, :]
    sine_row = sine[:, None, :]
    if inverse:
        sine_row = -sine_row
    turned = jnp.concatenate(
        [first * cosine_row - second * sine_row, second * cosine_row + first * sine_row], axis=-1
    )
    return turned.reshape(rows, -1)


def gelu_value(gate):
    bent = jnp.tanh(gelu_coef * (gate + cubic_coef * gate * gate * gate))
    return 0.5 * gate * (1.0 + bent)


def gelu_slope(gate):
    bent = jnp.tanh(gelu_coef * (gate + cubic_coef * gate * gate * gate))
    return 0.5 * (1.0 + bent) + 0.5 * gate * (1.0 - bent * bent) * gelu_coef * (
        1.0 + 3.0 * cubic_coef * gate * gate
    )


def contract_rows(left, right):
    return lax.dot_general(
        left, right, (((0,), (0,)), ((), ())), preferred_element_type=jnp.float32
    )


def contract_cols(left, right):
    return lax.dot_general(
        left, right, (((1,), (1,)), ((), ())), preferred_element_type=jnp.float32
    )


def attend_kernel(heads, live_ref, query_ref, pair_ref, at_ref, pos_ref, start_ref, mixed_ref, log_ref, sums, totals):
    step = pl.program_id(0)
    scale = HEAD_DIM ** (-0.5)

    @pl.when(step == 0)
    def _():
        sums[...] = jnp.zeros_like(sums)
        totals[...] = jnp.zeros_like(totals)

    @pl.when(live_ref[step] > 0)
    def _():
        keys = pair_ref[:, :HEAD_DIM]
        turned = pair_ref[:, HEAD_DIM:].T
        allowed = (at_ref[...] >= start_ref[...]) & (at_ref[...] <= pos_ref[...])
        for head in range(heads):
            cols = slice(head * HEAD_DIM, (head + 1) * HEAD_DIM)
            bent = jnp.tanh(contract_cols(keys, query_ref[:, cols]) * (scale / softcap))
            expo = jnp.where(allowed, jnp.exp(softcap * bent), 0.0)
            totals[head : head + 1, :] += jnp.sum(expo, axis=0, keepdims=True)
            sums[head] += jnp.dot(turned, expo.astype(jnp.bfloat16), preferred_element_type=jnp.float32)

    @pl.when(step == pl.num_programs(0) - 1)
    def _():
        log_ref[...] = jnp.log(totals[...])
        for head in range(heads):
            cols = slice(head * HEAD_DIM, (head + 1) * HEAD_DIM)
            mixed = sums[head] / totals[head : head + 1, :]
            mixed_ref[:, cols] = mixed.T.astype(jnp.bfloat16)


def attend(live, query, pairs, key_at, query_pos, query_start, block):
    rows, width = query.shape
    heads = width // HEAD_DIM
    steps = pairs.shape[0] // block
    row = pl.BlockSpec((1, rows), lambda i, live: (0, 0))
    return pl.pallas_call(
        functools.partial(attend_kernel, heads),
        grid_spec=pltpu.PrefetchScalarGridSpec(
            num_scalar_prefetch=1,
            grid=(steps,),
            in_specs=[
                pl.BlockSpec((rows, width), lambda i, live: (0, 0)),
                pl.BlockSpec((block, pairs.shape[1]), lambda i, live: (i, 0)),
                pl.BlockSpec((block, 1), lambda i, live: (i, 0)),
                row,
                row,
            ],
            out_specs=[
                pl.BlockSpec((rows, width), lambda i, live: (0, 0)),
                pl.BlockSpec((heads, rows), lambda i, live: (0, 0)),
            ],
            scratch_shapes=[
                pltpu.VMEM((heads, HEAD_DIM, rows), jnp.float32),
                pltpu.VMEM((heads, rows), jnp.float32),
            ],
        ),
        out_shape=[
            jax.ShapeDtypeStruct((rows, width), jnp.bfloat16),
            jax.ShapeDtypeStruct((heads, rows), jnp.float32),
        ],
        cost_estimate=pl.CostEstimate(
            flops=4 * rows * width * pairs.shape[0],
            bytes_accessed=2 * pairs.size + 4 * query.size,
            transcendentals=2 * rows * heads * pairs.shape[0],
        ),
        name="attend",
    )(live, query, pairs, key_at[:, None], query_pos[None, :], query_start[None, :])


def attend_back_kernel(
    heads, first, last, live_ref, query_ref, grad_ref, pair_ref, at_ref, pos_ref, start_ref, log_ref,
    delta_ref, carry_ref, query_grad_ref, pair_grad_ref, sums,
):
    step = pl.program_id(0)
    scale = HEAD_DIM ** (-0.5)

    @pl.when(step == 0)
    def _():
        sums[...] = carry_ref[...]

    @pl.when(live_ref[step + first] == 0)
    def _():
        pair_grad_ref[...] = jnp.zeros_like(pair_grad_ref)

    @pl.when(live_ref[step + first] > 0)
    def _():
        keys = pair_ref[:, :HEAD_DIM]
        values = pair_ref[:, HEAD_DIM:]
        allowed = (at_ref[...] >= start_ref[...]) & (at_ref[...] <= pos_ref[...])
        key_grad = None
        value_grad = None
        for head in range(heads):
            cols = slice(head * HEAD_DIM, (head + 1) * HEAD_DIM)
            query = query_ref[:, cols]
            grad = grad_ref[:, cols]
            bent = jnp.tanh(contract_cols(keys, query) * (scale / softcap))
            probs = jnp.where(allowed, jnp.exp(softcap * bent - log_ref[head : head + 1, :]), 0.0)
            value_part = jnp.dot(probs.astype(jnp.bfloat16), grad, preferred_element_type=jnp.float32)
            slope = contract_cols(values, grad) - delta_ref[head : head + 1, :]
            score = (probs * slope * (1.0 - bent * bent)).astype(jnp.bfloat16)
            key_part = jnp.dot(score, query, preferred_element_type=jnp.float32)
            sums[:, cols] += contract_rows(score, keys)
            key_grad = key_part if key_grad is None else key_grad + key_part
            value_grad = value_part if value_grad is None else value_grad + value_part
        pair_grad_ref[:, :HEAD_DIM] = (key_grad * scale).astype(jnp.bfloat16)
        pair_grad_ref[:, HEAD_DIM:] = value_grad.astype(jnp.bfloat16)

    @pl.when(step == pl.num_programs(0) - 1)
    def _():
        query_grad_ref[...] = sums[...] * scale if last else sums[...]


def attend_back(
    live, query, grad, pairs, key_at, query_pos, query_start, log_totals, delta, carry, block, first, steps
):
    rows, width = query.shape
    heads = width // HEAD_DIM
    row = pl.BlockSpec((1, rows), lambda i, live: (0, 0))
    head_row = pl.BlockSpec((heads, rows), lambda i, live: (0, 0))
    full = pl.BlockSpec((rows, width), lambda i, live: (0, 0))
    pair_spec = pl.BlockSpec((block, pairs.shape[1]), lambda i, live: (i + first, 0))
    out_spec = pl.BlockSpec((block, pairs.shape[1]), lambda i, live: (i, 0))
    return pl.pallas_call(
        functools.partial(attend_back_kernel, heads, first, first == 0),
        grid_spec=pltpu.PrefetchScalarGridSpec(
            num_scalar_prefetch=1,
            grid=(steps,),
            in_specs=[
                full,
                full,
                pair_spec,
                pl.BlockSpec((block, 1), lambda i, live: (i + first, 0)),
                row,
                row,
                head_row,
                head_row,
                full,
            ],
            out_specs=[full, out_spec],
            scratch_shapes=[pltpu.VMEM((rows, width), jnp.float32)],
        ),
        out_shape=[
            jax.ShapeDtypeStruct((rows, width), jnp.float32),
            jax.ShapeDtypeStruct((steps * block, pairs.shape[1]), jnp.bfloat16),
        ],
        cost_estimate=pl.CostEstimate(
            flops=10 * rows * width * steps * block,
            bytes_accessed=4 * steps * block * width + 8 * query.size,
            transcendentals=2 * rows * heads * steps * block,
        ),
        name="attend_back",
    )(live, query, grad, pairs, key_at[:, None], query_pos[None, :], query_start[None, :], log_totals, delta, carry)


def after(value, *others):
    return lax.optimization_barrier((value,) + others)[0]


def layer(
    inputs,
    cotangent,
    segments,
    first_gain,
    second_gain,
    third_gain,
    fourth_gain,
    query_weight,
    key_weight,
    value_weight,
    output_weight,
    gate_weight,
    up_weight,
    down_weight,
):
    tokens = inputs.shape[0]
    width = inputs.shape[1]
    own_rows = query_weight.shape[0]
    seq_count = lax.axis_size("seq")
    count = lax.axis_size("fsdp")
    seq_rank = lax.axis_index("seq")
    fsdp_rank = lax.axis_index("fsdp")
    half = count // 2
    bf16 = jnp.bfloat16
    head_rows = tokens * seq_count
    query_cols = query_weight.shape[1] // seq_count
    key_cols = key_weight.shape[1] // seq_count

    cycle = [2 * i for i in range(half)] + [2 * i + 1 for i in reversed(range(half))]
    ahead = [(cycle[i], cycle[(i + 1) % count]) for i in range(count)]
    behind = [(b, a) for a, b in ahead]
    place = jnp.where(fsdp_rank % 2 == 0, fsdp_rank // 2, count - 1 - fsdp_rank // 2)

    def rank_at(step):
        spot = lax.rem(place + step + count, count)
        return jnp.where(spot < half, 2 * spot, 2 * (count - 1 - spot) + 1)

    def flip(value, bits):
        return lax.ppermute(value, "seq", [(i, i ^ bits) for i in range(seq_count)])

    def hop(value, pairs):
        return lax.ppermute(value, "fsdp", pairs)

    def ring_gather(value, axis):
        groups = [[value]]
        from_behind = value
        from_ahead = value
        for _ in range(1, half):
            from_behind = hop(from_behind, ahead)
            from_ahead = hop(from_ahead, behind)
            groups.append([from_behind, from_ahead])
        cut = value.shape[axis] // 2
        low = lax.slice_in_dim(from_behind, 0, cut, axis=axis)
        high = lax.slice_in_dim(from_ahead, cut, value.shape[axis], axis=axis)
        low = hop(low, ahead)
        high = hop(high, behind)
        groups.append([jnp.concatenate([low, high], axis=axis)])
        return groups

    def ring_scatter(part_at, axis):
        far = part_at(half)
        cut = far.shape[axis] // 2
        low = lax.slice_in_dim(far, 0, cut, axis=axis).astype(bf16)
        high = lax.slice_in_dim(far, cut, far.shape[axis], axis=axis).astype(bf16)
        low, high = lax.optimization_barrier((hop(low, ahead), hop(high, behind)))
        low = low.astype(jnp.float32)
        high = high.astype(jnp.float32)
        blank = jnp.zeros_like(low)
        onward = jnp.concatenate([low, blank], axis=axis)
        back = jnp.concatenate([blank, high], axis=axis)
        for step in range(half - 1, 0, -1):
            onward = (part_at(step) + onward).astype(bf16)
            back = (part_at(-step) + back).astype(bf16)
            onward, back = lax.optimization_barrier((hop(onward, ahead), hop(back, behind)))
            onward = onward.astype(jnp.float32)
            back = back.astype(jnp.float32)
        return part_at(0) + onward + back

    def seq_gather(value):
        across = flip(value, 2)
        beside = flip(value, 1)
        return [value, beside, across, flip(across, 1)]

    def seq_scatter(parts):
        near = flip(parts[1].astype(bf16), 1).astype(jnp.float32)
        far = flip(parts[3].astype(bf16), 1).astype(jnp.float32)
        across = flip((parts[2] + far).astype(bf16), 2).astype(jnp.float32)
        return parts[0] + near + across

    def turn(value, step):
        return hop(value, [(i, (i + step) % count) for i in range(count)])

    packed = jnp.stack([first_gain, second_gain, third_gain, fourth_gain])
    row = jnp.zeros((seq_count, 4, own_rows), bf16)
    for j in range(seq_count):
        piece = flip(packed, j) if j else packed
        row = lax.dynamic_update_slice(row, piece[None], (seq_rank ^ j, 0, 0))
    gains = jnp.zeros((count, seq_count, 4, own_rows), bf16)
    for step in range(count):
        piece = turn(row, step) if step else row
        gains = lax.dynamic_update_slice(
            gains, piece[None], (lax.rem(fsdp_rank - step + count, count), 0, 0, 0)
        )
    gains = jnp.transpose(gains, (2, 1, 0, 3)).reshape(4, width)
    gain_one, gain_two, gain_three, gain_four = gains[0], gains[1], gains[2], gains[3]

    def columns(weight, rank, size):
        return lax.dynamic_slice_in_dim(weight, rank * size, size, 1)

    def head_columns(rank):
        return jnp.concatenate(
            [
                columns(query_weight, rank, query_cols),
                columns(key_weight, rank, key_cols),
                columns(value_weight, rank, key_cols),
            ],
            axis=1,
        )

    def exchange(pick):
        pieces = [pick(seq_rank)] + [
            flip(pick(seq_rank ^ j), j) for j in range(1, seq_count)
        ]
        chunk = jnp.zeros((seq_count,) + pieces[0].shape, bf16)
        for j, piece in enumerate(pieces):
            chunk = lax.dynamic_update_slice(chunk, piece[None], (seq_rank ^ j, 0, 0))
        return chunk

    def assemble(groups):
        cols = groups[0][0].shape[2]
        whole_weight = jnp.zeros((seq_count, count, own_rows, cols), bf16)
        for step, group in enumerate(groups):
            for rank, piece in zip((rank_at(-step), rank_at(step)), group):
                whole_weight = lax.dynamic_update_slice(
                    whole_weight, piece[:, None], (0, rank, 0, 0)
                )
        return whole_weight.reshape(width, cols)

    head_chunk = exchange(head_columns)
    rows_in = seq_gather(after(inputs, head_chunk))
    out_chunk = exchange(lambda rank: columns(output_weight, rank, query_cols))
    head_groups = ring_gather(head_chunk, 2)
    in_full = assemble(head_groups)

    def block_pos(rank):
        return jnp.concatenate(
            [
                (rank * seq_count + (seq_rank ^ j)) * tokens + jnp.arange(tokens, dtype=jnp.int32)
                for j in range(seq_count)
            ]
        )

    head_pos = block_pos(fsdp_rank)
    head_seg = jnp.concatenate(
        [
            lax.dynamic_slice_in_dim(
                segments, (fsdp_rank * seq_count + (seq_rank ^ j)) * tokens, tokens, 0
            )
            for j in range(seq_count)
        ]
    )
    head_start = jnp.sum((segments[None, :] < head_seg[:, None]).astype(jnp.int32), axis=1)

    head_in = jnp.concatenate(rows_in, axis=0).astype(jnp.float32)
    whole = inputs.astype(jnp.float32)
    normed = lax.optimization_barrier(rms_forward(head_in, gain_one).astype(bf16))
    head_cos, head_sin = rotation(head_pos)
    projected = jnp.dot(normed, in_full, preferred_element_type=jnp.float32)
    turned = rope_apply(projected[:, : query_cols + key_cols], head_cos, head_sin, False)
    query_head = turned[:, :query_cols].astype(bf16)
    pair = jnp.concatenate(
        [turned[:, query_cols:], projected[:, query_cols + key_cols :]], axis=1
    ).astype(bf16)

    up_line = [(i, i + 2) for i in range(count - 2)]
    down_line = [(b, a) for a, b in up_line]
    reach = half // 2

    def sideways(step, reverse):
        to_odd = [(2 * i, 2 * i + 1) for i in range(half)]
        to_even = [(2 * i + 1, 2 * i) for i in range(half)]
        pairs = to_odd if step == 0 else to_even if step == reach else to_odd + to_even
        return [(b, a) for a, b in pairs] if reverse else pairs

    line = [pair]
    while len(line) <= reach:
        line.append(hop(line[-1], up_line))
    side = [hop(line[k], sideways(k, False)) for k in range(reach + 1)]
    out_chunk = after(out_chunk, head_groups[-1][0])
    out_groups = ring_gather(out_chunk, 2)
    out_full = assemble(out_groups)

    pieces = []
    places = []
    for k in range(reach + 1):
        pieces += [line[k], side[k]]
        places += [block_pos(fsdp_rank - 2 * k), block_pos((fsdp_rank ^ 1) - 2 * k)]
    pairs_all = jnp.concatenate(pieces, axis=0)
    key_pos = jnp.concatenate(places)
    low_start = jnp.min(head_start)
    ranks = []
    for k in range(reach + 1):
        ranks += [fsdp_rank - 2 * k, (fsdp_rank ^ 1) - 2 * k]
    ranks = jnp.stack(ranks)
    live = (ranks >= 0) & (ranks <= fsdp_rank) & ((ranks + 1) * head_rows > low_start)
    live = live.astype(jnp.int32)
    mixed_head, log_totals = attend(
        live, query_head, pairs_all, key_pos, head_pos, head_start, head_rows
    )
    attended_part = contract_cols(mixed_head, out_full)
    attended = seq_scatter(jnp.split(attended_part, seq_count, axis=0))
    middle = whole + rms_forward(attended, gain_two)
    ffn_in = rms_forward(middle, gain_three).astype(bf16)
    upstream = cotangent.astype(jnp.float32)

    def unit_rows(weight):
        weight = after(weight, rows_in[2])
        across = flip(weight, 2)
        beside = flip(weight, 1)
        both = flip(after(across, line[reach]), 1)
        return jnp.concatenate([weight, across, beside, both], axis=0)

    gate_units, up_units, down_units = (
        unit_rows(weight) for weight in (gate_weight, up_weight, down_weight)
    )

    def joined(groups):
        return [group[0] if len(group) == 1 else jnp.concatenate(group, axis=0) for group in groups]

    def part_of(parts):
        def part_at(step):
            if step == 0:
                return parts[0]
            if abs(step) == half:
                return parts[half]
            part = parts[abs(step)]
            return part[tokens:] if step > 0 else part[:tokens]

        return part_at

    row_groups = joined(ring_gather(ffn_in, 0))
    gates, ups, hiddens, mlp_parts = [], [], [], []
    for rows in row_groups:
        gate = contract_cols(rows, gate_units)
        up = contract_cols(rows, up_units)
        hidden = (gelu_value(gate) * up).astype(bf16)
        gates.append(gate)
        ups.append(up)
        hiddens.append(hidden)
        mlp_parts.append(jnp.dot(hidden, down_units, preferred_element_type=jnp.float32))
    mlp = ring_scatter(part_of(mlp_parts), 0)
    layer_out = middle + rms_forward(mlp, gain_four)
    mlp_grad, fourth_part = rms_backward(mlp, gain_four, upstream)
    mlp_round = mlp_grad.astype(bf16)
    grad_groups = joined(ring_gather(mlp_round, 0))
    gate_deltas, up_deltas, in_parts = [], [], []
    for grads, gate, up in zip(grad_groups, gates, ups):
        hidden_grad = contract_cols(grads, down_units)
        gate_delta = (hidden_grad * up * gelu_slope(gate)).astype(bf16)
        up_delta = (hidden_grad * gelu_value(gate)).astype(bf16)
        gate_deltas.append(gate_delta)
        up_deltas.append(up_delta)
        in_parts.append(
            jnp.dot(gate_delta, gate_units, preferred_element_type=jnp.float32)
            + jnp.dot(up_delta, up_units, preferred_element_type=jnp.float32)
        )
    ffn_in_grad = ring_scatter(part_of(in_parts), 0)

    middle_part, third_part = rms_backward(middle, gain_three, ffn_in_grad)
    middle_grad = upstream + middle_part
    attended_grad, second_part = rms_backward(attended, gain_two, middle_grad)
    attended_round = attended_grad.astype(bf16)
    attended_blocks = seq_gather(attended_round)
    attended_rows = jnp.concatenate(attended_blocks, axis=0)

    all_rows = jnp.concatenate(row_groups, axis=0)
    all_grads = jnp.concatenate(grad_groups, axis=0)

    def unit_grad(left, right):
        full = contract_rows(jnp.concatenate(left, axis=0), right).astype(bf16)
        cut = full.shape[0] // 2
        near = full[:cut].astype(jnp.float32) + flip(full[cut:], 1).astype(jnp.float32)
        across = flip(near[cut // 2 :].astype(bf16), 2)
        return near[: cut // 2] + across.astype(jnp.float32)

    down_grad = unit_grad(hiddens, all_grads)
    gate_grad = unit_grad(gate_deltas, all_rows)
    up_grad = unit_grad(up_deltas, all_rows)

    mixed_grad_head = jnp.dot(
        attended_rows, out_full, preferred_element_type=jnp.float32
    ).astype(bf16)

    def weight_grad(left, right):
        full = contract_rows(left, right).reshape(seq_count, count, own_rows, -1)
        chunk = ring_scatter(
            lambda step: lax.dynamic_slice_in_dim(full, rank_at(step), 1, 1)[:, 0], 2
        )
        chunk = chunk.astype(bf16)
        return [
            flip(lax.dynamic_slice_in_dim(chunk, seq_rank ^ j, 1, 0)[0], j)
            if j
            else lax.dynamic_slice_in_dim(chunk, seq_rank, 1, 0)[0]
            for j in range(seq_count)
        ]

    def spread(pieces):
        cols = pieces[0].shape[1]
        out = jnp.zeros((own_rows, cols * seq_count), jnp.float32)
        for j, piece in enumerate(pieces):
            out = lax.dynamic_update_slice(
                out, piece.astype(jnp.float32), (0, (seq_rank ^ j) * cols)
            )
        return out

    delta = jnp.sum(
        (mixed_grad_head.astype(jnp.float32) * mixed_head.astype(jnp.float32)).reshape(
            head_rows, -1, HEAD_DIM
        ),
        axis=-1,
    ).T
    queries_grad = jnp.zeros(query_head.shape, jnp.float32)
    total = None
    for k in range(reach, -1, -1):
        queries_grad, pair_part = attend_back(
            live,
            query_head,
            mixed_grad_head,
            pairs_all,
            key_pos,
            head_pos,
            head_start,
            log_totals,
            delta,
            queries_grad,
            head_rows,
            2 * k,
            2,
        )
        here = pair_part[:head_rows].astype(jnp.float32) + hop(
            pair_part[head_rows:], sideways(k, True)
        ).astype(jnp.float32)
        if total is not None:
            here = here + hop(total.astype(bf16), down_line).astype(jnp.float32)
        total = here
    query_back = rope_apply(queries_grad, head_cos, head_sin, True).astype(bf16)
    key_back = rope_apply(total[:, :key_cols], head_cos, head_sin, True).astype(bf16)
    value_back = total[:, key_cols:].astype(bf16)
    output_grad = spread(weight_grad(attended_rows, mixed_head))
    query_grad = spread(weight_grad(normed, query_back))
    pair_back = jnp.concatenate([key_back, value_back], axis=1)
    pair_pieces = weight_grad(normed, pair_back)
    key_grad = spread([piece[:, :key_cols] for piece in pair_pieces])
    value_grad = spread([piece[:, key_cols:] for piece in pair_pieces])
    normed_part = contract_cols(jnp.concatenate([query_back, pair_back], axis=1), in_full)
    normed_grad = seq_scatter(jnp.split(normed_part, seq_count, axis=0))
    head_scaling = lax.rsqrt(jnp.mean(head_in * head_in, axis=-1, keepdims=True) + epsilon)
    first_part = jnp.sum(normed_part * head_in * head_scaling, axis=0)
    input_part, _ = rms_backward(whole, gain_one, normed_grad)
    input_grad = middle_grad + input_part

    gain_parts = jnp.stack([first_part, second_part, third_part, fourth_part])
    gain_parts = gain_parts.reshape(4, seq_count, count, own_rows)
    gain_sums = None
    for step in range(count):
        piece = lax.dynamic_slice_in_dim(gain_parts, lax.rem(fsdp_rank + step, count), 1, 2)
        piece = turn(piece, step) if step else piece
        gain_sums = piece if gain_sums is None else gain_sums + piece
    gain_sums = gain_sums[:, :, 0]
    gain_grads = None
    for j in range(seq_count):
        piece = lax.dynamic_slice_in_dim(gain_sums, seq_rank ^ j, 1, 1)[:, 0]
        piece = flip(piece, j) if j else piece
        gain_grads = piece if gain_grads is None else gain_grads + piece
    return (
        layer_out,
        input_grad,
        gain_grads[0],
        gain_grads[1],
        gain_grads[2],
        gain_grads[3],
        query_grad,
        key_grad,
        value_grad,
        output_grad,
        gate_grad,
        up_grad,
        down_grad,
    )


def solution(mesh):
    placed = (
        P(("fsdp", "seq"), None),
        P(("fsdp", "seq"), None),
        P(),
        P(("seq", "fsdp")),
        P(("seq", "fsdp")),
        P(("seq", "fsdp")),
        P(("seq", "fsdp")),
        P(("seq", "fsdp"), None),
        P(("seq", "fsdp"), None),
        P(("seq", "fsdp"), None),
        P(("seq", "fsdp"), None),
        P(("seq", "fsdp"), None),
        P(("seq", "fsdp"), None),
        P(("seq", "fsdp"), None),
    )
    return jax.shard_map(
        layer,
        mesh=mesh,
        in_specs=placed,
        out_specs=(
            P(("fsdp", "seq"), None),
            P(("fsdp", "seq"), None),
            P(("seq", "fsdp")),
            P(("seq", "fsdp")),
            P(("seq", "fsdp")),
            P(("seq", "fsdp")),
            P(("seq", "fsdp"), None),
            P(("seq", "fsdp"), None),
            P(("seq", "fsdp"), None),
            P(("seq", "fsdp"), None),
            P(("seq", "fsdp"), None),
            P(("seq", "fsdp"), None),
            P(("seq", "fsdp"), None),
        ),
        check_vma=False,
    )
```

```python
import functools

import jax
import jax.numpy as jnp
from jax import lax
from jax.experimental import pallas as pl
from jax.experimental.pallas import tpu as pltpu
from jax.sharding import PartitionSpec as P


HEAD_DIM = 256


epsilon = 1e-06
softcap = 50.0
rope_base = 10000.0
gelu_coef = 0.7978845608028654
cubic_coef = 0.044715


def rms_forward(values, gain):
    scaling = lax.rsqrt(jnp.mean(values * values, axis=-1, keepdims=True) + epsilon)
    return values * scaling * (1.0 + gain.astype(jnp.float32))


def rms_backward(values, gain, upstream):
    scaling = lax.rsqrt(jnp.mean(values * values, axis=-1, keepdims=True) + epsilon)
    weighted = upstream * (1.0 + gain.astype(jnp.float32))
    inner = jnp.mean(weighted * values, axis=-1, keepdims=True)
    grad_values = scaling * weighted - values * (scaling * scaling * scaling) * inner
    grad_gain = jnp.sum(upstream * values * scaling, axis=0)
    return (grad_values, grad_gain)


def rotation(positions):
    half = HEAD_DIM // 2
    frequency = jnp.power(rope_base, -jnp.arange(half, dtype=jnp.float32) / half)
    angles = positions.astype(jnp.float32)[:, None] * frequency[None, :]
    return (jnp.cos(angles), jnp.sin(angles))


def rope_apply(values, cosine, sine, inverse):
    rows = values.shape[0]
    half = HEAD_DIM // 2
    shaped = values.reshape(rows, -1, HEAD_DIM)
    first = shaped[:, :, :half]
    second = shaped[:, :, half:]
    cosine_row = cosine[:, None, :]
    sine_row = sine[:, None, :]
    if inverse:
        sine_row = -sine_row
    turned = jnp.concatenate(
        [first * cosine_row - second * sine_row, second * cosine_row + first * sine_row], axis=-1
    )
    return turned.reshape(rows, -1)


def gelu_value(gate):
    bent = jnp.tanh(gelu_coef * (gate + cubic_coef * gate * gate * gate))
    return 0.5 * gate * (1.0 + bent)


def gelu_slope(gate):
    bent = jnp.tanh(gelu_coef * (gate + cubic_coef * gate * gate * gate))
    return 0.5 * (1.0 + bent) + 0.5 * gate * (1.0 - bent * bent) * gelu_coef * (
        1.0 + 3.0 * cubic_coef * gate * gate
    )


def contract_rows(left, right):
    return lax.dot_general(
        left, right, (((0,), (0,)), ((), ())), preferred_element_type=jnp.float32
    )


def contract_cols(left, right):
    return lax.dot_general(
        left, right, (((1,), (1,)), ((), ())), preferred_element_type=jnp.float32
    )


def attend_kernel(heads, live_ref, query_ref, pair_ref, at_ref, pos_ref, start_ref, mixed_ref, log_ref, sums, totals):
    step = pl.program_id(0)
    scale = HEAD_DIM ** (-0.5)

    @pl.when(step == 0)
    def _():
        sums[...] = jnp.zeros_like(sums)
        totals[...] = jnp.zeros_like(totals)

    @pl.when(live_ref[step] > 0)
    def _():
        keys = pair_ref[:, :HEAD_DIM]
        turned = pair_ref[:, HEAD_DIM:].T
        allowed = (at_ref[...] >= start_ref[...]) & (at_ref[...] <= pos_ref[...])
        for head in range(heads):
            cols = slice(head * HEAD_DIM, (head + 1) * HEAD_DIM)
            bent = jnp.tanh(contract_cols(keys, query_ref[:, cols]) * (scale / softcap))
            expo = jnp.where(allowed, jnp.exp(softcap * bent), 0.0)
            totals[head : head + 1, :] += jnp.sum(expo, axis=0, keepdims=True)
            sums[head] += jnp.dot(turned, expo.astype(jnp.bfloat16), preferred_element_type=jnp.float32)

    @pl.when(step == pl.num_programs(0) - 1)
    def _():
        log_ref[...] = jnp.log(totals[...])
        for head in range(heads):
            cols = slice(head * HEAD_DIM, (head + 1) * HEAD_DIM)
            mixed = sums[head] / totals[head : head + 1, :]
            mixed_ref[:, cols] = mixed.T.astype(jnp.bfloat16)


def attend(live, query, pairs, key_at, query_pos, query_start, block):
    rows, width = query.shape
    heads = width // HEAD_DIM
    steps = pairs.shape[0] // block
    row = pl.BlockSpec((1, rows), lambda i, live: (0, 0))
    return pl.pallas_call(
        functools.partial(attend_kernel, heads),
        grid_spec=pltpu.PrefetchScalarGridSpec(
            num_scalar_prefetch=1,
            grid=(steps,),
            in_specs=[
                pl.BlockSpec((rows, width), lambda i, live: (0, 0)),
                pl.BlockSpec((block, pairs.shape[1]), lambda i, live: (i, 0)),
                pl.BlockSpec((block, 1), lambda i, live: (i, 0)),
                row,
                row,
            ],
            out_specs=[
                pl.BlockSpec((rows, width), lambda i, live: (0, 0)),
                pl.BlockSpec((heads, rows), lambda i, live: (0, 0)),
            ],
            scratch_shapes=[
                pltpu.VMEM((heads, HEAD_DIM, rows), jnp.float32),
                pltpu.VMEM((heads, rows), jnp.float32),
            ],
        ),
        out_shape=[
            jax.ShapeDtypeStruct((rows, width), jnp.bfloat16),
            jax.ShapeDtypeStruct((heads, rows), jnp.float32),
        ],
        cost_estimate=pl.CostEstimate(
            flops=4 * rows * width * pairs.shape[0],
            bytes_accessed=2 * pairs.size + 4 * query.size,
            transcendentals=2 * rows * heads * pairs.shape[0],
        ),
        name="attend",
    )(live, query, pairs, key_at[:, None], query_pos[None, :], query_start[None, :])


def attend_back_kernel(heads, first, begins, ends, *refs):
    live_ref, query_ref, grad_ref, mixed_ref, pair_ref, at_ref, pos_ref, start_ref, log_ref = refs[:9]
    refs = refs[9:]
    if not begins:
        carry_ref, refs = refs[0], refs[1:]
    if ends:
        cos_ref, sin_ref, refs = refs[0], refs[1], refs[2:]
    query_grad_ref, line_ref, side_ref, sums, delta = refs
    step = pl.program_id(0)
    scale = HEAD_DIM ** (-0.5)

    @pl.when(step == 0)
    def _():
        sums[...] = jnp.zeros_like(sums) if begins else carry_ref[...]
        ones = jnp.ones((8, HEAD_DIM), jnp.bfloat16)
        for head in range(heads):
            cols = slice(head * HEAD_DIM, (head + 1) * HEAD_DIM)
            grad = grad_ref[:, cols].astype(jnp.float32)
            product = grad * mixed_ref[:, cols].astype(jnp.float32)
            high = product.astype(jnp.bfloat16)
            low = (product - high.astype(jnp.float32)).astype(jnp.bfloat16)
            delta[head * 8 : head * 8 + 8, :] = contract_cols(ones, high) + contract_cols(ones, low)

    def work(out_ref):
        keys = pair_ref[:, :HEAD_DIM]
        values = pair_ref[:, HEAD_DIM:]
        allowed = (at_ref[...] >= start_ref[...]) & (at_ref[...] <= pos_ref[...])
        key_grad = None
        value_grad = None
        for head in range(heads):
            cols = slice(head * HEAD_DIM, (head + 1) * HEAD_DIM)
            query = query_ref[:, cols]
            grad = grad_ref[:, cols]
            bent = jnp.tanh(contract_cols(keys, query) * (scale / softcap))
            probs = jnp.where(
                allowed, jnp.exp(softcap * bent - log_ref[head : head + 1, :]), 0.0
            )
            value_part = jnp.dot(
                probs.astype(jnp.bfloat16), grad, preferred_element_type=jnp.float32
            )
            slope = contract_cols(values, grad) - delta[head * 8 : head * 8 + 1, :]
            score = (probs * slope * (1.0 - bent * bent)).astype(jnp.bfloat16)
            key_part = jnp.dot(score, query, preferred_element_type=jnp.float32)
            sums[:, cols] += contract_rows(score, keys)
            key_grad = key_part if key_grad is None else key_grad + key_part
            value_grad = value_part if value_grad is None else value_grad + value_part
        out_ref[:, :HEAD_DIM] = (key_grad * scale).astype(jnp.bfloat16)
        out_ref[:, HEAD_DIM:] = value_grad.astype(jnp.bfloat16)

    @pl.when(step == 0)
    def _():
        line_ref[...] = jnp.zeros_like(line_ref)
        side_ref[...] = jnp.zeros_like(side_ref)

    @pl.when((step == 0) & (live_ref[first] > 0))
    def _():
        work(line_ref)

    @pl.when((step == 1) & (live_ref[first + 1] > 0))
    def _():
        work(side_ref)

    @pl.when(step == 1)
    def _():
        if not ends:
            query_grad_ref[...] = sums[...]
            return
        half = HEAD_DIM // 2
        for head in range(heads):
            near = slice(head * HEAD_DIM, head * HEAD_DIM + half)
            far = slice(head * HEAD_DIM + half, (head + 1) * HEAD_DIM)
            one = sums[:, near] * scale
            two = sums[:, far] * scale
            query_grad_ref[:, near] = (one * cos_ref[...] + two * sin_ref[...]).astype(jnp.bfloat16)
            query_grad_ref[:, far] = (two * cos_ref[...] - one * sin_ref[...]).astype(jnp.bfloat16)


def attend_back(
    live, query, grad, mixed, pairs, key_at, query_pos, query_start, log_totals, carry, turns, first
):
    rows, width = query.shape
    heads = width // HEAD_DIM
    block = rows
    row = pl.BlockSpec((1, rows), lambda i, live: (0, 0))
    head_row = pl.BlockSpec((heads, rows), lambda i, live: (0, 0))
    full = pl.BlockSpec((rows, width), lambda i, live: (0, 0))
    part = pl.BlockSpec((block, pairs.shape[1]), lambda i, live: (0, 0))
    more_specs = []
    more = []
    if carry is not None:
        more_specs.append(full)
        more.append(carry)
    if turns is not None:
        turn_spec = pl.BlockSpec((rows, HEAD_DIM // 2), lambda i, live: (0, 0))
        more_specs += [turn_spec, turn_spec]
        more += list(turns)
    part_shape = jax.ShapeDtypeStruct((block, pairs.shape[1]), jnp.bfloat16)
    return pl.pallas_call(
        functools.partial(attend_back_kernel, heads, first, carry is None, turns is not None),
        grid_spec=pltpu.PrefetchScalarGridSpec(
            num_scalar_prefetch=1,
            grid=(2,),
            in_specs=[
                full,
                full,
                full,
                pl.BlockSpec((block, pairs.shape[1]), lambda i, live: (i + first, 0)),
                pl.BlockSpec((block, 1), lambda i, live: (i + first, 0)),
                row,
                row,
                head_row,
                *more_specs,
            ],
            out_specs=[full, part, part],
            scratch_shapes=[
                pltpu.VMEM((rows, width), jnp.float32),
                pltpu.VMEM((heads * 8, rows), jnp.float32),
            ],
        ),
        out_shape=[
            jax.ShapeDtypeStruct(
                (rows, width), jnp.float32 if turns is None else jnp.bfloat16
            ),
            part_shape,
            part_shape,
        ],
        cost_estimate=pl.CostEstimate(
            flops=20 * rows * width * block,
            bytes_accessed=8 * block * width + 8 * query.size,
            transcendentals=4 * rows * heads * block,
        ),
        name="attend_back",
    )(
        live,
        query,
        grad,
        mixed,
        pairs,
        key_at[:, None],
        query_pos[None, :],
        query_start[None, :],
        log_totals,
        *more,
    )


def project_kernel(turned, split, rows_ref, weight_ref, cos_ref, sin_ref, query_ref, pair_ref):
    step = pl.program_id(0)
    half = HEAD_DIM // 2
    product = jnp.dot(rows_ref[...], weight_ref[...], preferred_element_type=jnp.float32)

    def store(out_ref, turn):
        one = product[:, :half]
        two = product[:, half:]
        if turn:
            cosine = cos_ref[...]
            sine = sin_ref[...]
            one, two = one * cosine - two * sine, two * cosine + one * sine
        out_ref[:, :half] = one.astype(jnp.bfloat16)
        out_ref[:, half:] = two.astype(jnp.bfloat16)

    @pl.when(step < split)
    def _():
        store(query_ref, True)

    @pl.when((step >= split) & (step < turned))
    def _():
        store(pair_ref, True)

    @pl.when(step >= turned)
    def _():
        store(pair_ref, False)


def project(rows, weight, cosine, sine, query_cols, key_cols):
    count = rows.shape[0]
    split = query_cols // HEAD_DIM
    steps = weight.shape[1] // HEAD_DIM
    turn_spec = pl.BlockSpec((count, HEAD_DIM // 2), lambda i: (0, 0))
    return pl.pallas_call(
        functools.partial(project_kernel, split + key_cols // HEAD_DIM, split),
        grid=(steps,),
        in_specs=[
            pl.BlockSpec(rows.shape, lambda i: (0, 0)),
            pl.BlockSpec((weight.shape[0], HEAD_DIM), lambda i: (0, i)),
            turn_spec,
            turn_spec,
        ],
        out_specs=[
            pl.BlockSpec((count, HEAD_DIM), lambda i: (0, jnp.minimum(i, split - 1))),
            pl.BlockSpec((count, HEAD_DIM), lambda i: (0, jnp.maximum(i - split, 0))),
        ],
        out_shape=[
            jax.ShapeDtypeStruct((count, query_cols), jnp.bfloat16),
            jax.ShapeDtypeStruct((count, 2 * key_cols), jnp.bfloat16),
        ],
        cost_estimate=pl.CostEstimate(
            flops=2 * rows.size * weight.shape[1],
            bytes_accessed=2 * (rows.size + weight.size + count * weight.shape[1]),
            transcendentals=0,
        ),
        name="project",
    )(rows, weight, cosine, sine)


def after(value, *others):
    return lax.optimization_barrier((value,) + others)[0]


def layer(
    inputs,
    cotangent,
    segments,
    first_gain,
    second_gain,
    third_gain,
    fourth_gain,
    query_weight,
    key_weight,
    value_weight,
    output_weight,
    gate_weight,
    up_weight,
    down_weight,
):
    tokens = inputs.shape[0]
    width = inputs.shape[1]
    own_rows = query_weight.shape[0]
    seq_count = lax.axis_size("seq")
    count = lax.axis_size("fsdp")
    seq_rank = lax.axis_index("seq")
    fsdp_rank = lax.axis_index("fsdp")
    half = count // 2
    bf16 = jnp.bfloat16
    head_rows = tokens * seq_count
    query_cols = query_weight.shape[1] // seq_count
    key_cols = key_weight.shape[1] // seq_count

    cycle = [2 * i for i in range(half)] + [2 * i + 1 for i in reversed(range(half))]
    ahead = [(cycle[i], cycle[(i + 1) % count]) for i in range(count)]
    behind = [(b, a) for a, b in ahead]
    place = jnp.where(fsdp_rank % 2 == 0, fsdp_rank // 2, count - 1 - fsdp_rank // 2)

    def rank_at(step):
        spot = lax.rem(place + step + count, count)
        return jnp.where(spot < half, 2 * spot, 2 * (count - 1 - spot) + 1)

    def flip(value, bits):
        return lax.ppermute(value, "seq", [(i, i ^ bits) for i in range(seq_count)])

    def hop(value, pairs):
        return lax.ppermute(value, "fsdp", pairs)

    def ring_gather(value, axis):
        groups = [[value]]
        from_behind = value
        from_ahead = value
        for _ in range(1, half):
            from_behind = hop(from_behind, ahead)
            from_ahead = hop(from_ahead, behind)
            groups.append([from_behind, from_ahead])
        cut = value.shape[axis] // 2
        low = lax.slice_in_dim(from_behind, 0, cut, axis=axis)
        high = lax.slice_in_dim(from_ahead, cut, value.shape[axis], axis=axis)
        low = hop(low, ahead)
        high = hop(high, behind)
        groups.append([jnp.concatenate([low, high], axis=axis)])
        return groups

    def ring_scatter(part_at, axis):
        far = part_at(half)
        cut = far.shape[axis] // 2
        low = lax.slice_in_dim(far, 0, cut, axis=axis).astype(bf16)
        high = lax.slice_in_dim(far, cut, far.shape[axis], axis=axis).astype(bf16)
        low, high = lax.optimization_barrier((hop(low, ahead), hop(high, behind)))
        low = low.astype(jnp.float32)
        high = high.astype(jnp.float32)
        blank = jnp.zeros_like(low)
        onward = jnp.concatenate([low, blank], axis=axis)
        back = jnp.concatenate([blank, high], axis=axis)
        for step in range(half - 1, 0, -1):
            onward = (part_at(step) + onward).astype(bf16)
            back = (part_at(-step) + back).astype(bf16)
            onward, back = lax.optimization_barrier((hop(onward, ahead), hop(back, behind)))
            onward = onward.astype(jnp.float32)
            back = back.astype(jnp.float32)
        return part_at(0) + onward + back

    def seq_gather(value):
        across = flip(value, 2)
        beside = flip(value, 1)
        return [value, beside, across, flip(across, 1)]

    def seq_scatter(parts):
        near = flip(parts[1].astype(bf16), 1).astype(jnp.float32)
        far = flip(parts[3].astype(bf16), 1).astype(jnp.float32)
        across = flip((parts[2] + far).astype(bf16), 2).astype(jnp.float32)
        return parts[0] + near + across

    def sum_all(value):
        bits = 1
        while bits < seq_count:
            value = value + flip(value, bits)
            bits *= 2
        bits = 1
        while bits < count:
            value = value + hop(value, [(i, i ^ bits) for i in range(count)])
            bits *= 2
        return value

    own_start = (seq_rank * count + fsdp_rank) * own_rows
    packed = jnp.stack([first_gain, second_gain, third_gain, fourth_gain])
    gains = sum_all(lax.dynamic_update_slice(jnp.zeros((4, width), bf16), packed, (0, own_start)))
    gain_one, gain_two, gain_three, gain_four = gains[0], gains[1], gains[2], gains[3]

    def columns(weight, rank, size):
        return lax.dynamic_slice_in_dim(weight, rank * size, size, 1)

    def head_columns(rank):
        return jnp.concatenate(
            [
                columns(query_weight, rank, query_cols),
                columns(key_weight, rank, key_cols),
                columns(value_weight, rank, key_cols),
            ],
            axis=1,
        )

    def exchange(pick):
        pieces = [pick(seq_rank)] + [
            flip(pick(seq_rank ^ j), j) for j in range(1, seq_count)
        ]
        chunk = jnp.zeros((seq_count,) + pieces[0].shape, bf16)
        for j, piece in enumerate(pieces):
            chunk = lax.dynamic_update_slice(chunk, piece[None], (seq_rank ^ j, 0, 0))
        return chunk

    def assemble(groups):
        cols = groups[0][0].shape[2]
        whole_weight = jnp.zeros((seq_count, count, own_rows, cols), bf16)
        for step, group in enumerate(groups):
            for rank, piece in zip((rank_at(-step), rank_at(step)), group):
                whole_weight = lax.dynamic_update_slice(
                    whole_weight, piece[:, None], (0, rank, 0, 0)
                )
        return whole_weight.reshape(width, cols)

    head_chunk = exchange(head_columns)
    rows_in = seq_gather(after(inputs, head_chunk))
    out_chunk = exchange(lambda rank: columns(output_weight, rank, query_cols))
    head_groups = ring_gather(head_chunk, 2)
    in_full = assemble(head_groups)

    def block_pos(rank):
        return jnp.concatenate(
            [
                (rank * seq_count + (seq_rank ^ j)) * tokens + jnp.arange(tokens, dtype=jnp.int32)
                for j in range(seq_count)
            ]
        )

    head_pos = block_pos(fsdp_rank)
    head_seg = jnp.concatenate(
        [
            lax.dynamic_slice_in_dim(
                segments, (fsdp_rank * seq_count + (seq_rank ^ j)) * tokens, tokens, 0
            )
            for j in range(seq_count)
        ]
    )
    head_start = jnp.sum((segments[None, :] < head_seg[:, None]).astype(jnp.int32), axis=1)

    head_in = jnp.concatenate(rows_in, axis=0).astype(jnp.float32)
    whole = inputs.astype(jnp.float32)
    normed = lax.optimization_barrier(rms_forward(head_in, gain_one).astype(bf16))
    head_cos, head_sin = rotation(head_pos)
    query_head, pair = project(normed, in_full, head_cos, head_sin, query_cols, key_cols)

    up_line = [(i, i + 2) for i in range(count - 2)]
    down_line = [(b, a) for a, b in up_line]
    reach = half // 2

    def sideways(step, reverse):
        to_odd = [(2 * i, 2 * i + 1) for i in range(half)]
        to_even = [(2 * i + 1, 2 * i) for i in range(half)]
        pairs = to_odd if step == 0 else to_even if step == reach else to_odd + to_even
        return [(b, a) for a, b in pairs] if reverse else pairs

    line = [pair]
    while len(line) <= reach:
        line.append(hop(line[-1], up_line))
    side = [hop(line[k], sideways(k, False)) for k in range(reach + 1)]
    out_chunk = after(out_chunk, head_groups[-1][0])
    out_groups = ring_gather(out_chunk, 2)
    out_full = assemble(out_groups)

    pieces = []
    places = []
    for k in range(reach + 1):
        pieces += [line[k], side[k]]
        places += [block_pos(fsdp_rank - 2 * k), block_pos((fsdp_rank ^ 1) - 2 * k)]
    pairs_all = jnp.concatenate(pieces, axis=0)
    key_pos = jnp.concatenate(places)
    low_start = jnp.min(head_start)
    ranks = []
    for k in range(reach + 1):
        ranks += [fsdp_rank - 2 * k, (fsdp_rank ^ 1) - 2 * k]
    ranks = jnp.stack(ranks)
    live = (ranks >= 0) & (ranks <= fsdp_rank) & ((ranks + 1) * head_rows > low_start)
    live = live.astype(jnp.int32)
    mixed_head, log_totals = attend(
        live, query_head, pairs_all, key_pos, head_pos, head_start, head_rows
    )
    attended_part = contract_cols(mixed_head, out_full)
    attended = seq_scatter(jnp.split(attended_part, seq_count, axis=0))
    middle = whole + rms_forward(attended, gain_two)
    ffn_in = rms_forward(middle, gain_three).astype(bf16)
    upstream = cotangent.astype(jnp.float32)

    blank = jnp.zeros((-2 * gate_weight.shape[0] % 128, width), bf16)

    def unit_rows(weight):
        weight = after(weight, rows_in[2])
        across = flip(weight, 2)
        beside = flip(weight, 1)
        both = flip(after(across, line[reach]), 1)
        return jnp.concatenate([weight, across, blank, beside, both, blank], axis=0)

    gate_units, up_units, down_units = (
        unit_rows(weight)
        for weight in (gate_weight, up_weight, down_weight)
    )

    def joined(groups):
        return [group[0] if len(group) == 1 else jnp.concatenate(group, axis=0) for group in groups]

    def part_of(parts):
        def part_at(step):
            if step == 0:
                return parts[0]
            if abs(step) == half:
                return parts[half]
            part = parts[abs(step)]
            return part[tokens:] if step > 0 else part[:tokens]

        return part_at

    row_groups = joined(ring_gather(ffn_in, 0))
    gates, ups, hiddens, mlp_parts = [], [], [], []
    for rows in row_groups:
        gate = contract_cols(rows, gate_units)
        up = contract_cols(rows, up_units)
        hidden = (gelu_value(gate) * up).astype(bf16)
        gates.append(gate)
        ups.append(up)
        hiddens.append(hidden)
        mlp_parts.append(jnp.dot(hidden, down_units, preferred_element_type=jnp.float32))
    mlp = ring_scatter(part_of(mlp_parts), 0)
    layer_out = middle + rms_forward(mlp, gain_four)
    mlp_grad, fourth_part = rms_backward(mlp, gain_four, upstream)
    mlp_round = mlp_grad.astype(bf16)
    grad_groups = joined(ring_gather(mlp_round, 0))
    gate_deltas, up_deltas, in_parts = [], [], []
    for grads, gate, up in zip(grad_groups, gates, ups):
        hidden_grad = contract_cols(grads, down_units)
        gate_delta = (hidden_grad * up * gelu_slope(gate)).astype(bf16)
        up_delta = (hidden_grad * gelu_value(gate)).astype(bf16)
        gate_deltas.append(gate_delta)
        up_deltas.append(up_delta)
        in_parts.append(
            jnp.dot(gate_delta, gate_units, preferred_element_type=jnp.float32)
            + jnp.dot(up_delta, up_units, preferred_element_type=jnp.float32)
        )
    ffn_in_grad = ring_scatter(part_of(in_parts), 0)

    middle_part, third_part = rms_backward(middle, gain_three, ffn_in_grad)
    middle_grad = upstream + middle_part
    attended_grad, second_part = rms_backward(attended, gain_two, middle_grad)
    attended_round = attended_grad.astype(bf16)
    attended_blocks = seq_gather(attended_round)
    attended_rows = jnp.concatenate(attended_blocks, axis=0)

    all_rows = jnp.concatenate(row_groups, axis=0)
    all_grads = jnp.concatenate(grad_groups, axis=0)

    def unit_grad(left, right):
        units = gate_weight.shape[0]
        left = jnp.concatenate(left, axis=0)
        cut = left.shape[1] // 2
        far = contract_rows(left[:, cut:], right).astype(bf16)
        near = contract_rows(left[:, :cut], right).astype(bf16)
        beside = flip(far, 1)

        def both(begin):
            return near[begin : begin + units].astype(jnp.float32) + beside[
                begin : begin + units
            ].astype(jnp.float32)

        across = flip(both(units).astype(bf16), 2)
        return both(0) + across.astype(jnp.float32)

    down_grad = unit_grad(hiddens, all_grads)
    gate_grad = unit_grad(gate_deltas, all_rows)
    up_grad = unit_grad(up_deltas, all_rows)

    mixed_grad_head = jnp.dot(
        attended_rows, out_full, preferred_element_type=jnp.float32
    ).astype(bf16)

    def weight_grad(left, right):
        full = contract_rows(left, right).reshape(seq_count, count, own_rows, -1)
        return ring_scatter(
            lambda step: lax.dynamic_slice_in_dim(full, rank_at(step), 1, 1)[:, 0], 2
        ).astype(bf16)

    def to_owners(chunk):
        return [
            flip(lax.dynamic_slice_in_dim(chunk, seq_rank ^ j, 1, 0)[0], j)
            if j
            else lax.dynamic_slice_in_dim(chunk, seq_rank, 1, 0)[0]
            for j in range(seq_count)
        ]

    def spread(pieces):
        cols = pieces[0].shape[1]
        out = jnp.zeros((own_rows, cols * seq_count), jnp.float32)
        for j, piece in enumerate(pieces):
            out = lax.dynamic_update_slice(
                out, piece.astype(jnp.float32), (0, (seq_rank ^ j) * cols)
            )
        return out

    carry = None
    total = None
    for k in range(reach, -1, -1):
        carry, line_part, side_part = attend_back(
            live,
            query_head,
            mixed_grad_head,
            mixed_head,
            pairs_all,
            key_pos,
            head_pos,
            head_start,
            log_totals,
            carry,
            None if k else (head_cos, head_sin),
            2 * k,
        )
        here = line_part.astype(jnp.float32) + hop(side_part, sideways(k, True)).astype(jnp.float32)
        if total is not None:
            here = here + hop(total.astype(bf16), down_line).astype(jnp.float32)
        total = here
    query_back = carry
    key_back = rope_apply(total[:, :key_cols], head_cos, head_sin, True).astype(bf16)
    value_back = total[:, key_cols:].astype(bf16)
    output_chunk = weight_grad(attended_rows, mixed_head)
    query_chunk = weight_grad(normed, query_back)
    both_pieces = to_owners(jnp.concatenate([output_chunk, query_chunk], axis=2))
    output_grad = spread([piece[:, :query_cols] for piece in both_pieces])
    query_grad = spread([piece[:, query_cols:] for piece in both_pieces])
    pair_back = jnp.concatenate([key_back, value_back], axis=1)
    pair_pieces = to_owners(weight_grad(normed, pair_back))
    key_grad = spread([piece[:, :key_cols] for piece in pair_pieces])
    value_grad = spread([piece[:, key_cols:] for piece in pair_pieces])
    normed_part = contract_cols(jnp.concatenate([query_back, pair_back], axis=1), in_full)
    normed_grad = seq_scatter(jnp.split(normed_part, seq_count, axis=0))
    head_scaling = lax.rsqrt(jnp.mean(head_in * head_in, axis=-1, keepdims=True) + epsilon)
    first_part = jnp.sum(normed_part * head_in * head_scaling, axis=0)
    input_part, _ = rms_backward(whole, gain_one, normed_grad)
    input_grad = middle_grad + input_part

    gain_parts = jnp.stack([first_part, second_part, third_part, fourth_part])
    gain_grads = lax.dynamic_slice_in_dim(sum_all(gain_parts), own_start, own_rows, 1)
    return (
        layer_out,
        input_grad,
        gain_grads[0],
        gain_grads[1],
        gain_grads[2],
        gain_grads[3],
        query_grad,
        key_grad,
        value_grad,
        output_grad,
        gate_grad,
        up_grad,
        down_grad,
    )


def solution(mesh):
    placed = (
        P(("fsdp", "seq"), None),
        P(("fsdp", "seq"), None),
        P(),
        P(("seq", "fsdp")),
        P(("seq", "fsdp")),
        P(("seq", "fsdp")),
        P(("seq", "fsdp")),
        P(("seq", "fsdp"), None),
        P(("seq", "fsdp"), None),
        P(("seq", "fsdp"), None),
        P(("seq", "fsdp"), None),
        P(("seq", "fsdp"), None),
        P(("seq", "fsdp"), None),
        P(("seq", "fsdp"), None),
    )
    return jax.shard_map(
        layer,
        mesh=mesh,
        in_specs=placed,
        out_specs=(
            P(("fsdp", "seq"), None),
            P(("fsdp", "seq"), None),
            P(("seq", "fsdp")),
            P(("seq", "fsdp")),
            P(("seq", "fsdp")),
            P(("seq", "fsdp")),
            P(("seq", "fsdp"), None),
            P(("seq", "fsdp"), None),
            P(("seq", "fsdp"), None),
            P(("seq", "fsdp"), None),
            P(("seq", "fsdp"), None),
            P(("seq", "fsdp"), None),
            P(("seq", "fsdp"), None),
        ),
        check_vma=False,
    )
```

```python
import functools

import jax
import jax.numpy as jnp
from jax import lax
from jax.experimental import pallas as pl
from jax.experimental.pallas import tpu as pltpu
from jax.sharding import PartitionSpec as P


HEAD_DIM = 256


epsilon = 1e-06
softcap = 50.0
rope_base = 10000.0
gelu_coef = 0.7978845608028654
cubic_coef = 0.044715


def rms_forward(values, gain):
    scaling = lax.rsqrt(jnp.mean(values * values, axis=-1, keepdims=True) + epsilon)
    return values * scaling * (1.0 + gain.astype(jnp.float32))


def rms_backward(values, gain, upstream):
    scaling = lax.rsqrt(jnp.mean(values * values, axis=-1, keepdims=True) + epsilon)
    weighted = upstream * (1.0 + gain.astype(jnp.float32))
    inner = jnp.mean(weighted * values, axis=-1, keepdims=True)
    grad_values = scaling * weighted - values * (scaling * scaling * scaling) * inner
    grad_gain = jnp.sum(upstream * values * scaling, axis=0)
    return (grad_values, grad_gain)


def rotation(positions):
    half = HEAD_DIM // 2
    frequency = jnp.power(rope_base, -jnp.arange(half, dtype=jnp.float32) / half)
    angles = positions.astype(jnp.float32)[:, None] * frequency[None, :]
    return (jnp.cos(angles), jnp.sin(angles))


def rope_apply(values, cosine, sine, inverse):
    rows = values.shape[0]
    half = HEAD_DIM // 2
    shaped = values.reshape(rows, -1, HEAD_DIM)
    first = shaped[:, :, :half]
    second = shaped[:, :, half:]
    cosine_row = cosine[:, None, :]
    sine_row = sine[:, None, :]
    if inverse:
        sine_row = -sine_row
    turned = jnp.concatenate(
        [first * cosine_row - second * sine_row, second * cosine_row + first * sine_row], axis=-1
    )
    return turned.reshape(rows, -1)


def gelu_value(gate):
    bent = jnp.tanh(gelu_coef * (gate + cubic_coef * gate * gate * gate))
    return 0.5 * gate * (1.0 + bent)


def gelu_slope(gate):
    bent = jnp.tanh(gelu_coef * (gate + cubic_coef * gate * gate * gate))
    return 0.5 * (1.0 + bent) + 0.5 * gate * (1.0 - bent * bent) * gelu_coef * (
        1.0 + 3.0 * cubic_coef * gate * gate
    )


def contract_rows(left, right):
    return lax.dot_general(
        left, right, (((0,), (0,)), ((), ())), preferred_element_type=jnp.float32
    )


def contract_cols(left, right):
    return lax.dot_general(
        left, right, (((1,), (1,)), ((), ())), preferred_element_type=jnp.float32
    )


def attend_kernel(heads, live_ref, query_ref, pair_ref, at_ref, pos_ref, start_ref, mixed_ref, log_ref, sums, totals):
    step = pl.program_id(0)
    scale = HEAD_DIM ** (-0.5)

    @pl.when(step == 0)
    def _():
        sums[...] = jnp.zeros_like(sums)
        totals[...] = jnp.zeros_like(totals)

    @pl.when(live_ref[step] > 0)
    def _():
        keys = pair_ref[:, :HEAD_DIM]
        turned = pair_ref[:, HEAD_DIM:].T
        allowed = (at_ref[...] >= start_ref[...]) & (at_ref[...] <= pos_ref[...])
        for head in range(heads):
            cols = slice(head * HEAD_DIM, (head + 1) * HEAD_DIM)
            bent = jnp.tanh(contract_cols(keys, query_ref[:, cols]) * (scale / softcap))
            expo = jnp.where(allowed, jnp.exp(softcap * bent), 0.0)
            totals[head : head + 1, :] += jnp.sum(expo, axis=0, keepdims=True)
            sums[head] += jnp.dot(turned, expo.astype(jnp.bfloat16), preferred_element_type=jnp.float32)

    @pl.when(step == pl.num_programs(0) - 1)
    def _():
        log_ref[...] = jnp.log(totals[...])
        for head in range(heads):
            cols = slice(head * HEAD_DIM, (head + 1) * HEAD_DIM)
            mixed = sums[head] / totals[head : head + 1, :]
            mixed_ref[:, cols] = mixed.T.astype(jnp.bfloat16)


def attend(live, query, pairs, key_at, query_pos, query_start, block):
    rows, width = query.shape
    heads = width // HEAD_DIM
    steps = pairs.shape[0] // block
    row = pl.BlockSpec((1, rows), lambda i, live: (0, 0))
    return pl.pallas_call(
        functools.partial(attend_kernel, heads),
        grid_spec=pltpu.PrefetchScalarGridSpec(
            num_scalar_prefetch=1,
            grid=(steps,),
            in_specs=[
                pl.BlockSpec((rows, width), lambda i, live: (0, 0)),
                pl.BlockSpec((block, pairs.shape[1]), lambda i, live: (i, 0)),
                pl.BlockSpec((block, 1), lambda i, live: (i, 0)),
                row,
                row,
            ],
            out_specs=[
                pl.BlockSpec((rows, width), lambda i, live: (0, 0)),
                pl.BlockSpec((heads, rows), lambda i, live: (0, 0)),
            ],
            scratch_shapes=[
                pltpu.VMEM((heads, HEAD_DIM, rows), jnp.float32),
                pltpu.VMEM((heads, rows), jnp.float32),
            ],
        ),
        out_shape=[
            jax.ShapeDtypeStruct((rows, width), jnp.bfloat16),
            jax.ShapeDtypeStruct((heads, rows), jnp.float32),
        ],
        cost_estimate=pl.CostEstimate(
            flops=4 * rows * width * pairs.shape[0],
            bytes_accessed=2 * pairs.size + 4 * query.size,
            transcendentals=2 * rows * heads * pairs.shape[0],
        ),
        name="attend",
    )(live, query, pairs, key_at[:, None], query_pos[None, :], query_start[None, :])


def attend_back_kernel(heads, first, begins, ends, *refs):
    live_ref, query_ref, grad_ref, mixed_ref, pair_ref, at_ref, pos_ref, start_ref, log_ref = refs[:9]
    refs = refs[9:]
    if not begins:
        carry_ref, refs = refs[0], refs[1:]
    if ends:
        cos_ref, sin_ref, refs = refs[0], refs[1], refs[2:]
    query_grad_ref, line_ref, side_ref, sums, delta = refs
    step = pl.program_id(0)
    scale = HEAD_DIM ** (-0.5)

    @pl.when(step == 0)
    def _():
        sums[...] = jnp.zeros_like(sums) if begins else carry_ref[...]
        ones = jnp.ones((8, HEAD_DIM), jnp.bfloat16)
        for head in range(heads):
            cols = slice(head * HEAD_DIM, (head + 1) * HEAD_DIM)
            grad = grad_ref[:, cols].astype(jnp.float32)
            product = grad * mixed_ref[:, cols].astype(jnp.float32)
            high = product.astype(jnp.bfloat16)
            low = (product - high.astype(jnp.float32)).astype(jnp.bfloat16)
            delta[head * 8 : head * 8 + 8, :] = contract_cols(ones, high) + contract_cols(ones, low)

    def work(out_ref):
        keys = pair_ref[:, :HEAD_DIM]
        values = pair_ref[:, HEAD_DIM:]
        allowed = (at_ref[...] >= start_ref[...]) & (at_ref[...] <= pos_ref[...])
        key_grad = None
        value_grad = None
        for head in range(heads):
            cols = slice(head * HEAD_DIM, (head + 1) * HEAD_DIM)
            query = query_ref[:, cols]
            grad = grad_ref[:, cols]
            bent = jnp.tanh(contract_cols(keys, query) * (scale / softcap))
            probs = jnp.where(
                allowed, jnp.exp(softcap * bent - log_ref[head : head + 1, :]), 0.0
            )
            value_part = jnp.dot(
                probs.astype(jnp.bfloat16), grad, preferred_element_type=jnp.float32
            )
            slope = contract_cols(values, grad) - delta[head * 8 : head * 8 + 1, :]
            score = (probs * slope * (1.0 - bent * bent)).astype(jnp.bfloat16)
            key_part = jnp.dot(score, query, preferred_element_type=jnp.float32)
            sums[:, cols] += contract_rows(score, keys)
            key_grad = key_part if key_grad is None else key_grad + key_part
            value_grad = value_part if value_grad is None else value_grad + value_part
        out_ref[:, :HEAD_DIM] = (key_grad * scale).astype(jnp.bfloat16)
        out_ref[:, HEAD_DIM:] = value_grad.astype(jnp.bfloat16)

    @pl.when(step == 0)
    def _():
        line_ref[...] = jnp.zeros_like(line_ref)
        side_ref[...] = jnp.zeros_like(side_ref)

    @pl.when((step == 0) & (live_ref[first] > 0))
    def _():
        work(line_ref)

    @pl.when((step == 1) & (live_ref[first + 1] > 0))
    def _():
        work(side_ref)

    @pl.when(step == 1)
    def _():
        if not ends:
            query_grad_ref[...] = sums[...]
            return
        half = HEAD_DIM // 2
        for head in range(heads):
            near = slice(head * HEAD_DIM, head * HEAD_DIM + half)
            far = slice(head * HEAD_DIM + half, (head + 1) * HEAD_DIM)
            one = sums[:, near] * scale
            two = sums[:, far] * scale
            query_grad_ref[:, near] = (one * cos_ref[...] + two * sin_ref[...]).astype(jnp.bfloat16)
            query_grad_ref[:, far] = (two * cos_ref[...] - one * sin_ref[...]).astype(jnp.bfloat16)


def attend_back(
    live, query, grad, mixed, pairs, key_at, query_pos, query_start, log_totals, carry, turns, first
):
    rows, width = query.shape
    heads = width // HEAD_DIM
    block = rows
    row = pl.BlockSpec((1, rows), lambda i, live: (0, 0))
    head_row = pl.BlockSpec((heads, rows), lambda i, live: (0, 0))
    full = pl.BlockSpec((rows, width), lambda i, live: (0, 0))
    part = pl.BlockSpec((block, pairs.shape[1]), lambda i, live: (0, 0))
    more_specs = []
    more = []
    if carry is not None:
        more_specs.append(full)
        more.append(carry)
    if turns is not None:
        turn_spec = pl.BlockSpec((rows, HEAD_DIM // 2), lambda i, live: (0, 0))
        more_specs += [turn_spec, turn_spec]
        more += list(turns)
    part_shape = jax.ShapeDtypeStruct((block, pairs.shape[1]), jnp.bfloat16)
    return pl.pallas_call(
        functools.partial(attend_back_kernel, heads, first, carry is None, turns is not None),
        grid_spec=pltpu.PrefetchScalarGridSpec(
            num_scalar_prefetch=1,
            grid=(2,),
            in_specs=[
                full,
                full,
                full,
                pl.BlockSpec((block, pairs.shape[1]), lambda i, live: (i + first, 0)),
                pl.BlockSpec((block, 1), lambda i, live: (i + first, 0)),
                row,
                row,
                head_row,
                *more_specs,
            ],
            out_specs=[full, part, part],
            scratch_shapes=[
                pltpu.VMEM((rows, width), jnp.float32),
                pltpu.VMEM((heads * 8, rows), jnp.float32),
            ],
        ),
        out_shape=[
            jax.ShapeDtypeStruct(
                (rows, width), jnp.float32 if turns is None else jnp.bfloat16
            ),
            part_shape,
            part_shape,
        ],
        cost_estimate=pl.CostEstimate(
            flops=20 * rows * width * block,
            bytes_accessed=8 * block * width + 8 * query.size,
            transcendentals=4 * rows * heads * block,
        ),
        name="attend_back",
    )(
        live,
        query,
        grad,
        mixed,
        pairs,
        key_at[:, None],
        query_pos[None, :],
        query_start[None, :],
        log_totals,
        *more,
    )


def project_kernel(turned, split, rows_ref, weight_ref, cos_ref, sin_ref, query_ref, pair_ref):
    step = pl.program_id(0)
    half = HEAD_DIM // 2
    product = jnp.dot(rows_ref[...], weight_ref[...], preferred_element_type=jnp.float32)

    def store(out_ref, turn):
        one = product[:, :half]
        two = product[:, half:]
        if turn:
            cosine = cos_ref[...]
            sine = sin_ref[...]
            one, two = one * cosine - two * sine, two * cosine + one * sine
        out_ref[:, :half] = one.astype(jnp.bfloat16)
        out_ref[:, half:] = two.astype(jnp.bfloat16)

    @pl.when(step < split)
    def _():
        store(query_ref, True)

    @pl.when((step >= split) & (step < turned))
    def _():
        store(pair_ref, True)

    @pl.when(step >= turned)
    def _():
        store(pair_ref, False)


def project(rows, weight, cosine, sine, query_cols, key_cols):
    count = rows.shape[0]
    split = query_cols // HEAD_DIM
    steps = weight.shape[1] // HEAD_DIM
    turn_spec = pl.BlockSpec((count, HEAD_DIM // 2), lambda i: (0, 0))
    return pl.pallas_call(
        functools.partial(project_kernel, split + key_cols // HEAD_DIM, split),
        grid=(steps,),
        in_specs=[
            pl.BlockSpec(rows.shape, lambda i: (0, 0)),
            pl.BlockSpec((weight.shape[0], HEAD_DIM), lambda i: (0, i)),
            turn_spec,
            turn_spec,
        ],
        out_specs=[
            pl.BlockSpec((count, HEAD_DIM), lambda i: (0, jnp.minimum(i, split - 1))),
            pl.BlockSpec((count, HEAD_DIM), lambda i: (0, jnp.maximum(i - split, 0))),
        ],
        out_shape=[
            jax.ShapeDtypeStruct((count, query_cols), jnp.bfloat16),
            jax.ShapeDtypeStruct((count, 2 * key_cols), jnp.bfloat16),
        ],
        cost_estimate=pl.CostEstimate(
            flops=2 * rows.size * weight.shape[1],
            bytes_accessed=2 * (rows.size + weight.size + count * weight.shape[1]),
            transcendentals=0,
        ),
        name="project",
    )(rows, weight, cosine, sine)


def after(value, *others):
    return lax.optimization_barrier((value,) + others)[0]


def layer(
    inputs,
    cotangent,
    segments,
    first_gain,
    second_gain,
    third_gain,
    fourth_gain,
    query_weight,
    key_weight,
    value_weight,
    output_weight,
    gate_weight,
    up_weight,
    down_weight,
):
    tokens = inputs.shape[0]
    width = inputs.shape[1]
    own_rows = query_weight.shape[0]
    seq_count = lax.axis_size("seq")
    count = lax.axis_size("fsdp")
    seq_rank = lax.axis_index("seq")
    fsdp_rank = lax.axis_index("fsdp")
    half = count // 2
    bf16 = jnp.bfloat16
    head_rows = tokens * seq_count
    query_cols = query_weight.shape[1] // seq_count
    key_cols = key_weight.shape[1] // seq_count

    cycle = [2 * i for i in range(half)] + [2 * i + 1 for i in reversed(range(half))]
    ahead = [(cycle[i], cycle[(i + 1) % count]) for i in range(count)]
    behind = [(b, a) for a, b in ahead]
    place = jnp.where(fsdp_rank % 2 == 0, fsdp_rank // 2, count - 1 - fsdp_rank // 2)

    def rank_at(step):
        spot = lax.rem(place + step + count, count)
        return jnp.where(spot < half, 2 * spot, 2 * (count - 1 - spot) + 1)

    def flip(value, bits):
        return lax.ppermute(value, "seq", [(i, i ^ bits) for i in range(seq_count)])

    def hop(value, pairs):
        return lax.ppermute(value, "fsdp", pairs)

    def ring_gather(value, axis):
        groups = [[value]]
        from_behind = value
        from_ahead = value
        for _ in range(1, half):
            from_behind = hop(from_behind, ahead)
            from_ahead = hop(from_ahead, behind)
            groups.append([from_behind, from_ahead])
        cut = value.shape[axis] // 2
        low = lax.slice_in_dim(from_behind, 0, cut, axis=axis)
        high = lax.slice_in_dim(from_ahead, cut, value.shape[axis], axis=axis)
        low = hop(low, ahead)
        high = hop(high, behind)
        groups.append([jnp.concatenate([low, high], axis=axis)])
        return groups

    def ring_scatter(part_at, axis):
        far = part_at(half)
        cut = far.shape[axis] // 2
        low = lax.slice_in_dim(far, 0, cut, axis=axis).astype(bf16)
        high = lax.slice_in_dim(far, cut, far.shape[axis], axis=axis).astype(bf16)
        low, high = lax.optimization_barrier((hop(low, ahead), hop(high, behind)))
        low = low.astype(jnp.float32)
        high = high.astype(jnp.float32)
        blank = jnp.zeros_like(low)
        onward = jnp.concatenate([low, blank], axis=axis)
        back = jnp.concatenate([blank, high], axis=axis)
        for step in range(half - 1, 0, -1):
            onward = (part_at(step) + onward).astype(bf16)
            back = (part_at(-step) + back).astype(bf16)
            onward, back = lax.optimization_barrier((hop(onward, ahead), hop(back, behind)))
            onward = onward.astype(jnp.float32)
            back = back.astype(jnp.float32)
        return part_at(0) + onward + back

    def seq_gather(value):
        across = flip(value, 2)
        beside = flip(value, 1)
        return [value, beside, across, flip(across, 1)]

    def seq_scatter(parts):
        near = flip(parts[1].astype(bf16), 1).astype(jnp.float32)
        far = flip(parts[3].astype(bf16), 1).astype(jnp.float32)
        across = flip((parts[2] + far).astype(bf16), 2).astype(jnp.float32)
        return parts[0] + near + across

    def sum_all(value):
        bits = 1
        while bits < count:
            value = value + hop(value, [(i, i ^ bits) for i in range(count)])
            bits *= 2
        bits = 1
        while bits < seq_count:
            value = value + flip(value, bits)
            bits *= 2
        return value

    own_start = (seq_rank * count + fsdp_rank) * own_rows
    packed = jnp.stack([first_gain, second_gain, third_gain, fourth_gain])
    gains = sum_all(lax.dynamic_update_slice(jnp.zeros((4, width), bf16), packed, (0, own_start)))
    gain_one, gain_two, gain_three, gain_four = gains[0], gains[1], gains[2], gains[3]

    def columns(weight, rank, size):
        return lax.dynamic_slice_in_dim(weight, rank * size, size, 1)

    def head_columns(rank):
        return jnp.concatenate(
            [
                columns(query_weight, rank, query_cols),
                columns(key_weight, rank, key_cols),
                columns(value_weight, rank, key_cols),
            ],
            axis=1,
        )

    def exchange(pick):
        pieces = [pick(seq_rank)] + [
            flip(pick(seq_rank ^ j), j) for j in range(1, seq_count)
        ]
        chunk = jnp.zeros((seq_count,) + pieces[0].shape, bf16)
        for j, piece in enumerate(pieces):
            chunk = lax.dynamic_update_slice(chunk, piece[None], (seq_rank ^ j, 0, 0))
        return chunk

    def assemble(groups):
        cols = groups[0][0].shape[2]
        whole_weight = jnp.zeros((seq_count, count, own_rows, cols), bf16)
        for step, group in enumerate(groups):
            for rank, piece in zip((rank_at(-step), rank_at(step)), group):
                whole_weight = lax.dynamic_update_slice(
                    whole_weight, piece[:, None], (0, rank, 0, 0)
                )
        return whole_weight.reshape(width, cols)

    head_chunk = exchange(head_columns)
    rows_in = seq_gather(after(inputs, head_chunk))
    out_chunk = exchange(lambda rank: columns(output_weight, rank, query_cols))
    head_groups = ring_gather(head_chunk, 2)
    in_full = assemble(head_groups)

    def block_pos(rank):
        return jnp.concatenate(
            [
                (rank * seq_count + (seq_rank ^ j)) * tokens + jnp.arange(tokens, dtype=jnp.int32)
                for j in range(seq_count)
            ]
        )

    head_pos = block_pos(fsdp_rank)
    head_seg = jnp.concatenate(
        [
            lax.dynamic_slice_in_dim(
                segments, (fsdp_rank * seq_count + (seq_rank ^ j)) * tokens, tokens, 0
            )
            for j in range(seq_count)
        ]
    )
    head_start = jnp.sum((segments[None, :] < head_seg[:, None]).astype(jnp.int32), axis=1)

    head_in = jnp.concatenate(rows_in, axis=0).astype(jnp.float32)
    whole = inputs.astype(jnp.float32)
    normed = lax.optimization_barrier(rms_forward(head_in, gain_one).astype(bf16))
    head_cos, head_sin = rotation(head_pos)
    query_head, pair = project(normed, in_full, head_cos, head_sin, query_cols, key_cols)

    up_line = [(i, i + 2) for i in range(count - 2)]
    down_line = [(b, a) for a, b in up_line]
    reach = half // 2

    def sideways(step, reverse):
        to_odd = [(2 * i, 2 * i + 1) for i in range(half)]
        to_even = [(2 * i + 1, 2 * i) for i in range(half)]
        pairs = to_odd if step == 0 else to_even if step == reach else to_odd + to_even
        return [(b, a) for a, b in pairs] if reverse else pairs

    line = [pair]
    while len(line) <= reach:
        line.append(hop(line[-1], up_line))
    side = [hop(line[k], sideways(k, False)) for k in range(reach + 1)]
    out_chunk = after(out_chunk, head_groups[-1][0])
    out_groups = ring_gather(out_chunk, 2)
    out_full = assemble(out_groups)

    pieces = []
    places = []
    for k in range(reach + 1):
        pieces += [line[k], side[k]]
        places += [block_pos(fsdp_rank - 2 * k), block_pos((fsdp_rank ^ 1) - 2 * k)]
    pairs_all = jnp.concatenate(pieces, axis=0)
    key_pos = jnp.concatenate(places)
    low_start = jnp.min(head_start)
    ranks = []
    for k in range(reach + 1):
        ranks += [fsdp_rank - 2 * k, (fsdp_rank ^ 1) - 2 * k]
    ranks = jnp.stack(ranks)
    live = (ranks >= 0) & (ranks <= fsdp_rank) & ((ranks + 1) * head_rows > low_start)
    live = live.astype(jnp.int32)
    mixed_head, log_totals = attend(
        live, query_head, pairs_all, key_pos, head_pos, head_start, head_rows
    )
    attended_part = contract_cols(mixed_head, out_full)
    attended = seq_scatter(jnp.split(attended_part, seq_count, axis=0))
    middle = whole + rms_forward(attended, gain_two)
    ffn_in = rms_forward(middle, gain_three).astype(bf16)
    upstream = cotangent.astype(jnp.float32)

    blank = jnp.zeros((-2 * gate_weight.shape[0] % 128, width), bf16)

    def unit_rows(weight):
        weight = after(weight, rows_in[2])
        across = flip(weight, 2)
        beside = flip(weight, 1)
        both = flip(after(across, line[reach]), 1)
        return jnp.concatenate([weight, across, blank, beside, both, blank], axis=0)

    gate_units, up_units, down_units = (
        unit_rows(weight)
        for weight in (gate_weight, up_weight, down_weight)
    )

    def joined(groups):
        return [group[0] if len(group) == 1 else jnp.concatenate(group, axis=0) for group in groups]

    def part_of(parts):
        def part_at(step):
            if step == 0:
                return parts[0]
            if abs(step) == half:
                return parts[half]
            part = parts[abs(step)]
            return part[tokens:] if step > 0 else part[:tokens]

        return part_at

    row_groups = joined(ring_gather(ffn_in, 0))
    gates, ups, hiddens, mlp_parts = [], [], [], []
    for rows in row_groups:
        gate = contract_cols(rows, gate_units)
        up = contract_cols(rows, up_units)
        hidden = (gelu_value(gate) * up).astype(bf16)
        gates.append(gate)
        ups.append(up)
        hiddens.append(hidden)
        mlp_parts.append(jnp.dot(hidden, down_units, preferred_element_type=jnp.float32))
    mlp = ring_scatter(part_of(mlp_parts), 0)
    layer_out = middle + rms_forward(mlp, gain_four)
    mlp_grad, fourth_part = rms_backward(mlp, gain_four, upstream)
    mlp_round = mlp_grad.astype(bf16)
    grad_groups = joined(ring_gather(mlp_round, 0))
    gate_deltas, up_deltas, in_parts = [], [], []
    for grads, gate, up in zip(grad_groups, gates, ups):
        hidden_grad = contract_cols(grads, down_units)
        gate_delta = (hidden_grad * up * gelu_slope(gate)).astype(bf16)
        up_delta = (hidden_grad * gelu_value(gate)).astype(bf16)
        gate_deltas.append(gate_delta)
        up_deltas.append(up_delta)
        in_parts.append(
            jnp.dot(gate_delta, gate_units, preferred_element_type=jnp.float32)
            + jnp.dot(up_delta, up_units, preferred_element_type=jnp.float32)
        )
    ffn_in_grad = ring_scatter(part_of(in_parts), 0)

    middle_part, third_part = rms_backward(middle, gain_three, ffn_in_grad)
    middle_grad = upstream + middle_part
    attended_grad, second_part = rms_backward(attended, gain_two, middle_grad)
    attended_round = attended_grad.astype(bf16)
    attended_blocks = seq_gather(attended_round)
    attended_rows = jnp.concatenate(attended_blocks, axis=0)

    all_rows = jnp.concatenate(row_groups, axis=0)
    all_grads = jnp.concatenate(grad_groups, axis=0)

    def unit_grad(left, right):
        units = gate_weight.shape[0]
        left = jnp.concatenate(left, axis=0)
        cut = left.shape[1] // 2
        far = contract_rows(left[:, cut:], right).astype(bf16)
        near = contract_rows(left[:, :cut], right).astype(bf16)
        beside = flip(far, 1)

        def both(begin):
            return near[begin : begin + units].astype(jnp.float32) + beside[
                begin : begin + units
            ].astype(jnp.float32)

        across = flip(both(units).astype(bf16), 2)
        return both(0) + across.astype(jnp.float32)

    down_grad = unit_grad(hiddens, all_grads)
    gate_grad = unit_grad(gate_deltas, all_rows)
    up_grad = unit_grad(up_deltas, all_rows)

    mixed_grad_head = jnp.dot(
        attended_rows, out_full, preferred_element_type=jnp.float32
    ).astype(bf16)

    def weight_grad(left, right):
        full = contract_rows(left, right).reshape(seq_count, count, own_rows, -1)
        return ring_scatter(
            lambda step: lax.dynamic_slice_in_dim(full, rank_at(step), 1, 1)[:, 0], 2
        ).astype(bf16)

    def to_owners(chunk):
        return [
            flip(lax.dynamic_slice_in_dim(chunk, seq_rank ^ j, 1, 0)[0], j)
            if j
            else lax.dynamic_slice_in_dim(chunk, seq_rank, 1, 0)[0]
            for j in range(seq_count)
        ]

    def spread(pieces):
        cols = pieces[0].shape[1]
        out = jnp.zeros((own_rows, cols * seq_count), jnp.float32)
        for j, piece in enumerate(pieces):
            out = lax.dynamic_update_slice(
                out, piece.astype(jnp.float32), (0, (seq_rank ^ j) * cols)
            )
        return out

    carry = None
    total = None
    for k in range(reach, -1, -1):
        carry, line_part, side_part = attend_back(
            live,
            query_head,
            mixed_grad_head,
            mixed_head,
            pairs_all,
            key_pos,
            head_pos,
            head_start,
            log_totals,
            carry,
            None if k else (head_cos, head_sin),
            2 * k,
        )
        here = line_part.astype(jnp.float32) + hop(side_part, sideways(k, True)).astype(jnp.float32)
        if total is not None:
            here = here + hop(total.astype(bf16), down_line).astype(jnp.float32)
        total = here
    query_back = carry
    key_back = rope_apply(total[:, :key_cols], head_cos, head_sin, True).astype(bf16)
    value_back = total[:, key_cols:].astype(bf16)
    output_chunk = weight_grad(attended_rows, mixed_head)
    output_grad = spread(to_owners(output_chunk))
    head_back = jnp.concatenate([query_back, key_back, value_back], axis=1)
    head_pieces = to_owners(weight_grad(normed, head_back))
    value_begin = query_cols + key_cols
    query_grad = spread([piece[:, :query_cols] for piece in head_pieces])
    key_grad = spread([piece[:, query_cols:value_begin] for piece in head_pieces])
    value_grad = spread([piece[:, value_begin:] for piece in head_pieces])
    normed_part = contract_cols(head_back, in_full)
    normed_grad = seq_scatter(jnp.split(normed_part, seq_count, axis=0))
    head_scaling = lax.rsqrt(jnp.mean(head_in * head_in, axis=-1, keepdims=True) + epsilon)
    first_part = jnp.sum(normed_part * head_in * head_scaling, axis=0)
    input_part, _ = rms_backward(whole, gain_one, normed_grad)
    input_grad = middle_grad + input_part

    gain_parts = jnp.stack([first_part, second_part, third_part, fourth_part])
    gain_grads = lax.dynamic_slice_in_dim(sum_all(gain_parts), own_start, own_rows, 1)
    return (
        layer_out,
        input_grad,
        gain_grads[0],
        gain_grads[1],
        gain_grads[2],
        gain_grads[3],
        query_grad,
        key_grad,
        value_grad,
        output_grad,
        gate_grad,
        up_grad,
        down_grad,
    )


def solution(mesh):
    placed = (
        P(("fsdp", "seq"), None),
        P(("fsdp", "seq"), None),
        P(),
        P(("seq", "fsdp")),
        P(("seq", "fsdp")),
        P(("seq", "fsdp")),
        P(("seq", "fsdp")),
        P(("seq", "fsdp"), None),
        P(("seq", "fsdp"), None),
        P(("seq", "fsdp"), None),
        P(("seq", "fsdp"), None),
        P(("seq", "fsdp"), None),
        P(("seq", "fsdp"), None),
        P(("seq", "fsdp"), None),
    )
    return jax.shard_map(
        layer,
        mesh=mesh,
        in_specs=placed,
        out_specs=(
            P(("fsdp", "seq"), None),
            P(("fsdp", "seq"), None),
            P(("seq", "fsdp")),
            P(("seq", "fsdp")),
            P(("seq", "fsdp")),
            P(("seq", "fsdp")),
            P(("seq", "fsdp"), None),
            P(("seq", "fsdp"), None),
            P(("seq", "fsdp"), None),
            P(("seq", "fsdp"), None),
            P(("seq", "fsdp"), None),
            P(("seq", "fsdp"), None),
            P(("seq", "fsdp"), None),
        ),
        check_vma=False,
    )
```

```python
import functools

import jax
import jax.numpy as jnp
from jax import lax
from jax.experimental import pallas as pl
from jax.experimental.pallas import tpu as pltpu
from jax.sharding import PartitionSpec as P


HEAD_DIM = 256


epsilon = 1e-06
softcap = 50.0
rope_base = 10000.0
gelu_coef = 0.7978845608028654
cubic_coef = 0.044715


def rms_forward(values, gain):
    scaling = lax.rsqrt(jnp.mean(values * values, axis=-1, keepdims=True) + epsilon)
    return values * scaling * (1.0 + gain.astype(jnp.float32))


def rms_backward(values, gain, upstream):
    scaling = lax.rsqrt(jnp.mean(values * values, axis=-1, keepdims=True) + epsilon)
    weighted = upstream * (1.0 + gain.astype(jnp.float32))
    inner = jnp.mean(weighted * values, axis=-1, keepdims=True)
    grad_values = scaling * weighted - values * (scaling * scaling * scaling) * inner
    grad_gain = jnp.sum(upstream * values * scaling, axis=0)
    return (grad_values, grad_gain)


def rotation(positions):
    half = HEAD_DIM // 2
    frequency = jnp.power(rope_base, -jnp.arange(half, dtype=jnp.float32) / half)
    angles = positions.astype(jnp.float32)[:, None] * frequency[None, :]
    return (jnp.cos(angles), jnp.sin(angles))


def rope_apply(values, cosine, sine, inverse):
    rows = values.shape[0]
    half = HEAD_DIM // 2
    shaped = values.reshape(rows, -1, HEAD_DIM)
    first = shaped[:, :, :half]
    second = shaped[:, :, half:]
    cosine_row = cosine[:, None, :]
    sine_row = sine[:, None, :]
    if inverse:
        sine_row = -sine_row
    turned = jnp.concatenate(
        [first * cosine_row - second * sine_row, second * cosine_row + first * sine_row], axis=-1
    )
    return turned.reshape(rows, -1)


def gelu_value(gate):
    bent = jnp.tanh(gelu_coef * (gate + cubic_coef * gate * gate * gate))
    return 0.5 * gate * (1.0 + bent)


def gelu_slope(gate):
    bent = jnp.tanh(gelu_coef * (gate + cubic_coef * gate * gate * gate))
    return 0.5 * (1.0 + bent) + 0.5 * gate * (1.0 - bent * bent) * gelu_coef * (
        1.0 + 3.0 * cubic_coef * gate * gate
    )


def contract_rows(left, right):
    return lax.dot_general(
        left, right, (((0,), (0,)), ((), ())), preferred_element_type=jnp.float32
    )


def contract_cols(left, right):
    return lax.dot_general(
        left, right, (((1,), (1,)), ((), ())), preferred_element_type=jnp.float32
    )


def attend_kernel(heads, live_ref, query_ref, pair_ref, at_ref, pos_ref, start_ref, mixed_ref, log_ref, sums, totals):
    step = pl.program_id(0)
    scale = HEAD_DIM ** (-0.5)

    @pl.when(step == 0)
    def _():
        sums[...] = jnp.zeros_like(sums)
        totals[...] = jnp.zeros_like(totals)

    @pl.when(live_ref[step] > 0)
    def _():
        keys = pair_ref[:, :HEAD_DIM]
        turned = pair_ref[:, HEAD_DIM:].T
        allowed = (at_ref[...] >= start_ref[...]) & (at_ref[...] <= pos_ref[...])
        for head in range(heads):
            cols = slice(head * HEAD_DIM, (head + 1) * HEAD_DIM)
            bent = jnp.tanh(contract_cols(keys, query_ref[:, cols]) * (scale / softcap))
            expo = jnp.where(allowed, jnp.exp(softcap * bent), 0.0)
            totals[head : head + 1, :] += jnp.sum(expo, axis=0, keepdims=True)
            sums[head] += jnp.dot(turned, expo.astype(jnp.bfloat16), preferred_element_type=jnp.float32)

    @pl.when(step == pl.num_programs(0) - 1)
    def _():
        log_ref[...] = jnp.log(totals[...])
        for head in range(heads):
            cols = slice(head * HEAD_DIM, (head + 1) * HEAD_DIM)
            mixed = sums[head] / totals[head : head + 1, :]
            mixed_ref[:, cols] = mixed.T.astype(jnp.bfloat16)


def attend(live, query, pairs, key_at, query_pos, query_start, block):
    rows, width = query.shape
    heads = width // HEAD_DIM
    steps = pairs.shape[0] // block
    row = pl.BlockSpec((1, rows), lambda i, live: (0, 0))
    return pl.pallas_call(
        functools.partial(attend_kernel, heads),
        grid_spec=pltpu.PrefetchScalarGridSpec(
            num_scalar_prefetch=1,
            grid=(steps,),
            in_specs=[
                pl.BlockSpec((rows, width), lambda i, live: (0, 0)),
                pl.BlockSpec((block, pairs.shape[1]), lambda i, live: (i, 0)),
                pl.BlockSpec((block, 1), lambda i, live: (i, 0)),
                row,
                row,
            ],
            out_specs=[
                pl.BlockSpec((rows, width), lambda i, live: (0, 0)),
                pl.BlockSpec((heads, rows), lambda i, live: (0, 0)),
            ],
            scratch_shapes=[
                pltpu.VMEM((heads, HEAD_DIM, rows), jnp.float32),
                pltpu.VMEM((heads, rows), jnp.float32),
            ],
        ),
        out_shape=[
            jax.ShapeDtypeStruct((rows, width), jnp.bfloat16),
            jax.ShapeDtypeStruct((heads, rows), jnp.float32),
        ],
        cost_estimate=pl.CostEstimate(
            flops=4 * rows * width * pairs.shape[0],
            bytes_accessed=2 * pairs.size + 4 * query.size,
            transcendentals=2 * rows * heads * pairs.shape[0],
        ),
        name="attend",
    )(live, query, pairs, key_at[:, None], query_pos[None, :], query_start[None, :])


def attend_back_kernel(heads, first, begins, ends, *refs):
    live_ref, query_ref, grad_ref, mixed_ref, pair_ref, at_ref, pos_ref, start_ref, log_ref = refs[:9]
    refs = refs[9:]
    if not begins:
        carry_ref, refs = refs[0], refs[1:]
    if ends:
        cos_ref, sin_ref, refs = refs[0], refs[1], refs[2:]
    query_grad_ref, line_ref, side_ref, sums, delta = refs
    step = pl.program_id(0)
    scale = HEAD_DIM ** (-0.5)

    @pl.when(step == 0)
    def _():
        sums[...] = jnp.zeros_like(sums) if begins else carry_ref[...]
        ones = jnp.ones((8, HEAD_DIM), jnp.bfloat16)
        for head in range(heads):
            cols = slice(head * HEAD_DIM, (head + 1) * HEAD_DIM)
            grad = grad_ref[:, cols].astype(jnp.float32)
            product = grad * mixed_ref[:, cols].astype(jnp.float32)
            high = product.astype(jnp.bfloat16)
            low = (product - high.astype(jnp.float32)).astype(jnp.bfloat16)
            delta[head * 8 : head * 8 + 8, :] = contract_cols(ones, high) + contract_cols(ones, low)

    def work(out_ref):
        keys = pair_ref[:, :HEAD_DIM]
        values = pair_ref[:, HEAD_DIM:]
        allowed = (at_ref[...] >= start_ref[...]) & (at_ref[...] <= pos_ref[...])
        key_grad = None
        value_grad = None
        for head in range(heads):
            cols = slice(head * HEAD_DIM, (head + 1) * HEAD_DIM)
            query = query_ref[:, cols]
            grad = grad_ref[:, cols]
            bent = jnp.tanh(contract_cols(keys, query) * (scale / softcap))
            probs = jnp.where(
                allowed, jnp.exp(softcap * bent - log_ref[head : head + 1, :]), 0.0
            )
            value_part = jnp.dot(
                probs.astype(jnp.bfloat16), grad, preferred_element_type=jnp.float32
            )
            slope = contract_cols(values, grad) - delta[head * 8 : head * 8 + 1, :]
            score = (probs * slope * (1.0 - bent * bent)).astype(jnp.bfloat16)
            key_part = jnp.dot(score, query, preferred_element_type=jnp.float32)
            sums[:, cols] += contract_rows(score, keys)
            key_grad = key_part if key_grad is None else key_grad + key_part
            value_grad = value_part if value_grad is None else value_grad + value_part
        out_ref[:, :HEAD_DIM] = (key_grad * scale).astype(jnp.bfloat16)
        out_ref[:, HEAD_DIM:] = value_grad.astype(jnp.bfloat16)

    @pl.when(step == 0)
    def _():
        line_ref[...] = jnp.zeros_like(line_ref)
        side_ref[...] = jnp.zeros_like(side_ref)

    @pl.when((step == 0) & (live_ref[first] > 0))
    def _():
        work(line_ref)

    @pl.when((step == 1) & (live_ref[first + 1] > 0))
    def _():
        work(side_ref)

    @pl.when(step == 1)
    def _():
        if not ends:
            query_grad_ref[...] = sums[...]
            return
        half = HEAD_DIM // 2
        for head in range(heads):
            near = slice(head * HEAD_DIM, head * HEAD_DIM + half)
            far = slice(head * HEAD_DIM + half, (head + 1) * HEAD_DIM)
            one = sums[:, near] * scale
            two = sums[:, far] * scale
            query_grad_ref[:, near] = (one * cos_ref[...] + two * sin_ref[...]).astype(jnp.bfloat16)
            query_grad_ref[:, far] = (two * cos_ref[...] - one * sin_ref[...]).astype(jnp.bfloat16)


def attend_back(
    live, query, grad, mixed, pairs, key_at, query_pos, query_start, log_totals, carry, turns, first
):
    rows, width = query.shape
    heads = width // HEAD_DIM
    block = rows
    row = pl.BlockSpec((1, rows), lambda i, live: (0, 0))
    head_row = pl.BlockSpec((heads, rows), lambda i, live: (0, 0))
    full = pl.BlockSpec((rows, width), lambda i, live: (0, 0))
    part = pl.BlockSpec((block, pairs.shape[1]), lambda i, live: (0, 0))
    more_specs = []
    more = []
    if carry is not None:
        more_specs.append(full)
        more.append(carry)
    if turns is not None:
        turn_spec = pl.BlockSpec((rows, HEAD_DIM // 2), lambda i, live: (0, 0))
        more_specs += [turn_spec, turn_spec]
        more += list(turns)
    part_shape = jax.ShapeDtypeStruct((block, pairs.shape[1]), jnp.bfloat16)
    return pl.pallas_call(
        functools.partial(attend_back_kernel, heads, first, carry is None, turns is not None),
        grid_spec=pltpu.PrefetchScalarGridSpec(
            num_scalar_prefetch=1,
            grid=(2,),
            in_specs=[
                full,
                full,
                full,
                pl.BlockSpec((block, pairs.shape[1]), lambda i, live: (i + first, 0)),
                pl.BlockSpec((block, 1), lambda i, live: (i + first, 0)),
                row,
                row,
                head_row,
                *more_specs,
            ],
            out_specs=[full, part, part],
            scratch_shapes=[
                pltpu.VMEM((rows, width), jnp.float32),
                pltpu.VMEM((heads * 8, rows), jnp.float32),
            ],
        ),
        out_shape=[
            jax.ShapeDtypeStruct(
                (rows, width), jnp.float32 if turns is None else jnp.bfloat16
            ),
            part_shape,
            part_shape,
        ],
        cost_estimate=pl.CostEstimate(
            flops=20 * rows * width * block,
            bytes_accessed=8 * block * width + 8 * query.size,
            transcendentals=4 * rows * heads * block,
        ),
        name="attend_back",
    )(
        live,
        query,
        grad,
        mixed,
        pairs,
        key_at[:, None],
        query_pos[None, :],
        query_start[None, :],
        log_totals,
        *more,
    )


def project_kernel(turned, split, rows_ref, weight_ref, cos_ref, sin_ref, query_ref, pair_ref):
    step = pl.program_id(0)
    half = HEAD_DIM // 2
    product = jnp.dot(rows_ref[...], weight_ref[...], preferred_element_type=jnp.float32)

    def store(out_ref, turn):
        one = product[:, :half]
        two = product[:, half:]
        if turn:
            cosine = cos_ref[...]
            sine = sin_ref[...]
            one, two = one * cosine - two * sine, two * cosine + one * sine
        out_ref[:, :half] = one.astype(jnp.bfloat16)
        out_ref[:, half:] = two.astype(jnp.bfloat16)

    @pl.when(step < split)
    def _():
        store(query_ref, True)

    @pl.when((step >= split) & (step < turned))
    def _():
        store(pair_ref, True)

    @pl.when(step >= turned)
    def _():
        store(pair_ref, False)


def project(rows, weight, cosine, sine, query_cols, key_cols):
    count = rows.shape[0]
    split = query_cols // HEAD_DIM
    steps = weight.shape[1] // HEAD_DIM
    turn_spec = pl.BlockSpec((count, HEAD_DIM // 2), lambda i: (0, 0))
    return pl.pallas_call(
        functools.partial(project_kernel, split + key_cols // HEAD_DIM, split),
        grid=(steps,),
        in_specs=[
            pl.BlockSpec(rows.shape, lambda i: (0, 0)),
            pl.BlockSpec((weight.shape[0], HEAD_DIM), lambda i: (0, i)),
            turn_spec,
            turn_spec,
        ],
        out_specs=[
            pl.BlockSpec((count, HEAD_DIM), lambda i: (0, jnp.minimum(i, split - 1))),
            pl.BlockSpec((count, HEAD_DIM), lambda i: (0, jnp.maximum(i - split, 0))),
        ],
        out_shape=[
            jax.ShapeDtypeStruct((count, query_cols), jnp.bfloat16),
            jax.ShapeDtypeStruct((count, 2 * key_cols), jnp.bfloat16),
        ],
        cost_estimate=pl.CostEstimate(
            flops=2 * rows.size * weight.shape[1],
            bytes_accessed=2 * (rows.size + weight.size + count * weight.shape[1]),
            transcendentals=0,
        ),
        name="project",
    )(rows, weight, cosine, sine)


def after(value, *others):
    return lax.optimization_barrier((value,) + others)[0]


def layer(
    inputs,
    cotangent,
    segments,
    first_gain,
    second_gain,
    third_gain,
    fourth_gain,
    query_weight,
    key_weight,
    value_weight,
    output_weight,
    gate_weight,
    up_weight,
    down_weight,
):
    tokens = inputs.shape[0]
    width = inputs.shape[1]
    own_rows = query_weight.shape[0]
    seq_count = lax.axis_size("seq")
    count = lax.axis_size("fsdp")
    seq_rank = lax.axis_index("seq")
    fsdp_rank = lax.axis_index("fsdp")
    half = count // 2
    bf16 = jnp.bfloat16
    head_rows = tokens * seq_count
    query_cols = query_weight.shape[1] // seq_count
    key_cols = key_weight.shape[1] // seq_count

    cycle = [2 * i for i in range(half)] + [2 * i + 1 for i in reversed(range(half))]
    ahead = [(cycle[i], cycle[(i + 1) % count]) for i in range(count)]
    behind = [(b, a) for a, b in ahead]
    place = jnp.where(fsdp_rank % 2 == 0, fsdp_rank // 2, count - 1 - fsdp_rank // 2)

    def rank_at(step):
        spot = lax.rem(place + step + count, count)
        return jnp.where(spot < half, 2 * spot, 2 * (count - 1 - spot) + 1)

    def flip(value, bits):
        return lax.ppermute(value, "seq", [(i, i ^ bits) for i in range(seq_count)])

    def hop(value, pairs):
        return lax.ppermute(value, "fsdp", pairs)

    def ring_gather(value, axis):
        groups = [[value]]
        from_behind = value
        from_ahead = value
        for _ in range(1, half):
            from_behind = hop(from_behind, ahead)
            from_ahead = hop(from_ahead, behind)
            groups.append([from_behind, from_ahead])
        cut = value.shape[axis] // 2
        low = lax.slice_in_dim(from_behind, 0, cut, axis=axis)
        high = lax.slice_in_dim(from_ahead, cut, value.shape[axis], axis=axis)
        low = hop(low, ahead)
        high = hop(high, behind)
        groups.append([jnp.concatenate([low, high], axis=axis)])
        return groups

    def ring_scatter(part_at, axis):
        far = part_at(half)
        cut = far.shape[axis] // 2
        low = lax.slice_in_dim(far, 0, cut, axis=axis).astype(bf16)
        high = lax.slice_in_dim(far, cut, far.shape[axis], axis=axis).astype(bf16)
        low, high = lax.optimization_barrier((hop(low, ahead), hop(high, behind)))
        low = low.astype(jnp.float32)
        high = high.astype(jnp.float32)
        blank = jnp.zeros_like(low)
        onward = jnp.concatenate([low, blank], axis=axis)
        back = jnp.concatenate([blank, high], axis=axis)
        for step in range(half - 1, 0, -1):
            onward = (part_at(step) + onward).astype(bf16)
            back = (part_at(-step) + back).astype(bf16)
            onward, back = lax.optimization_barrier((hop(onward, ahead), hop(back, behind)))
            onward = onward.astype(jnp.float32)
            back = back.astype(jnp.float32)
        return part_at(0) + onward + back

    def seq_gather(value):
        across = flip(value, 2)
        beside = flip(value, 1)
        return [value, beside, across, flip(across, 1)]

    def seq_scatter(parts):
        near = flip(parts[1].astype(bf16), 1).astype(jnp.float32)
        far = flip(parts[3].astype(bf16), 1).astype(jnp.float32)
        across = flip((parts[2] + far).astype(bf16), 2).astype(jnp.float32)
        return parts[0] + near + across

    def sum_all(value):
        bits = seq_count // 2
        while bits:
            value = value + flip(value, bits)
            bits //= 2
        bits = 1
        while bits < count:
            value = value + hop(value, [(i, i ^ bits) for i in range(count)])
            bits *= 2
        return value

    own_start = (seq_rank * count + fsdp_rank) * own_rows
    packed = jnp.stack([first_gain, second_gain, third_gain, fourth_gain])
    gains = sum_all(lax.dynamic_update_slice(jnp.zeros((4, width), bf16), packed, (0, own_start)))
    gain_one, gain_two, gain_three, gain_four = gains[0], gains[1], gains[2], gains[3]

    def columns(weight, rank, size):
        return lax.dynamic_slice_in_dim(weight, rank * size, size, 1)

    def head_columns(rank):
        return jnp.concatenate(
            [
                columns(query_weight, rank, query_cols),
                columns(key_weight, rank, key_cols),
                columns(value_weight, rank, key_cols),
            ],
            axis=1,
        )

    def exchange(pick):
        pieces = [pick(seq_rank)] + [flip(pick(seq_rank ^ j), j) for j in range(1, seq_count)]
        chunk = jnp.zeros((seq_count,) + pieces[0].shape, bf16)
        for j, piece in enumerate(pieces):
            chunk = lax.dynamic_update_slice(chunk, piece[None], (seq_rank ^ j, 0, 0))
        return chunk

    def assemble(groups):
        cols = groups[0][0].shape[2]
        whole_weight = jnp.zeros((seq_count, count, own_rows, cols), bf16)
        for step, group in enumerate(groups):
            for rank, piece in zip((rank_at(-step), rank_at(step)), group):
                whole_weight = lax.dynamic_update_slice(
                    whole_weight, piece[:, None], (0, rank, 0, 0)
                )
        return whole_weight.reshape(width, cols)

    head_chunk = exchange(head_columns)
    rows_in = seq_gather(after(inputs, head_chunk))
    out_chunk = exchange(lambda rank: columns(output_weight, rank, query_cols))
    head_groups = ring_gather(head_chunk, 2)
    in_full = assemble(head_groups)

    def block_pos(rank):
        return jnp.concatenate(
            [
                (rank * seq_count + (seq_rank ^ j)) * tokens + jnp.arange(tokens, dtype=jnp.int32)
                for j in range(seq_count)
            ]
        )

    head_pos = block_pos(fsdp_rank)
    head_seg = jnp.concatenate(
        [
            lax.dynamic_slice_in_dim(
                segments, (fsdp_rank * seq_count + (seq_rank ^ j)) * tokens, tokens, 0
            )
            for j in range(seq_count)
        ]
    )
    head_start = jnp.sum((segments[None, :] < head_seg[:, None]).astype(jnp.int32), axis=1)

    head_in = jnp.concatenate(rows_in, axis=0).astype(jnp.float32)
    whole = inputs.astype(jnp.float32)
    normed = lax.optimization_barrier(rms_forward(head_in, gain_one).astype(bf16))
    head_cos, head_sin = rotation(head_pos)
    query_head, pair = project(normed, in_full, head_cos, head_sin, query_cols, key_cols)

    up_line = [(i, i + 2) for i in range(count - 2)]
    down_line = [(b, a) for a, b in up_line]
    reach = half // 2

    def sideways(step, reverse):
        to_odd = [(2 * i, 2 * i + 1) for i in range(half)]
        to_even = [(2 * i + 1, 2 * i) for i in range(half)]
        pairs = to_odd if step == 0 else to_even if step == reach else to_odd + to_even
        return [(b, a) for a, b in pairs] if reverse else pairs

    line = [pair]
    while len(line) <= reach:
        line.append(hop(line[-1], up_line))
    side = [hop(line[k], sideways(k, False)) for k in range(reach + 1)]
    out_chunk = after(out_chunk, head_groups[-1][0])
    out_groups = ring_gather(out_chunk, 2)
    out_full = assemble(out_groups)

    pieces = []
    places = []
    for k in range(reach + 1):
        pieces += [line[k], side[k]]
        places += [block_pos(fsdp_rank - 2 * k), block_pos((fsdp_rank ^ 1) - 2 * k)]
    pairs_all = jnp.concatenate(pieces, axis=0)
    key_pos = jnp.concatenate(places)
    low_start = jnp.min(head_start)
    ranks = []
    for k in range(reach + 1):
        ranks += [fsdp_rank - 2 * k, (fsdp_rank ^ 1) - 2 * k]
    ranks = jnp.stack(ranks)
    live = (ranks >= 0) & (ranks <= fsdp_rank) & ((ranks + 1) * head_rows > low_start)
    live = live.astype(jnp.int32)
    mixed_head, log_totals = attend(
        live, query_head, pairs_all, key_pos, head_pos, head_start, head_rows
    )
    attended_part = contract_cols(mixed_head, out_full)
    attended = seq_scatter(jnp.split(attended_part, seq_count, axis=0))
    middle = whole + rms_forward(attended, gain_two)
    ffn_in = rms_forward(middle, gain_three).astype(bf16)
    upstream = cotangent.astype(jnp.float32)

    blank = jnp.zeros((-2 * gate_weight.shape[0] % 128, width), bf16)

    def unit_rows(weight):
        across = flip(weight, 2)
        beside = flip(weight, 1)
        both = flip(after(across, line[reach]), 1)
        weight, beside = after(weight, rows_in[2]), after(beside, rows_in[2])
        across = after(across, side[1])
        return jnp.concatenate([weight, across, blank, beside, both, blank], axis=0)

    gate_units, up_units, down_units = (
        unit_rows(weight)
        for weight in (gate_weight, up_weight, down_weight)
    )

    def joined(groups):
        return [group[0] if len(group) == 1 else jnp.concatenate(group, axis=0) for group in groups]

    def part_of(parts):
        def part_at(step):
            if step == 0:
                return parts[0]
            if abs(step) == half:
                return parts[half]
            part = parts[abs(step)]
            return part[tokens:] if step > 0 else part[:tokens]

        return part_at

    row_groups = joined(ring_gather(ffn_in, 0))
    gates, ups, hiddens, mlp_parts = [], [], [], []
    for rows in row_groups:
        gate = contract_cols(rows, gate_units)
        up = contract_cols(rows, up_units)
        hidden = (gelu_value(gate) * up).astype(bf16)
        gates.append(gate)
        ups.append(up)
        hiddens.append(hidden)
        mlp_parts.append(jnp.dot(hidden, down_units, preferred_element_type=jnp.float32))
    mlp = ring_scatter(part_of(mlp_parts), 0)
    layer_out = middle + rms_forward(mlp, gain_four)
    mlp_grad, fourth_part = rms_backward(mlp, gain_four, upstream)
    mlp_round = mlp_grad.astype(bf16)
    grad_groups = joined(ring_gather(mlp_round, 0))
    gate_deltas, up_deltas, in_parts = [], [], []
    for grads, gate, up in zip(grad_groups, gates, ups):
        hidden_grad = contract_cols(grads, down_units)
        gate_delta = (hidden_grad * up * gelu_slope(gate)).astype(bf16)
        up_delta = (hidden_grad * gelu_value(gate)).astype(bf16)
        gate_deltas.append(gate_delta)
        up_deltas.append(up_delta)
        in_parts.append(
            jnp.dot(gate_delta, gate_units, preferred_element_type=jnp.float32)
            + jnp.dot(up_delta, up_units, preferred_element_type=jnp.float32)
        )
    ffn_in_grad = ring_scatter(part_of(in_parts), 0)

    middle_part, third_part = rms_backward(middle, gain_three, ffn_in_grad)
    middle_grad = upstream + middle_part
    attended_grad, second_part = rms_backward(attended, gain_two, middle_grad)
    attended_round = attended_grad.astype(bf16)
    attended_blocks = seq_gather(attended_round)
    attended_rows = jnp.concatenate(attended_blocks, axis=0)

    all_rows = jnp.concatenate(row_groups, axis=0)
    all_grads = jnp.concatenate(grad_groups, axis=0)

    def unit_grad(left, right):
        units = gate_weight.shape[0]
        left = jnp.concatenate(left, axis=0)
        cut = left.shape[1] // 2
        far = contract_rows(left[:, cut:], right).astype(bf16)
        near = contract_rows(left[:, :cut], right).astype(bf16)
        beside = flip(far, 1)

        def both(begin):
            return near[begin : begin + units].astype(jnp.float32) + beside[
                begin : begin + units
            ].astype(jnp.float32)

        across = flip(both(units).astype(bf16), 2)
        return both(0) + across.astype(jnp.float32)

    down_grad = unit_grad(hiddens, all_grads)
    gate_grad = unit_grad(gate_deltas, all_rows)
    up_grad = unit_grad(up_deltas, all_rows)

    mixed_grad_head = jnp.dot(
        attended_rows, out_full, preferred_element_type=jnp.float32
    ).astype(bf16)

    def weight_grad(left, right):
        full = contract_rows(left, right).reshape(seq_count, count, own_rows, -1)
        return ring_scatter(
            lambda step: lax.dynamic_slice_in_dim(full, rank_at(step), 1, 1)[:, 0], 2
        ).astype(bf16)

    def to_owners(chunk):
        return [
            flip(lax.dynamic_slice_in_dim(chunk, seq_rank ^ j, 1, 0)[0], j)
            if j
            else lax.dynamic_slice_in_dim(chunk, seq_rank, 1, 0)[0]
            for j in range(seq_count)
        ]

    def spread(pieces):
        cols = pieces[0].shape[1]
        out = jnp.zeros((own_rows, cols * seq_count), jnp.float32)
        for j, piece in enumerate(pieces):
            out = lax.dynamic_update_slice(
                out, piece.astype(jnp.float32), (0, (seq_rank ^ j) * cols)
            )
        return out

    carry = None
    total = None
    for k in range(reach, -1, -1):
        carry, line_part, side_part = attend_back(
            live,
            query_head,
            mixed_grad_head,
            mixed_head,
            pairs_all,
            key_pos,
            head_pos,
            head_start,
            log_totals,
            carry,
            None if k else (head_cos, head_sin),
            2 * k,
        )
        side_sum = hop(side_part, sideways(k, True))
        line_sum = None if total is None else hop(total, down_line)
        total = line_part.astype(jnp.float32) + side_sum.astype(jnp.float32)
        if line_sum is not None:
            total = total + line_sum.astype(jnp.float32)
        if k:
            total = total.astype(bf16)
    query_back = carry
    key_back = rope_apply(total[:, :key_cols], head_cos, head_sin, True).astype(bf16)
    value_back = total[:, key_cols:].astype(bf16)
    output_chunk = weight_grad(attended_rows, mixed_head)
    output_grad = spread(to_owners(output_chunk))
    head_back = jnp.concatenate([query_back, key_back, value_back], axis=1)
    head_pieces = to_owners(weight_grad(normed, head_back))
    value_begin = query_cols + key_cols
    query_grad = spread([piece[:, :query_cols] for piece in head_pieces])
    key_grad = spread([piece[:, query_cols:value_begin] for piece in head_pieces])
    value_grad = spread([piece[:, value_begin:] for piece in head_pieces])
    normed_part = contract_cols(head_back, in_full)
    normed_grad = seq_scatter(jnp.split(normed_part, seq_count, axis=0))
    head_scaling = lax.rsqrt(jnp.mean(head_in * head_in, axis=-1, keepdims=True) + epsilon)
    first_part = jnp.sum(normed_part * head_in * head_scaling, axis=0)
    input_part, _ = rms_backward(whole, gain_one, normed_grad)
    input_grad = middle_grad + input_part

    gain_parts = jnp.stack([first_part, second_part, third_part, fourth_part])
    gain_parts = gain_parts.reshape(4, seq_count, count, own_rows)
    gain_sums = gain_parts
    bits = 1
    while bits < count:
        pairs = [(i, i ^ bits) for i in range(count)]
        gain_sums = gain_sums + hop(gain_sums, pairs)
        bits *= 2
    gain_sums = lax.dynamic_slice_in_dim(gain_sums, fsdp_rank, 1, 2)[:, :, 0]
    gain_grads = None
    for j in range(seq_count):
        piece = lax.dynamic_slice_in_dim(gain_sums, seq_rank ^ j, 1, 1)[:, 0]
        piece = flip(piece, j) if j else piece
        gain_grads = piece if gain_grads is None else gain_grads + piece
    return (
        layer_out,
        input_grad,
        gain_grads[0],
        gain_grads[1],
        gain_grads[2],
        gain_grads[3],
        query_grad,
        key_grad,
        value_grad,
        output_grad,
        gate_grad,
        up_grad,
        down_grad,
    )


def solution(mesh):
    placed = (
        P(("fsdp", "seq"), None),
        P(("fsdp", "seq"), None),
        P(),
        P(("seq", "fsdp")),
        P(("seq", "fsdp")),
        P(("seq", "fsdp")),
        P(("seq", "fsdp")),
        P(("seq", "fsdp"), None),
        P(("seq", "fsdp"), None),
        P(("seq", "fsdp"), None),
        P(("seq", "fsdp"), None),
        P(("seq", "fsdp"), None),
        P(("seq", "fsdp"), None),
        P(("seq", "fsdp"), None),
    )
    return jax.shard_map(
        layer,
        mesh=mesh,
        in_specs=placed,
        out_specs=(
            P(("fsdp", "seq"), None),
            P(("fsdp", "seq"), None),
            P(("seq", "fsdp")),
            P(("seq", "fsdp")),
            P(("seq", "fsdp")),
            P(("seq", "fsdp")),
            P(("seq", "fsdp"), None),
            P(("seq", "fsdp"), None),
            P(("seq", "fsdp"), None),
            P(("seq", "fsdp"), None),
            P(("seq", "fsdp"), None),
            P(("seq", "fsdp"), None),
            P(("seq", "fsdp"), None),
        ),
        check_vma=False,
    )
```

```python
import functools

import jax
import jax.numpy as jnp
from jax import lax
from jax.experimental import pallas as pl
from jax.experimental.pallas import tpu as pltpu
from jax.sharding import PartitionSpec as P


HEAD_DIM = 256


epsilon = 1e-06
softcap = 50.0
rope_base = 10000.0
gelu_coef = 0.7978845608028654
cubic_coef = 0.044715


def rms_forward(values, gain):
    scaling = lax.rsqrt(jnp.mean(values * values, axis=-1, keepdims=True) + epsilon)
    return values * scaling * (1.0 + gain.astype(jnp.float32))


def rms_backward(values, gain, upstream):
    scaling = lax.rsqrt(jnp.mean(values * values, axis=-1, keepdims=True) + epsilon)
    weighted = upstream * (1.0 + gain.astype(jnp.float32))
    inner = jnp.mean(weighted * values, axis=-1, keepdims=True)
    grad_values = scaling * weighted - values * (scaling * scaling * scaling) * inner
    grad_gain = jnp.sum(upstream * values * scaling, axis=0)
    return (grad_values, grad_gain)


def rotation(positions):
    half = HEAD_DIM // 2
    frequency = jnp.power(rope_base, -jnp.arange(half, dtype=jnp.float32) / half)
    angles = positions.astype(jnp.float32)[:, None] * frequency[None, :]
    return (jnp.cos(angles), jnp.sin(angles))


def rope_apply(values, cosine, sine, inverse):
    rows = values.shape[0]
    half = HEAD_DIM // 2
    shaped = values.reshape(rows, -1, HEAD_DIM)
    first = shaped[:, :, :half]
    second = shaped[:, :, half:]
    cosine_row = cosine[:, None, :]
    sine_row = sine[:, None, :]
    if inverse:
        sine_row = -sine_row
    turned = jnp.concatenate(
        [first * cosine_row - second * sine_row, second * cosine_row + first * sine_row], axis=-1
    )
    return turned.reshape(rows, -1)


def gelu_value(gate):
    bent = jnp.tanh(gelu_coef * (gate + cubic_coef * gate * gate * gate))
    return 0.5 * gate * (1.0 + bent)


def gelu_slope(gate):
    bent = jnp.tanh(gelu_coef * (gate + cubic_coef * gate * gate * gate))
    return 0.5 * (1.0 + bent) + 0.5 * gate * (1.0 - bent * bent) * gelu_coef * (
        1.0 + 3.0 * cubic_coef * gate * gate
    )


def contract_rows(left, right):
    return lax.dot_general(
        left, right, (((0,), (0,)), ((), ())), preferred_element_type=jnp.float32
    )


def contract_cols(left, right):
    return lax.dot_general(
        left, right, (((1,), (1,)), ((), ())), preferred_element_type=jnp.float32
    )


def attend_kernel(heads, live_ref, query_ref, pair_ref, at_ref, pos_ref, start_ref, mixed_ref, log_ref, sums, totals):
    step = pl.program_id(0)
    scale = HEAD_DIM ** (-0.5)

    @pl.when(step == 0)
    def _():
        sums[...] = jnp.zeros_like(sums)
        totals[...] = jnp.zeros_like(totals)

    @pl.when(live_ref[step] > 0)
    def _():
        keys = pair_ref[:, :HEAD_DIM]
        turned = pair_ref[:, HEAD_DIM:].T
        allowed = (at_ref[...] >= start_ref[...]) & (at_ref[...] <= pos_ref[...])
        for head in range(heads):
            cols = slice(head * HEAD_DIM, (head + 1) * HEAD_DIM)
            bent = jnp.tanh(contract_cols(keys, query_ref[:, cols]) * (scale / softcap))
            expo = jnp.where(allowed, jnp.exp(softcap * bent), 0.0)
            totals[head : head + 1, :] += jnp.sum(expo, axis=0, keepdims=True)
            sums[head] += jnp.dot(turned, expo.astype(jnp.bfloat16), preferred_element_type=jnp.float32)

    @pl.when(step == pl.num_programs(0) - 1)
    def _():
        log_ref[...] = jnp.log(totals[...])
        for head in range(heads):
            cols = slice(head * HEAD_DIM, (head + 1) * HEAD_DIM)
            mixed = sums[head] / totals[head : head + 1, :]
            mixed_ref[:, cols] = mixed.T.astype(jnp.bfloat16)


def attend(live, query, pairs, key_at, query_pos, query_start, block):
    rows, width = query.shape
    heads = width // HEAD_DIM
    steps = pairs.shape[0] // block
    row = pl.BlockSpec((1, rows), lambda i, live: (0, 0))
    return pl.pallas_call(
        functools.partial(attend_kernel, heads),
        grid_spec=pltpu.PrefetchScalarGridSpec(
            num_scalar_prefetch=1,
            grid=(steps,),
            in_specs=[
                pl.BlockSpec((rows, width), lambda i, live: (0, 0)),
                pl.BlockSpec((block, pairs.shape[1]), lambda i, live: (i, 0)),
                pl.BlockSpec((block, 1), lambda i, live: (i, 0)),
                row,
                row,
            ],
            out_specs=[
                pl.BlockSpec((rows, width), lambda i, live: (0, 0)),
                pl.BlockSpec((heads, rows), lambda i, live: (0, 0)),
            ],
            scratch_shapes=[
                pltpu.VMEM((heads, HEAD_DIM, rows), jnp.float32),
                pltpu.VMEM((heads, rows), jnp.float32),
            ],
        ),
        out_shape=[
            jax.ShapeDtypeStruct((rows, width), jnp.bfloat16),
            jax.ShapeDtypeStruct((heads, rows), jnp.float32),
        ],
        cost_estimate=pl.CostEstimate(
            flops=4 * rows * width * pairs.shape[0],
            bytes_accessed=2 * pairs.size + 4 * query.size,
            transcendentals=2 * rows * heads * pairs.shape[0],
        ),
        name="attend",
    )(live, query, pairs, key_at[:, None], query_pos[None, :], query_start[None, :])


def attend_back_kernel(heads, first, begins, ends, *refs):
    live_ref, query_ref, grad_ref, mixed_ref, pair_ref, at_ref, pos_ref, start_ref, log_ref = refs[:9]
    refs = refs[9:]
    if not begins:
        carry_ref, refs = refs[0], refs[1:]
    if ends:
        cos_ref, sin_ref, refs = refs[0], refs[1], refs[2:]
    query_grad_ref, line_ref, side_ref, sums, delta = refs
    step = pl.program_id(0)
    scale = HEAD_DIM ** (-0.5)

    @pl.when(step == 0)
    def _():
        sums[...] = jnp.zeros_like(sums) if begins else carry_ref[...]
        ones = jnp.ones((8, HEAD_DIM), jnp.bfloat16)
        for head in range(heads):
            cols = slice(head * HEAD_DIM, (head + 1) * HEAD_DIM)
            grad = grad_ref[:, cols].astype(jnp.float32)
            product = grad * mixed_ref[:, cols].astype(jnp.float32)
            high = product.astype(jnp.bfloat16)
            low = (product - high.astype(jnp.float32)).astype(jnp.bfloat16)
            delta[head * 8 : head * 8 + 8, :] = contract_cols(ones, high) + contract_cols(ones, low)

    def work(out_ref):
        keys = pair_ref[:, :HEAD_DIM]
        values = pair_ref[:, HEAD_DIM:]
        allowed = (at_ref[...] >= start_ref[...]) & (at_ref[...] <= pos_ref[...])
        key_grad = None
        value_grad = None
        for head in range(heads):
            cols = slice(head * HEAD_DIM, (head + 1) * HEAD_DIM)
            query = query_ref[:, cols]
            grad = grad_ref[:, cols]
            bent = jnp.tanh(contract_cols(keys, query) * (scale / softcap))
            probs = jnp.where(
                allowed, jnp.exp(softcap * bent - log_ref[head : head + 1, :]), 0.0
            )
            value_part = jnp.dot(
                probs.astype(jnp.bfloat16), grad, preferred_element_type=jnp.float32
            )
            slope = contract_cols(values, grad) - delta[head * 8 : head * 8 + 1, :]
            score = (probs * slope * (1.0 - bent * bent)).astype(jnp.bfloat16)
            key_part = jnp.dot(score, query, preferred_element_type=jnp.float32)
            sums[:, cols] += contract_rows(score, keys)
            key_grad = key_part if key_grad is None else key_grad + key_part
            value_grad = value_part if value_grad is None else value_grad + value_part
        out_ref[:, :HEAD_DIM] = (key_grad * scale).astype(jnp.bfloat16)
        out_ref[:, HEAD_DIM:] = value_grad.astype(jnp.bfloat16)

    @pl.when(step == 0)
    def _():
        line_ref[...] = jnp.zeros_like(line_ref)
        side_ref[...] = jnp.zeros_like(side_ref)

    @pl.when((step == 0) & (live_ref[first] > 0))
    def _():
        work(line_ref)

    @pl.when((step == 1) & (live_ref[first + 1] > 0))
    def _():
        work(side_ref)

    @pl.when(step == 1)
    def _():
        if not ends:
            query_grad_ref[...] = sums[...]
            return
        half = HEAD_DIM // 2
        for head in range(heads):
            near = slice(head * HEAD_DIM, head * HEAD_DIM + half)
            far = slice(head * HEAD_DIM + half, (head + 1) * HEAD_DIM)
            one = sums[:, near] * scale
            two = sums[:, far] * scale
            query_grad_ref[:, near] = (one * cos_ref[...] + two * sin_ref[...]).astype(jnp.bfloat16)
            query_grad_ref[:, far] = (two * cos_ref[...] - one * sin_ref[...]).astype(jnp.bfloat16)


def attend_back(
    live, query, grad, mixed, pairs, key_at, query_pos, query_start, log_totals, carry, turns, first
):
    rows, width = query.shape
    heads = width // HEAD_DIM
    block = rows
    row = pl.BlockSpec((1, rows), lambda i, live: (0, 0))
    head_row = pl.BlockSpec((heads, rows), lambda i, live: (0, 0))
    full = pl.BlockSpec((rows, width), lambda i, live: (0, 0))
    part = pl.BlockSpec((block, pairs.shape[1]), lambda i, live: (0, 0))
    more_specs = []
    more = []
    if carry is not None:
        more_specs.append(full)
        more.append(carry)
    if turns is not None:
        turn_spec = pl.BlockSpec((rows, HEAD_DIM // 2), lambda i, live: (0, 0))
        more_specs += [turn_spec, turn_spec]
        more += list(turns)
    part_shape = jax.ShapeDtypeStruct((block, pairs.shape[1]), jnp.bfloat16)
    return pl.pallas_call(
        functools.partial(attend_back_kernel, heads, first, carry is None, turns is not None),
        grid_spec=pltpu.PrefetchScalarGridSpec(
            num_scalar_prefetch=1,
            grid=(2,),
            in_specs=[
                full,
                full,
                full,
                pl.BlockSpec((block, pairs.shape[1]), lambda i, live: (i + first, 0)),
                pl.BlockSpec((block, 1), lambda i, live: (i + first, 0)),
                row,
                row,
                head_row,
                *more_specs,
            ],
            out_specs=[full, part, part],
            scratch_shapes=[
                pltpu.VMEM((rows, width), jnp.float32),
                pltpu.VMEM((heads * 8, rows), jnp.float32),
            ],
        ),
        out_shape=[
            jax.ShapeDtypeStruct(
                (rows, width), jnp.float32 if turns is None else jnp.bfloat16
            ),
            part_shape,
            part_shape,
        ],
        cost_estimate=pl.CostEstimate(
            flops=20 * rows * width * block,
            bytes_accessed=8 * block * width + 8 * query.size,
            transcendentals=4 * rows * heads * block,
        ),
        name="attend_back",
    )(
        live,
        query,
        grad,
        mixed,
        pairs,
        key_at[:, None],
        query_pos[None, :],
        query_start[None, :],
        log_totals,
        *more,
    )


def project_kernel(turned, split, rows_ref, weight_ref, cos_ref, sin_ref, query_ref, pair_ref):
    step = pl.program_id(0)
    half = HEAD_DIM // 2
    product = jnp.dot(rows_ref[...], weight_ref[...], preferred_element_type=jnp.float32)

    def store(out_ref, turn):
        one = product[:, :half]
        two = product[:, half:]
        if turn:
            cosine = cos_ref[...]
            sine = sin_ref[...]
            one, two = one * cosine - two * sine, two * cosine + one * sine
        out_ref[:, :half] = one.astype(jnp.bfloat16)
        out_ref[:, half:] = two.astype(jnp.bfloat16)

    @pl.when(step < split)
    def _():
        store(query_ref, True)

    @pl.when((step >= split) & (step < turned))
    def _():
        store(pair_ref, True)

    @pl.when(step >= turned)
    def _():
        store(pair_ref, False)


def project(rows, weight, cosine, sine, query_cols, key_cols):
    count = rows.shape[0]
    split = query_cols // HEAD_DIM
    steps = weight.shape[1] // HEAD_DIM
    turn_spec = pl.BlockSpec((count, HEAD_DIM // 2), lambda i: (0, 0))
    return pl.pallas_call(
        functools.partial(project_kernel, split + key_cols // HEAD_DIM, split),
        grid=(steps,),
        in_specs=[
            pl.BlockSpec(rows.shape, lambda i: (0, 0)),
            pl.BlockSpec((weight.shape[0], HEAD_DIM), lambda i: (0, i)),
            turn_spec,
            turn_spec,
        ],
        out_specs=[
            pl.BlockSpec((count, HEAD_DIM), lambda i: (0, jnp.minimum(i, split - 1))),
            pl.BlockSpec((count, HEAD_DIM), lambda i: (0, jnp.maximum(i - split, 0))),
        ],
        out_shape=[
            jax.ShapeDtypeStruct((count, query_cols), jnp.bfloat16),
            jax.ShapeDtypeStruct((count, 2 * key_cols), jnp.bfloat16),
        ],
        cost_estimate=pl.CostEstimate(
            flops=2 * rows.size * weight.shape[1],
            bytes_accessed=2 * (rows.size + weight.size + count * weight.shape[1]),
            transcendentals=0,
        ),
        name="project",
    )(rows, weight, cosine, sine)


def after(value, *others):
    return lax.optimization_barrier((value,) + others)[0]


def layer(
    inputs,
    cotangent,
    segments,
    first_gain,
    second_gain,
    third_gain,
    fourth_gain,
    query_weight,
    key_weight,
    value_weight,
    output_weight,
    gate_weight,
    up_weight,
    down_weight,
):
    tokens = inputs.shape[0]
    width = inputs.shape[1]
    own_rows = query_weight.shape[0]
    seq_count = lax.axis_size("seq")
    count = lax.axis_size("fsdp")
    seq_rank = lax.axis_index("seq")
    fsdp_rank = lax.axis_index("fsdp")
    half = count // 2
    bf16 = jnp.bfloat16
    head_rows = tokens * seq_count
    query_cols = query_weight.shape[1] // seq_count
    key_cols = key_weight.shape[1] // seq_count

    cycle = [2 * i for i in range(half)] + [2 * i + 1 for i in reversed(range(half))]
    ahead = [(cycle[i], cycle[(i + 1) % count]) for i in range(count)]
    behind = [(b, a) for a, b in ahead]
    place = jnp.where(fsdp_rank % 2 == 0, fsdp_rank // 2, count - 1 - fsdp_rank // 2)

    def rank_at(step):
        spot = lax.rem(place + step + count, count)
        return jnp.where(spot < half, 2 * spot, 2 * (count - 1 - spot) + 1)

    def flip(value, bits):
        return lax.ppermute(value, "seq", [(i, i ^ bits) for i in range(seq_count)])

    def hop(value, pairs):
        return lax.ppermute(value, "fsdp", pairs)

    def ring_gather(value, axis):
        groups = [[value]]
        from_behind = value
        from_ahead = value
        for _ in range(1, half):
            from_behind = hop(from_behind, ahead)
            from_ahead = hop(from_ahead, behind)
            groups.append([from_behind, from_ahead])
        cut = value.shape[axis] // 2
        low = lax.slice_in_dim(from_behind, 0, cut, axis=axis)
        high = lax.slice_in_dim(from_ahead, cut, value.shape[axis], axis=axis)
        low = hop(low, ahead)
        high = hop(high, behind)
        groups.append([jnp.concatenate([low, high], axis=axis)])
        return groups

    def ring_scatter(part_at, axis):
        far = part_at(half)
        cut = far.shape[axis] // 2
        low = lax.slice_in_dim(far, 0, cut, axis=axis).astype(bf16)
        high = lax.slice_in_dim(far, cut, far.shape[axis], axis=axis).astype(bf16)
        low, high = lax.optimization_barrier((hop(low, ahead), hop(high, behind)))
        low = low.astype(jnp.float32)
        high = high.astype(jnp.float32)
        blank = jnp.zeros_like(low)
        onward = jnp.concatenate([low, blank], axis=axis)
        back = jnp.concatenate([blank, high], axis=axis)
        for step in range(half - 1, 0, -1):
            onward = (part_at(step) + onward).astype(bf16)
            back = (part_at(-step) + back).astype(bf16)
            onward, back = lax.optimization_barrier((hop(onward, ahead), hop(back, behind)))
            onward = onward.astype(jnp.float32)
            back = back.astype(jnp.float32)
        return part_at(0) + onward + back

    def seq_gather(value):
        across = flip(value, 2)
        beside = flip(value, 1)
        return [value, beside, across, flip(across, 1)]

    def seq_scatter(parts):
        near = flip(parts[1].astype(bf16), 1).astype(jnp.float32)
        far = flip(parts[3].astype(bf16), 1).astype(jnp.float32)
        across = flip((parts[2] + far).astype(bf16), 2).astype(jnp.float32)
        return parts[0] + near + across

    def sum_all(value):
        bits = seq_count // 2
        while bits:
            value = value + flip(value, bits)
            bits //= 2
        bits = 1
        while bits < count:
            value = value + hop(value, [(i, i ^ bits) for i in range(count)])
            bits *= 2
        return value

    own_start = (seq_rank * count + fsdp_rank) * own_rows
    packed = jnp.stack([first_gain, second_gain, third_gain, fourth_gain])
    gains = sum_all(lax.dynamic_update_slice(jnp.zeros((4, width), bf16), packed, (0, own_start)))
    gain_one, gain_two, gain_three, gain_four = gains[0], gains[1], gains[2], gains[3]

    def columns(weight, rank, size):
        return lax.dynamic_slice_in_dim(weight, rank * size, size, 1)

    def head_columns(rank):
        return jnp.concatenate(
            [
                columns(query_weight, rank, query_cols),
                columns(key_weight, rank, key_cols),
                columns(value_weight, rank, key_cols),
            ],
            axis=1,
        )

    def exchange(pick):
        pieces = [pick(seq_rank)] + [flip(pick(seq_rank ^ j), j) for j in range(1, seq_count)]
        chunk = jnp.zeros((seq_count,) + pieces[0].shape, bf16)
        for j, piece in enumerate(pieces):
            chunk = lax.dynamic_update_slice(chunk, piece[None], (seq_rank ^ j, 0, 0))
        return chunk

    def assemble(groups):
        cols = groups[0][0].shape[2]
        whole_weight = jnp.zeros((seq_count, count, own_rows, cols), bf16)
        for step, group in enumerate(groups):
            for rank, piece in zip((rank_at(-step), rank_at(step)), group):
                whole_weight = lax.dynamic_update_slice(
                    whole_weight, piece[:, None], (0, rank, 0, 0)
                )
        return whole_weight.reshape(width, cols)

    head_chunk = exchange(head_columns)
    rows_in = seq_gather(after(inputs, head_chunk))
    out_chunk = exchange(lambda rank: columns(output_weight, rank, query_cols))
    head_groups = ring_gather(head_chunk, 2)
    in_full = assemble(head_groups)

    def block_pos(rank):
        return jnp.concatenate(
            [
                (rank * seq_count + (seq_rank ^ j)) * tokens + jnp.arange(tokens, dtype=jnp.int32)
                for j in range(seq_count)
            ]
        )

    head_pos = block_pos(fsdp_rank)
    head_seg = jnp.concatenate(
        [
            lax.dynamic_slice_in_dim(
                segments, (fsdp_rank * seq_count + (seq_rank ^ j)) * tokens, tokens, 0
            )
            for j in range(seq_count)
        ]
    )
    head_start = jnp.sum((segments[None, :] < head_seg[:, None]).astype(jnp.int32), axis=1)

    head_in = jnp.concatenate(rows_in, axis=0).astype(jnp.float32)
    whole = inputs.astype(jnp.float32)
    normed = lax.optimization_barrier(rms_forward(head_in, gain_one).astype(bf16))
    head_cos, head_sin = rotation(head_pos)
    query_head, pair = project(normed, in_full, head_cos, head_sin, query_cols, key_cols)

    up_line = [(i, i + 2) for i in range(count - 2)]
    down_line = [(b, a) for a, b in up_line]
    reach = half // 2

    def sideways(step, reverse):
        to_odd = [(2 * i, 2 * i + 1) for i in range(half)]
        to_even = [(2 * i + 1, 2 * i) for i in range(half)]
        pairs = to_odd if step == 0 else to_even if step == reach else to_odd + to_even
        return [(b, a) for a, b in pairs] if reverse else pairs

    line = [pair]
    while len(line) <= reach:
        line.append(hop(line[-1], up_line))
    side = [hop(line[k], sideways(k, False)) for k in range(reach + 1)]
    out_chunk = after(out_chunk, head_groups[-1][0])
    out_groups = ring_gather(out_chunk, 2)
    out_full = assemble(out_groups)

    pieces = []
    places = []
    for k in range(reach + 1):
        pieces += [line[k], side[k]]
        places += [block_pos(fsdp_rank - 2 * k), block_pos((fsdp_rank ^ 1) - 2 * k)]
    pairs_all = jnp.concatenate(pieces, axis=0)
    key_pos = jnp.concatenate(places)
    low_start = jnp.min(head_start)
    ranks = []
    for k in range(reach + 1):
        ranks += [fsdp_rank - 2 * k, (fsdp_rank ^ 1) - 2 * k]
    ranks = jnp.stack(ranks)
    live = (ranks >= 0) & (ranks <= fsdp_rank) & ((ranks + 1) * head_rows > low_start)
    live = live.astype(jnp.int32)
    mixed_head, log_totals = attend(
        live, query_head, pairs_all, key_pos, head_pos, head_start, head_rows
    )
    attended_part = contract_cols(mixed_head, out_full)
    attended = seq_scatter(jnp.split(attended_part, seq_count, axis=0))
    middle = whole + rms_forward(attended, gain_two)
    ffn_in = rms_forward(middle, gain_three).astype(bf16)
    upstream = cotangent.astype(jnp.float32)

    blank = jnp.zeros((-2 * gate_weight.shape[0] % 128, width), bf16)

    def unit_rows(weight):
        weight = after(weight, rows_in[2])
        across = flip(weight, 2)
        beside = flip(weight, 1)
        both = flip(after(across, line[reach]), 1)
        return jnp.concatenate([weight, across, blank, beside, both, blank], axis=0)

    gate_units, up_units, down_units = (
        unit_rows(weight)
        for weight in (gate_weight, up_weight, down_weight)
    )

    def joined(groups):
        return [group[0] if len(group) == 1 else jnp.concatenate(group, axis=0) for group in groups]

    def part_of(parts):
        def part_at(step):
            if step == 0:
                return parts[0]
            if abs(step) == half:
                return parts[half]
            part = parts[abs(step)]
            return part[tokens:] if step > 0 else part[:tokens]

        return part_at

    row_groups = joined(ring_gather(ffn_in, 0))
    gates, ups, hiddens, mlp_parts = [], [], [], []
    for rows in row_groups:
        gate = contract_cols(rows, gate_units)
        up = contract_cols(rows, up_units)
        hidden = (gelu_value(gate) * up).astype(bf16)
        gates.append(gate)
        ups.append(up)
        hiddens.append(hidden)
        mlp_parts.append(jnp.dot(hidden, down_units, preferred_element_type=jnp.float32))
    mlp = ring_scatter(part_of(mlp_parts), 0)
    layer_out = middle + rms_forward(mlp, gain_four)
    mlp_grad, fourth_part = rms_backward(mlp, gain_four, upstream)
    mlp_round = mlp_grad.astype(bf16)
    grad_groups = joined(ring_gather(mlp_round, 0))
    gate_deltas, up_deltas, in_parts = [], [], []
    for grads, gate, up in zip(grad_groups, gates, ups):
        hidden_grad = contract_cols(grads, down_units)
        gate_delta = (hidden_grad * up * gelu_slope(gate)).astype(bf16)
        up_delta = (hidden_grad * gelu_value(gate)).astype(bf16)
        gate_deltas.append(gate_delta)
        up_deltas.append(up_delta)
        in_parts.append(
            jnp.dot(gate_delta, gate_units, preferred_element_type=jnp.float32)
            + jnp.dot(up_delta, up_units, preferred_element_type=jnp.float32)
        )
    ffn_in_grad = ring_scatter(part_of(in_parts), 0)

    middle_part, third_part = rms_backward(middle, gain_three, ffn_in_grad)
    middle_grad = upstream + middle_part
    attended_grad, second_part = rms_backward(attended, gain_two, middle_grad)
    attended_round = attended_grad.astype(bf16)
    attended_blocks = seq_gather(attended_round)
    attended_rows = jnp.concatenate(attended_blocks, axis=0)

    all_rows = jnp.concatenate(row_groups, axis=0)
    all_grads = jnp.concatenate(grad_groups, axis=0)

    def unit_grad(left, right):
        units = gate_weight.shape[0]
        left = jnp.concatenate(left, axis=0)
        cut = left.shape[1] // 2
        far = contract_rows(left[:, cut:], right).astype(bf16)
        near = contract_rows(left[:, :cut], right).astype(bf16)
        beside = flip(far, 1)

        def both(begin):
            return near[begin : begin + units].astype(jnp.float32) + beside[
                begin : begin + units
            ].astype(jnp.float32)

        across = flip(both(units).astype(bf16), 2)
        return both(0) + across.astype(jnp.float32)

    down_grad = unit_grad(hiddens, all_grads)
    gate_grad = unit_grad(gate_deltas, all_rows)
    up_grad = unit_grad(up_deltas, all_rows)

    mixed_grad_head = jnp.dot(
        attended_rows, out_full, preferred_element_type=jnp.float32
    ).astype(bf16)

    def weight_grad(left, right):
        full = contract_rows(left, right).reshape(seq_count, count, own_rows, -1)
        return ring_scatter(
            lambda step: lax.dynamic_slice_in_dim(full, rank_at(step), 1, 1)[:, 0], 2
        ).astype(bf16)

    def to_owners(chunk):
        return [
            flip(lax.dynamic_slice_in_dim(chunk, seq_rank ^ j, 1, 0)[0], j)
            if j
            else lax.dynamic_slice_in_dim(chunk, seq_rank, 1, 0)[0]
            for j in range(seq_count)
        ]

    def spread(pieces):
        cols = pieces[0].shape[1]
        out = jnp.zeros((own_rows, cols * seq_count), jnp.float32)
        for j, piece in enumerate(pieces):
            out = lax.dynamic_update_slice(
                out, piece.astype(jnp.float32), (0, (seq_rank ^ j) * cols)
            )
        return out

    carry = None
    total = None
    for k in range(reach, -1, -1):
        carry, line_part, side_part = attend_back(
            live,
            query_head,
            mixed_grad_head,
            mixed_head,
            pairs_all,
            key_pos,
            head_pos,
            head_start,
            log_totals,
            carry,
            None if k else (head_cos, head_sin),
            2 * k,
        )
        side_sum = hop(side_part, sideways(k, True))
        line_sum = None if total is None else hop(total, down_line)
        total = line_part.astype(jnp.float32) + side_sum.astype(jnp.float32)
        if line_sum is not None:
            total = total + line_sum.astype(jnp.float32)
        if k:
            total = total.astype(bf16)
    query_back = carry
    key_back = rope_apply(total[:, :key_cols], head_cos, head_sin, True).astype(bf16)
    value_back = total[:, key_cols:].astype(bf16)
    output_chunk = weight_grad(attended_rows, mixed_head)
    output_grad = spread(to_owners(output_chunk))
    head_back = jnp.concatenate([query_back, key_back, value_back], axis=1)
    head_pieces = to_owners(weight_grad(normed, head_back))
    value_begin = query_cols + key_cols
    query_grad = spread([piece[:, :query_cols] for piece in head_pieces])
    key_grad = spread([piece[:, query_cols:value_begin] for piece in head_pieces])
    value_grad = spread([piece[:, value_begin:] for piece in head_pieces])
    normed_part = contract_cols(head_back, in_full)
    normed_grad = seq_scatter(jnp.split(normed_part, seq_count, axis=0))
    head_scaling = lax.rsqrt(jnp.mean(head_in * head_in, axis=-1, keepdims=True) + epsilon)
    first_part = jnp.sum(normed_part * head_in * head_scaling, axis=0)
    input_part, _ = rms_backward(whole, gain_one, normed_grad)
    input_grad = middle_grad + input_part

    gain_parts = jnp.stack([first_part, second_part, third_part, fourth_part])
    gain_parts = gain_parts.reshape(4, seq_count, count, own_rows)
    gain_sums = None
    for step in range(count):
        piece = lax.dynamic_slice_in_dim(gain_parts, lax.rem(fsdp_rank + step, count), 1, 2)
        if step:
            pairs = [(i, (i + step) % count) for i in range(count)]
            piece = hop(piece, pairs)
        gain_sums = piece if gain_sums is None else gain_sums + piece
    gain_sums = gain_sums[:, :, 0]
    gain_grads = None
    for j in range(seq_count):
        piece = lax.dynamic_slice_in_dim(gain_sums, seq_rank ^ j, 1, 1)[:, 0]
        piece = flip(piece, j) if j else piece
        gain_grads = piece if gain_grads is None else gain_grads + piece
    return (
        layer_out,
        input_grad,
        gain_grads[0],
        gain_grads[1],
        gain_grads[2],
        gain_grads[3],
        query_grad,
        key_grad,
        value_grad,
        output_grad,
        gate_grad,
        up_grad,
        down_grad,
    )


def solution(mesh):
    placed = (
        P(("fsdp", "seq"), None),
        P(("fsdp", "seq"), None),
        P(),
        P(("seq", "fsdp")),
        P(("seq", "fsdp")),
        P(("seq", "fsdp")),
        P(("seq", "fsdp")),
        P(("seq", "fsdp"), None),
        P(("seq", "fsdp"), None),
        P(("seq", "fsdp"), None),
        P(("seq", "fsdp"), None),
        P(("seq", "fsdp"), None),
        P(("seq", "fsdp"), None),
        P(("seq", "fsdp"), None),
    )
    return jax.shard_map(
        layer,
        mesh=mesh,
        in_specs=placed,
        out_specs=(
            P(("fsdp", "seq"), None),
            P(("fsdp", "seq"), None),
            P(("seq", "fsdp")),
            P(("seq", "fsdp")),
            P(("seq", "fsdp")),
            P(("seq", "fsdp")),
            P(("seq", "fsdp"), None),
            P(("seq", "fsdp"), None),
            P(("seq", "fsdp"), None),
            P(("seq", "fsdp"), None),
            P(("seq", "fsdp"), None),
            P(("seq", "fsdp"), None),
            P(("seq", "fsdp"), None),
        ),
        check_vma=False,
    )
```
